256 devices in a mesh: seq: 32 (over z, x), win: 4 (over y), wout: 2 (over core).
Axes of the slice: x: 4, y: 4, z: 8, core: 2. Of those that a mesh axis runs over, the one named last changes fastest.
Arguments:
- qkv_in: bfloat16 [8192, 3, 2048], P('seq', None, ('win', 'wout')), may hold values from -6 to 6
- conv_w: float32 [3, 4, 2048], P(None, None, ('win', 'wout')), may hold values from -3 to 3
- beta_logits: float32 [16, 8192], P(('win', 'wout'), 'seq'), may hold values from -10 to 3
- lengths: int32 [4], replicated, may hold values from 1 to 3968, as said below
- out_gain: float32 [128], replicated, may hold values from 0.1 to 1.9
- w_out: bfloat16 [2048, 2048], P(('win', 'wout')), may hold values from -0.125 to 0.125
- hidden_in: bfloat16 [8192, 2048], P(('seq', 'win', 'wout')), may hold values from -6 to 6
- norm_gain: float32 [2048], replicated, may hold values from 0.1 to 1.9
- w_qkv: bfloat16 [2048, 6144], P('win', 'wout'), may hold values from -0.125 to 0.125
Outputs:
- qkv_next: bfloat16 [8192, 6144], P(('seq', 'win'), 'wout')
- stream_out: bfloat16 [8192, 2048], P(('seq', 'win', 'wout'))
- final_states: float32 [4, 16, 128, 128], P(None, ('win', 'wout'))
- conv_edges: bfloat16 [4, 3, 3, 2048], P(None, None, None, ('win', 'wout'))
The draws below stay inside these ranges and needn't reach their ends.
Inputs may be any that keep to these rules, and one draw needn't show every extreme that they name: The lengths sum to 8192; the largest is exactly 3968.
All inputs are finite; a program needn't handle non-finite values.
Results may differ from the reference program's by a relative error of at most 0.022.
Values may be sent and summed in bfloat16 or wider, within the bound.
No kernel may reach another device: no remote copies, remote signals or barrier semaphores. Data moves between devices by JAX's collectives and lax.ppermute only.
A program may use at most 64 MiB of HBM per device.

```python
import jax
import jax.numpy as jnp
from jax import lax

D = 2048
H = 16
DK = 128
CONV = 4
TOK_DEV = 256
REQS = 4
HD = 2048
PROMPT_LENGTH_SUM = 8192
MOST = 3968
N_SEQ = 32


def draw_lengths(key, part):
    first_key = jax.random.fold_in(key, 11)
    second_key = jax.random.fold_in(key, 23)
    first = jax.random.randint(first_key, (), TOK_DEV + 1, min(2 * TOK_DEV, MOST) + 1)
    end_second = jax.random.randint(second_key, (), PROMPT_LENGTH_SUM // 2 + 1, PROMPT_LENGTH_SUM // 2 + TOK_DEV // 2)
    third = PROMPT_LENGTH_SUM - MOST - end_second
    last = jnp.int32(MOST)
    return jnp.stack([first, end_second - first, third, last]).astype(jnp.int32)


def draw_beta_logits(key, part):
    lookup_vectors = jax.random.split(key, 6)
    slow = jax.random.randint(lookup_vectors[0], (H,), 0, 2) > 0
    slow_rate = jax.random.uniform(lookup_vectors[1], (H,), minval=0.1, maxval=0.6) * (DK / MOST)
    fast_rate = jax.random.uniform(lookup_vectors[2], (H,), minval=0.2, maxval=0.8)
    rate = jnp.where(slow, slow_rate, fast_rate)
    block_count = PROMPT_LENGTH_SUM // TOK_DEV
    block_factor = jnp.exp(jax.random.uniform(lookup_vectors[3], (H, block_count), minval=-0.7, maxval=0.7))
    block_factor = jnp.repeat(block_factor, TOK_DEV, axis=1)
    token_factor = jnp.exp(jax.random.uniform(lookup_vectors[4], (H, PROMPT_LENGTH_SUM), minval=-0.7, maxval=0.7))
    beta_coefficient = jnp.clip(rate[:, None] * block_factor * token_factor, 5e-05, 0.95)
    position_group = jax.random.uniform(lookup_vectors[5], (PROMPT_LENGTH_SUM,)) < 8.0 / PROMPT_LENGTH_SUM
    beta_coefficient = jnp.where(position_group[None, :], 0.6, beta_coefficient)
    return (jnp.log(beta_coefficient) - jnp.log1p(-beta_coefficient)).astype(jnp.float32)


def shard_levels(stream_key, extent, cuts, smallest, largest):
    level = 1.0
    for position, shards_of in cuts:
        steps = jax.random.uniform(jax.random.fold_in(jax.random.fold_in(stream_key, 6), position), (shards_of,), jnp.float32, smallest / len(cuts), largest / len(cuts))
        level = level * jnp.repeat(jnp.exp(steps), extent[position] // shards_of).reshape((-1,) + (1,) * (len(extent) - 1 - position))
    return level


def noise(stream_key, shape, spread, reach, pieces=(), kind=jnp.bfloat16):
    level = shard_levels(stream_key, shape, pieces, -0.22, 0.18) if pieces else 1.0
    entries = jax.random.normal(stream_key, shape, jnp.float32) * spread * level
    return jnp.minimum(jnp.maximum(entries, -reach), reach).astype(kind)


def setup_inputs(seed: int = 0) -> dict:
    keys = jax.random.split(jax.random.key(seed), 10)
    qkv_in = noise(keys[0], (PROMPT_LENGTH_SUM, 3, HD), 1.0, 6.0, ((0, 32), (2, 8)))
    conv_w = noise(keys[1], (3, CONV, HD), CONV ** -0.5, 3.0, ((2, 8),), jnp.float32)
    beta_logits = draw_beta_logits(jax.random.fold_in(keys[9], 71), 0)
    lengths = draw_lengths(jax.random.fold_in(keys[9], 71), 0)
    out_gain = jnp.clip(1.0 + 0.18 * jax.random.normal(keys[4], (DK,), jnp.float32), 0.1, 1.9)
    w_out = noise(keys[5], (HD, D), HD ** -0.5, 0.125, ((0, 8),))
    hidden_in = noise(keys[6], (PROMPT_LENGTH_SUM, D), 1.0, 6.0, ((0, 256),))
    norm_gain = jnp.clip(1.0 + 0.18 * jax.random.normal(keys[7], (D,), jnp.float32), 0.1, 1.9)
    w_qkv = noise(keys[8], (D, 3 * D), D ** -0.5, 0.125, ((0, 4), (1, 2)))
    return dict(qkv_in=qkv_in, conv_w=conv_w, beta_logits=beta_logits, lengths=lengths, out_gain=out_gain, w_out=w_out, hidden_in=hidden_in, norm_gain=norm_gain, w_qkv=w_qkv)


def segment_ids(positions, seg_ends):
    counts = lax.optimization_barrier(jnp.sum((positions[:, None] >= seg_ends[None, :]).astype(jnp.int32), axis=1))
    return jnp.where(positions < 0, -1, counts).astype(jnp.int32)

def unit_rows(values):
    return values / jnp.sqrt(lax.optimization_barrier(jnp.sum(values * values, axis=-1, keepdims=True)) + 1e-06)

def reference(qkv_in, conv_w, beta_logits, lengths, out_gain, w_out, hidden_in, norm_gain, w_qkv):
    seg_ends = jnp.cumsum(lengths).astype(jnp.int32)
    positions = jnp.arange(PROMPT_LENGTH_SUM, dtype=jnp.int32)
    segment = segment_ids(positions, seg_ends)
    inputs_wide = qkv_in.astype(jnp.float32)
    pre = jnp.zeros((PROMPT_LENGTH_SUM, 3, HD), jnp.float32)
    for offset in range(CONV):
        shift_by = CONV - 1 - offset
        moved = jnp.concatenate([jnp.zeros((shift_by, 3, HD), jnp.float32), inputs_wide[:PROMPT_LENGTH_SUM - shift_by]], axis=0)
        moved_seg = jnp.concatenate([jnp.full((shift_by,), -1, jnp.int32), segment[:PROMPT_LENGTH_SUM - shift_by]], axis=0)
        same_request = (moved_seg == segment).astype(jnp.float32)
        pre = pre + conv_w[:, offset, :][None] * moved * same_request[:, None, None]
    activated = jax.nn.silu(pre).astype(jnp.bfloat16)
    query = unit_rows(activated[:, 0].astype(jnp.float32).reshape(PROMPT_LENGTH_SUM, H, DK))
    keys_all = unit_rows(activated[:, 1].astype(jnp.float32).reshape(PROMPT_LENGTH_SUM, H, DK))
    values_all = activated[:, 2].astype(jnp.float32).reshape(PROMPT_LENGTH_SUM, H, DK)
    beta_coefficient = jax.nn.sigmoid(beta_logits).T

    def token_step(carried_state, inputs):
        memory_state, previous, finished = carried_state
        query_t, key_t, value_t, strength_t, segment_t = inputs
        boundary = (segment_t != previous) & (previous >= 0)
        slot = jnp.maximum(previous, 0)
        finished = finished.at[slot].set(jnp.where(boundary, memory_state, finished[slot]))
        prior = jnp.where(segment_t == previous, memory_state, jnp.zeros_like(memory_state))
        predicted = lax.optimization_barrier(jnp.sum(prior * key_t[:, :, None], axis=1))
        memory_state = prior + strength_t[:, None, None] * key_t[:, :, None] * (value_t - predicted)[:, None, :]
        attended_t = lax.optimization_barrier(jnp.sum(memory_state * query_t[:, :, None], axis=1))
        return ((memory_state, segment_t, finished), attended_t)
    start = (jnp.zeros((H, DK, DK), jnp.float32), jnp.int32(-1), jnp.zeros((REQS, H, DK, DK), jnp.float32))
    (memory_state, previous, finished), attended = lax.scan(token_step, start, (query, keys_all, values_all, beta_coefficient, segment))
    final_states = finished.at[REQS - 1].set(memory_state)
    rim_rows = CONV - 1
    last_tok = seg_ends - 1
    wanted = last_tok[:, None] - rim_rows + 1 + jnp.arange(rim_rows, dtype=jnp.int32)[None, :]
    valid = wanted >= (seg_ends - lengths)[:, None]
    picked = qkv_in[jnp.clip(wanted, 0, PROMPT_LENGTH_SUM - 1)]
    conv_edges = jnp.where(valid[:, :, None, None], picked, jnp.zeros_like(picked))
    scale_heads = jnp.sqrt(lax.optimization_barrier(jnp.mean(attended * attended, axis=-1, keepdims=True)) + 1e-05)
    normed_heads = (attended / scale_heads * out_gain).reshape(PROMPT_LENGTH_SUM, HD).astype(jnp.bfloat16)
    mixed = jnp.dot(normed_heads, w_out, preferred_element_type=jnp.float32)
    summed = hidden_in.astype(jnp.float32) + mixed
    stream_out = summed.astype(jnp.bfloat16)
    scale_stream = jnp.sqrt(lax.optimization_barrier(jnp.mean(summed * summed, axis=-1, keepdims=True)) + 1e-05)
    normed_stream = (summed / scale_stream * norm_gain).astype(jnp.bfloat16)

    def project(rows_block):
        return jnp.dot(rows_block, w_qkv, preferred_element_type=jnp.float32).astype(jnp.bfloat16)
    qkv_next = lax.map(project, normed_stream.reshape(N_SEQ, TOK_DEV, D)).reshape(PROMPT_LENGTH_SUM, 3 * D)
    return (qkv_next, stream_out, final_states, conv_edges)
```

```python
import functools

import jax
import jax.numpy as jnp
from jax import lax
from jax.experimental import pallas as pl
from jax.experimental.pallas import tpu as pltpu
from jax.sharding import PartitionSpec as P

DK = 128
CONV = 4
REQS = 4
HALO = 16
EDGE_ROWS = 16
INTERPRET = False
F32 = jnp.float32
BF16 = jnp.bfloat16
NN = ((1,), (0,))
NT = ((1,), (1,))
TN = ((0,), (0,))
VMEM = pl.BlockSpec(memory_space=pltpu.VMEM)
SMEM = pl.BlockSpec(memory_space=pltpu.SMEM)


def shift(value, axis, steps):
    count = lax.axis_size(axis)
    return lax.ppermute(value, axis, [(s, s + steps) for s in range(count - steps)])


def rotate(value, axis, steps):
    count = lax.axis_size(axis)
    return lax.ppermute(value, axis, [(s, (s + steps) % count) for s in range(count)])


def exchange(value, axis, bit):
    return lax.ppermute(value, axis, [(s, s ^ bit) for s in range(lax.axis_size(axis))])


def dot(left, right, dims=NN):
    return lax.dot_general(left, right, (dims, ((), ())), preferred_element_type=F32)


def split(value):
    high = value.astype(BF16)
    return high, (value - high.astype(F32)).astype(BF16)


def dot_split(left, right, dims=NN):
    lh, ll = left
    rh, rl = right
    return dot(lh, rh, dims) + (dot(lh, rl, dims) + dot(ll, rh, dims))


def dot32(left, right, dims=NN):
    return dot_split(split(left), split(right), dims)


def call(kernel, outs, name, flops, *args, scratch=(), smem=1):
    size = sum(a.size * a.dtype.itemsize for a in args) + sum(
        o.size * o.dtype.itemsize for o in outs
    )
    return pl.pallas_call(
        kernel,
        out_shape=outs,
        in_specs=[SMEM] * smem + [VMEM] * (len(args) - smem),
        out_specs=[VMEM] * len(outs),
        scratch_shapes=list(scratch),
        name=name,
        interpret=INTERPRET,
        cost_estimate=pl.CostEstimate(flops=flops, bytes_accessed=size, transcendentals=0),
        compiler_params=pltpu.CompilerParams(vmem_limit_bytes=40 * 1024 * 1024),
    )(*args)


def out(shape, dtype):
    return jax.ShapeDtypeStruct(shape, dtype)


def request_ends(meta):
    ends = [meta[0]]
    for r in range(1, REQS):
        ends.append(ends[-1] + meta[r])
    return ends


def seg_of(pos, ends):
    total = jnp.where(pos >= ends[0], 1, 0)
    for r in range(1, REQS):
        total = total + jnp.where(pos >= ends[r], 1, 0)
    return total


def start_of(pos, ends):
    begin = jnp.where(pos >= ends[0], ends[0], 0)
    for r in range(1, REQS):
        begin = jnp.maximum(begin, jnp.where(pos >= ends[r], ends[r], 0))
    return begin


def iota(shape, dim):
    return lax.broadcasted_iota(jnp.int32, shape, dim)


def prep_kernel(
    meta, x_ref, halo_ref, taps_ref, beta_ref,
    map_ref, uw_ref, local_ref, link_ref, kb_ref, ks_ref, edge_ref,
):
    rows = x_ref.shape[1]
    heads = x_ref.shape[2] // DK
    half = rows // 2
    ends = request_ends(meta)
    first = meta[4]
    pos = first + iota((rows, 1), 0)
    pos_r = first + iota((1, rows), 1)
    seg = seg_of(pos, ends)
    seg_r = seg_of(pos_r, ends)
    begin = start_of(pos, ends)
    coupled = jnp.where(begin < first, 1.0, 0.0).astype(F32)
    last = first + rows - 1
    last_seg = seg_of(last, ends)
    last_link = start_of(last, ends) < first
    in_last = jnp.where(seg == last_seg, 1.0, 0.0).astype(F32)

    edge_id = iota((EDGE_ROWS, 1), 0)
    wanted = jnp.full((EDGE_ROWS, 1), -1, jnp.int32)
    for r in range(REQS):
        end = ends[r]
        begin_r = end - meta[r]
        owned = (end - 1 >= first) & (end - 1 <= last)
        for i in range(CONV - 1):
            spot = end - (CONV - 1) + i
            good = owned & (spot >= begin_r)
            wanted = jnp.where(edge_id == r * (CONV - 1) + i, jnp.where(good, spot, -1), wanted)
    ext_pos = first - HALO + iota((EDGE_ROWS, rows + HALO), 1)
    select = jnp.where((ext_pos == wanted) & (ext_pos >= 0), 1.0, 0.0).astype(BF16)

    planes = []
    for c in range(3):
        ext = jnp.concatenate([halo_ref[c], x_ref[c]], axis=0)
        picked = dot(select, ext).astype(BF16)
        for b in range(heads):
            edge_ref[c * heads + b] = picked[:, b * DK : (b + 1) * DK]
        wide = ext.astype(F32)
        taps = taps_ref[c]
        pre = wide[HALO:] * taps[CONV - 1 : CONV]
        for back in range(1, CONV):
            moved = pltpu.roll(wide, back, 0)[HALO:]
            ok = jnp.where(pos - back >= begin, 1.0, 0.0).astype(F32)
            pre = pre + moved * taps[CONV - 1 - back : CONV - back] * ok
        planes.append((pre / (1.0 + jnp.exp(-pre))).astype(BF16))

    row_id = iota((rows, rows), 0)
    col_id = iota((rows, rows), 1)
    same = seg == seg_r
    strict = same & (row_id > col_id)
    causal = same & (row_id >= col_id)
    diag = row_id == col_id
    row_h = iota((half, half), 0)
    col_h = iota((half, half), 1)
    eye_h = jnp.where(row_h == col_h, 1.0, 0.0).astype(F32)

    def as_row(column):
        return jnp.sum(jnp.where(diag, column, 0.0), axis=0, keepdims=True)

    def as_column(row):
        return jnp.sum(jnp.where(diag, row, 0.0), axis=1, keepdims=True)

    state = []
    for h in range(heads):
        lanes = slice(h * DK, (h + 1) * DK)
        qb, kb, vb = (planes[c][:, lanes] for c in range(3))
        q32, k32, v32 = (t.astype(F32) for t in (qb, kb, vb))
        qs = lax.rsqrt(jnp.sum(q32 * q32, axis=1, keepdims=True) + 1e-06)
        ks = lax.rsqrt(jnp.sum(k32 * k32, axis=1, keepdims=True) + 1e-06)
        ks_row = as_row(ks)
        beta = as_column(1.0 / (1.0 + jnp.exp(-beta_ref[h : h + 1, :])))
        system = jnp.where(strict, dot(kb, kb, NT) * (beta * ks) * ks_row, 0.0)
        scores = jnp.where(causal, dot(qb, kb, NT) * qs * ks_row, 0.0)
        targets = jnp.concatenate([beta * v32, (beta * coupled * ks) * k32], axis=1)
        state.append((q32 * qs, kb, ks, system, scores, targets))

    blocks = []
    for h in range(heads):
        system = state[h][3]
        for d in range(2):
            blocks.append(system[d * half : (d + 1) * half, d * half : (d + 1) * half])
    inverses = []
    low = ((row_h ^ col_h) == 1) & (row_h > col_h)
    for a in blocks:
        inverses.append(eye_h - jnp.where(low, a, 0.0))
    level = 1
    while (2 << level) <= half:
        low = (((row_h >> level) ^ (col_h >> level)) == 1) & (row_h > col_h)
        parts = [split(x) for x in inverses]
        inner = [dot_split(split(jnp.where(low, a, 0.0)), p) for a, p in zip(blocks, parts)]
        inverses = [x - dot_split(p, split(t)) for x, p, t in zip(inverses, parts, inner)]
        level += 1

    for h in range(heads):
        q32, kb, ks, system, scores, targets = state[h]
        top = dot32(inverses[2 * h], targets[:half])
        rest = targets[half:] - dot32(system[half:, :half], top)
        uw = jnp.concatenate([top, dot32(inverses[2 * h + 1], rest)], axis=0)
        uw_ref[h] = uw
        mixed = dot32(scores, uw)
        local_ref[h] = mixed[:, :DK]
        link_ref[h] = coupled * q32 - mixed[:, DK:]
        kb_ref[h] = kb
        ks_ref[h] = ks
        scaled = jnp.concatenate([uw[:, DK:] * ks, uw[:, :DK] * (ks * in_last)], axis=1)
        high, less = split(scaled)
        fold = dot(kb, high, TN) + dot(kb, less, TN)
        eye_k = jnp.where(iota((DK, DK), 0) == iota((DK, DK), 1), 1.0, 0.0).astype(F32)
        map_ref[h, :, :DK] = jnp.where(last_link, fold[:, :DK], eye_k).astype(BF16)
        map_ref[h, :, DK:] = fold[:, DK:].astype(BF16)


def window_kernel(m1_ref, m2_ref, m3_ref, m4_ref, wide_ref, send_ref, tail_ref):
    for h in range(m1_ref.shape[0]):
        pairs = []
        for newer, older in ((m1_ref, m2_ref), (m3_ref, m4_ref)):
            a, b = newer[h], older[h]
            pairs.append(a.astype(F32) + b.astype(F32) - dot(a[:, :DK], b))
        joined = pairs[0] + pairs[1] - dot32(pairs[0][:, :DK], pairs[1])
        wide_ref[h] = joined
        send_ref[h] = joined.astype(BF16)
        tail_ref[h] = joined[:, DK:].astype(BF16)


def attend_kernel(
    meta, e0_ref, e4_ref, e8_ref, e12_ref, uw_ref, local_ref, link_ref, kb_ref, ks_ref,
    edge_ref, gain_ref, w_ref, own_ref, other_ref, pay_ref, heads_ref,
):
    heads, rows, _ = local_ref.shape
    wins, cores, piece, _ = heads_ref.shape
    ends = request_ends(meta)
    first, win, core = meta[4], meta[5], meta[6]
    last = first + rows - 1
    seg = seg_of(first + iota((rows, 1), 0), ends)
    gain = gain_ref[...]
    for h in range(heads):
        e0, e4, e8 = e0_ref[h], e4_ref[h], e8_ref[h]
        near = e0 + e4.astype(F32) - dot32(e0[:, :DK], e4.astype(F32))
        far = (
            e8[:, DK:].astype(F32) + e12_ref[h].astype(F32) - dot(e8[:, :DK], e12_ref[h])
        )
        enter = near[:, DK:] + far - dot32(near[:, :DK], far)
        parts = split(enter)
        attended = local_ref[h] + dot_split(split(link_ref[h]), parts)
        scale = lax.rsqrt(jnp.mean(attended * attended, axis=1, keepdims=True) + 1e-05)
        normed = attended * scale * gain
        lanes = slice(h * DK, (h + 1) * DK)
        for p in range(wins * cores):
            heads_ref[p // cores, p % cores, :, lanes] = normed[p * piece : (p + 1) * piece].astype(
                BF16
            )
        uw = uw_ref[h]
        corrected = (uw[:, :DK] - dot_split(split(uw[:, DK:]), parts)) * ks_ref[h]
        for r in range(REQS):
            owned = (ends[r] - 1 >= first) & (ends[r] - 1 <= last)
            carried = owned & (ends[r] - meta[r] < first)
            member = (seg == r) & owned
            high, less = split(jnp.where(member, corrected, 0.0))
            final = dot(kb_ref[h], high, TN) + dot(kb_ref[h], less, TN)
            final = final + jnp.where(carried, enter, 0.0)
            spot = (r * heads + h) * DK
            pay_ref[spot : spot + DK, :] = final.astype(BF16)
    base = REQS * heads * DK
    for b in range(edge_ref.shape[0]):
        pay_ref[base + b * EDGE_ROWS : base + (b + 1) * EDGE_ROWS, :] = edge_ref[b]
    order = [lax.rem(win + k, wins) for k in range(wins)]
    w = w_ref[...]
    mine = jnp.concatenate([heads_ref[o, core] for o in order], axis=0)
    own_ref[...] = dot(mine, w)
    theirs = jnp.concatenate([heads_ref[o, cores - 1 - core] for o in order], axis=0)
    other_ref[...] = dot(theirs, w).astype(BF16)


def pair_kernel(own_ref, got_ref, keep_ref, *send_refs):
    piece = keep_ref.shape[0]
    keep_ref[...] = own_ref[:piece] + got_ref[:piece].astype(F32)
    for k, ref in enumerate(send_refs):
        part = slice((k + 1) * piece, (k + 2) * piece)
        ref[...] = (own_ref[part] + got_ref[part].astype(F32)).astype(BF16)


def norm_kernel(meta, hidden_ref, gain_ref, keep_ref, *refs):
    wins = refs[-1].shape[0]
    got, (stream_ref, *piece_refs), cols_ref = refs[: wins - 1], refs[wins - 1 : -1], refs[-1]
    total = keep_ref[...]
    for ref in got:
        total = total + ref[...].astype(F32)
    total = hidden_ref[...].astype(F32) + total
    stream_ref[...] = total.astype(BF16)
    scale = lax.rsqrt(jnp.mean(total * total, axis=1, keepdims=True) + 1e-05)
    normed = (total * scale * gain_ref[...]).astype(BF16)
    width = normed.shape[1] // wins
    for k in range(wins):
        cols_ref[k] = normed[:, k * width : (k + 1) * width]
    for k, ref in enumerate(piece_refs):
        ref[...] = cols_ref[lax.rem(meta[5] + k, wins)]


def body(qkv_in, conv_w, beta_logits, lengths, out_gain, w_out, hidden_in, norm_gain, w_qkv):
    rows = qkv_in.shape[0]
    width = qkv_in.shape[2]
    heads = width // DK
    model = w_out.shape[1]
    n_seq, wins, cores = (lax.axis_size(a) for a in ("seq", "win", "wout"))
    piece = rows // (wins * cores)
    seq, win, core = (lax.axis_index(a).astype(jnp.int32) for a in ("seq", "win", "wout"))
    meta = jnp.concatenate([lengths, jnp.stack([seq * rows, win, core, core])])
    x = qkv_in.transpose(1, 0, 2)
    halo = shift(x[:, rows - HALO :], "seq", 1)
    maps, uw, local, link, kb, ks, edges = call(
        prep_kernel,
        [
            out((heads, DK, 2 * DK), BF16),
            out((heads, rows, 2 * DK), F32),
            out((heads, rows, DK), F32),
            out((heads, rows, DK), F32),
            out((heads, rows, DK), BF16),
            out((heads, rows, 1), F32),
            out((3 * heads, EDGE_ROWS, DK), BF16),
        ],
        "prep",
        2 * 10**9,
        meta, x, halo, conv_w, beta_logits,
    )

    def sent(value, steps):
        return shift(value, "seq", steps) if steps < n_seq else jnp.zeros_like(value)

    near = [sent(maps, k) for k in range(1, 5)]
    wide, send, tail = call(
        window_kernel,
        [
            out((heads, DK, 2 * DK), F32),
            out((heads, DK, 2 * DK), BF16),
            out((heads, DK, DK), BF16),
        ],
        "window",
        10**8,
        *near,
        smem=0,
    )
    far = [sent(send, 4), sent(send, 8), sent(tail, 12)]
    state_rows = REQS * heads * DK
    pay_rows = state_rows + 3 * heads * EDGE_ROWS
    own, other, payload = call(
        attend_kernel,
        [
            out((wins * piece, model), F32),
            out((wins * piece, model), BF16),
            out((pay_rows, DK), BF16),
        ],
        "attend",
        10**9,
        meta, wide, *far, uw, local, link, kb, ks, edges, out_gain.reshape(1, DK), w_out,
        scratch=[pltpu.VMEM((wins, cores, piece, width), BF16)],
    )
    got = rotate(other, "wout", 1)
    sums = call(
        pair_kernel,
        [out((piece, model), F32)] + [out((piece, model), BF16)] * (wins - 1),
        "pair",
        10**6,
        own, got,
        smem=0,
    )
    reduced = [rotate(sums[k], "win", k) for k in range(1, wins)]
    stream_out, *cols = call(
        norm_kernel,
        [out((piece, model), BF16)] + [out((piece, model // wins), BF16)] * wins,
        "norm",
        10**6,
        meta, hidden_in, norm_gain.reshape(1, model), sums[0], *reduced,
        scratch=[pltpu.VMEM((wins, piece, model // wins), BF16)],
    )
    blocks = [cols[0]] + [rotate(cols[k], "win", k) for k in range(1, wins)]
    peers = rotate(jnp.concatenate(blocks, axis=0), "wout", 1)

    def partial(k):
        j = (wins - k) % wins
        mine, theirs = blocks[j], peers[j * piece : (j + 1) * piece]
        lower = jnp.where(core == 0, mine, theirs)
        upper = jnp.where(core == 0, theirs, mine)
        return jnp.dot(
            jnp.concatenate([lower, upper], axis=0), w_qkv, preferred_element_type=F32
        )

    arrived = [rotate(partial(k).astype(BF16), "win", k) for k in range(1, wins)]
    total = partial(0)
    for part in arrived:
        total = total + part.astype(F32)
    projected = total.astype(BF16)

    bit = 1
    while bit < n_seq:
        payload = payload + exchange(payload, "seq", bit)
        bit *= 2
    final_states = payload[:state_rows].astype(F32).reshape(REQS, heads, DK, DK)
    edges = payload[state_rows:].reshape(3 * heads, EDGE_ROWS, DK)[:, : REQS * (CONV - 1)]
    conv_edges = edges.transpose(1, 0, 2).reshape(REQS, CONV - 1, 3, width)
    return (projected, stream_out, final_states, conv_edges)


def solution(mesh):
    return jax.shard_map(
        body,
        mesh=mesh,
        in_specs=(
            P("seq", None, ("win", "wout")),
            P(None, None, ("win", "wout")),
            P(("win", "wout"), "seq"),
            P(),
            P(),
            P(("win", "wout"), None),
            P(("seq", "win", "wout"), None),
            P(),
            P("win", "wout"),
        ),
        out_specs=(
            P(("seq", "win"), "wout"),
            P(("seq", "win", "wout"), None),
            P(None, ("win", "wout"), None, None),
            P(None, None, None, ("win", "wout")),
        ),
        check_vma=False,
    )
```

```python
import functools

import jax
import jax.numpy as jnp
from jax import lax
from jax.experimental import pallas as pl
from jax.experimental.pallas import tpu as pltpu
from jax.sharding import PartitionSpec as P

DK = 128
CONV = 4
REQS = 4
HALO = 16
EDGE_ROWS = 16
INTERPRET = False
F32 = jnp.float32
BF16 = jnp.bfloat16
NN = ((1,), (0,))
NT = ((1,), (1,))
TN = ((0,), (0,))
VMEM = pl.BlockSpec(memory_space=pltpu.VMEM)
SMEM = pl.BlockSpec(memory_space=pltpu.SMEM)
HBM = pl.BlockSpec(memory_space=pltpu.HBM)


def shift(value, axis, steps):
    count = lax.axis_size(axis)
    return lax.ppermute(value, axis, [(s, s + steps) for s in range(count - steps)])


def rotate(value, axis, steps):
    count = lax.axis_size(axis)
    return lax.ppermute(value, axis, [(s, (s + steps) % count) for s in range(count)])


def exchange(value, axis, bit):
    return lax.ppermute(value, axis, [(s, s ^ bit) for s in range(lax.axis_size(axis))])


def dot(left, right, dims=NN):
    return lax.dot_general(left, right, (dims, ((), ())), preferred_element_type=F32)


def split(value):
    high = value.astype(BF16)
    return high, (value - high.astype(F32)).astype(BF16)


def dot_split(left, right, dims=NN):
    lh, ll = left
    rh, rl = right
    return dot(lh, rh, dims) + (dot(lh, rl, dims) + dot(ll, rh, dims))


def dot32(left, right, dims=NN):
    return dot_split(split(left), split(right), dims)


def call(kernel, outs, name, flops, *args, scratch=(), smem=1, hbm=0):
    size = sum(a.size * a.dtype.itemsize for a in args) + sum(
        o.size * o.dtype.itemsize for o in outs
    )
    return pl.pallas_call(
        kernel,
        out_shape=outs,
        in_specs=[SMEM] * smem + [HBM] * hbm + [VMEM] * (len(args) - smem - hbm),
        out_specs=[VMEM] * len(outs),
        scratch_shapes=list(scratch),
        name=name,
        interpret=INTERPRET,
        cost_estimate=pl.CostEstimate(flops=flops, bytes_accessed=size, transcendentals=0),
        compiler_params=pltpu.CompilerParams(vmem_limit_bytes=40 * 1024 * 1024),
    )(*args)


def in_hbm(value):
    return value if INTERPRET else pltpu.with_memory_space_constraint(value, pltpu.HBM)


def out(shape, dtype):
    return jax.ShapeDtypeStruct(shape, dtype)


def request_ends(meta):
    ends = [meta[0]]
    for r in range(1, REQS):
        ends.append(ends[-1] + meta[r])
    return ends


def seg_of(pos, ends):
    total = jnp.where(pos >= ends[0], 1, 0)
    for r in range(1, REQS):
        total = total + jnp.where(pos >= ends[r], 1, 0)
    return total


def start_of(pos, ends):
    begin = jnp.where(pos >= ends[0], ends[0], 0)
    for r in range(1, REQS):
        begin = jnp.maximum(begin, jnp.where(pos >= ends[r], ends[r], 0))
    return begin


def iota(shape, dim):
    return lax.broadcasted_iota(jnp.int32, shape, dim)


def conv_rows(ext, taps, pos, begin):
    pre = ext[HALO:] * taps[CONV - 1 : CONV]
    for back in range(1, CONV):
        moved = pltpu.roll(ext, back, 0)[HALO:]
        ok = jnp.where(pos - back >= begin, 1.0, 0.0).astype(F32)
        pre = pre + moved * taps[CONV - 1 - back : CONV - back] * ok
    return (pre / (1.0 + jnp.exp(-pre))).astype(BF16)


def edge_select(meta, ends, first, last, ext_pos):
    edge_id = iota((EDGE_ROWS, 1), 0)
    wanted = jnp.full((EDGE_ROWS, 1), -1, jnp.int32)
    for r in range(REQS):
        begin = ends[r] - meta[r]
        owned = (ends[r] - 1 >= first) & (ends[r] - 1 <= last)
        for i in range(CONV - 1):
            spot = ends[r] - (CONV - 1) + i
            good = owned & (spot >= begin)
            wanted = jnp.where(edge_id == r * (CONV - 1) + i, jnp.where(good, spot, -1), wanted)
    return jnp.where((ext_pos == wanted) & (ext_pos >= 0), 1.0, 0.0).astype(BF16)


def conv_kernel(
    meta, x_hbm, taps_hbm, beta_hbm,
    act_ref, head_ref, edge_ref, taps_ref, beta_ref, x_ref, sems,
):
    copies = [
        pltpu.make_async_copy(x_hbm, x_ref, sems.at[0]),
        pltpu.make_async_copy(taps_hbm, taps_ref, sems.at[1]),
        pltpu.make_async_copy(beta_hbm, beta_ref, sems.at[2]),
    ]
    for copy in copies:
        copy.start()
    for copy in copies:
        copy.wait()
    rows = x_ref.shape[1]
    ends = request_ends(meta)
    first = meta[4]
    pos = first + iota((rows, 1), 0)
    begin = start_of(pos, ends)
    select = edge_select(
        meta, ends, first, first + rows - 1, first + iota((EDGE_ROWS, rows), 1)
    )
    for c in range(3):
        x = x_ref[c]
        edge_ref[c] = dot(select, x).astype(BF16)
        head_ref[c] = x[:HALO]
        wide = x.astype(F32)
        act_ref[c, HALO:] = conv_rows(wide, taps_ref[c], pos[HALO:], begin[HALO:])
        act_ref[c, :HALO] = jnp.zeros((HALO, x.shape[1]), BF16)


def prep_kernel(
    meta, act_ref, head_ref, part_ref, taps_ref, beta_ref, halo_ref,
    map_ref, uw_ref, local_ref, link_ref, kb_ref, ks_ref, edge_ref,
):
    rows = act_ref.shape[1]
    heads = act_ref.shape[2] // DK
    half = rows // 2
    ends = request_ends(meta)
    first = meta[4]
    pos = first + iota((rows, 1), 0)
    pos_r = first + iota((1, rows), 1)
    seg = seg_of(pos, ends)
    seg_r = seg_of(pos_r, ends)
    begin = start_of(pos, ends)
    coupled = jnp.where(begin < first, 1.0, 0.0).astype(F32)
    last = first + rows - 1
    last_seg = seg_of(last, ends)
    last_link = start_of(last, ends) < first
    in_last = jnp.where(seg == last_seg, 1.0, 0.0).astype(F32)
    select = edge_select(meta, ends, first, last, first - HALO + iota((EDGE_ROWS, HALO), 1))

    planes = []
    for c in range(3):
        halo = halo_ref[c]
        picked = part_ref[c] + dot(select, halo).astype(BF16)
        for b in range(heads):
            edge_ref[c * heads + b] = picked[:, b * DK : (b + 1) * DK]
        ext = jnp.concatenate([halo, head_ref[c]], axis=0).astype(F32)
        lead = conv_rows(ext, taps_ref[c], pos[:HALO], begin[:HALO])
        planes.append(jnp.concatenate([lead, act_ref[c, HALO:]], axis=0))

    row_id = iota((rows, rows), 0)
    col_id = iota((rows, rows), 1)
    same = seg == seg_r
    strict = same & (row_id > col_id)
    causal = same & (row_id >= col_id)
    diag = row_id == col_id
    row_h = iota((half, half), 0)
    col_h = iota((half, half), 1)
    eye_h = jnp.where(row_h == col_h, 1.0, 0.0).astype(F32)

    def as_row(column):
        return jnp.sum(jnp.where(diag, column, 0.0), axis=0, keepdims=True)

    def as_column(row):
        return jnp.sum(jnp.where(diag, row, 0.0), axis=1, keepdims=True)

    state = []
    for h in range(heads):
        lanes = slice(h * DK, (h + 1) * DK)
        qb, kb, vb = (planes[c][:, lanes] for c in range(3))
        q32, k32, v32 = (t.astype(F32) for t in (qb, kb, vb))
        qs = lax.rsqrt(jnp.sum(q32 * q32, axis=1, keepdims=True) + 1e-06)
        ks = lax.rsqrt(jnp.sum(k32 * k32, axis=1, keepdims=True) + 1e-06)
        ks_row = as_row(ks)
        beta = as_column(1.0 / (1.0 + jnp.exp(-beta_ref[h : h + 1, :])))
        system = jnp.where(strict, dot(kb, kb, NT) * (beta * ks) * ks_row, 0.0)
        scores = jnp.where(causal, dot(qb, kb, NT) * qs * ks_row, 0.0)
        targets = jnp.concatenate([beta * v32, (beta * coupled * ks) * k32], axis=1)
        state.append((q32 * qs, kb, ks, system, scores, targets))

    blocks = []
    for h in range(heads):
        system = state[h][3]
        for d in range(2):
            blocks.append(system[d * half : (d + 1) * half, d * half : (d + 1) * half])
    inverses = []
    low = ((row_h ^ col_h) == 1) & (row_h > col_h)
    for a in blocks:
        inverses.append(eye_h - jnp.where(low, a, 0.0))
    level = 1
    while (2 << level) <= half:
        low = (((row_h >> level) ^ (col_h >> level)) == 1) & (row_h > col_h)
        parts = [split(x) for x in inverses]
        inner = [dot_split(split(jnp.where(low, a, 0.0)), p) for a, p in zip(blocks, parts)]
        inverses = [x - dot_split(p, split(t)) for x, p, t in zip(inverses, parts, inner)]
        level += 1

    for h in range(heads):
        q32, kb, ks, system, scores, targets = state[h]
        top = dot32(inverses[2 * h], targets[:half])
        rest = targets[half:] - dot32(system[half:, :half], top)
        uw = jnp.concatenate([top, dot32(inverses[2 * h + 1], rest)], axis=0)
        uw_ref[h] = uw
        mixed = dot32(scores, uw)
        local_ref[h] = mixed[:, :DK]
        link_ref[h] = coupled * q32 - mixed[:, DK:]
        kb_ref[h] = kb
        ks_ref[h] = ks
        scaled = jnp.concatenate([uw[:, DK:] * ks, uw[:, :DK] * (ks * in_last)], axis=1)
        high, less = split(scaled)
        fold = dot(kb, high, TN) + dot(kb, less, TN)
        eye_k = jnp.where(iota((DK, DK), 0) == iota((DK, DK), 1), 1.0, 0.0).astype(F32)
        map_ref[h, :, :DK] = jnp.where(last_link, fold[:, :DK], eye_k).astype(BF16)
        map_ref[h, :, DK:] = fold[:, DK:].astype(BF16)


def window_kernel(m1_ref, m2_ref, m3_ref, m4_ref, wide_ref, send_ref, tail_ref):
    for h in range(m1_ref.shape[0]):
        pairs = []
        for newer, older in ((m1_ref, m2_ref), (m3_ref, m4_ref)):
            a, b = newer[h], older[h]
            pairs.append(a.astype(F32) + b.astype(F32) - dot(a[:, :DK], b))
        joined = pairs[0] + pairs[1] - dot32(pairs[0][:, :DK], pairs[1])
        wide_ref[h] = joined
        send_ref[h] = joined.astype(BF16)
        tail_ref[h] = joined[:, DK:].astype(BF16)


def attend_kernel(
    meta, e0_ref, e4_ref, e8_ref, e12_ref, uw_ref, local_ref, link_ref, kb_ref, ks_ref,
    edge_ref, gain_ref, w_ref, own_ref, other_ref, pay_ref, heads_ref,
):
    heads, rows, _ = local_ref.shape
    wins, cores, piece, _ = heads_ref.shape
    ends = request_ends(meta)
    first, win, core = meta[4], meta[5], meta[6]
    last = first + rows - 1
    seg = seg_of(first + iota((rows, 1), 0), ends)
    gain = gain_ref[...]
    for h in range(heads):
        e0, e4, e8 = e0_ref[h], e4_ref[h], e8_ref[h]
        near = e0 + e4.astype(F32) - dot32(e0[:, :DK], e4.astype(F32))
        far = (
            e8[:, DK:].astype(F32) + e12_ref[h].astype(F32) - dot(e8[:, :DK], e12_ref[h])
        )
        enter = near[:, DK:] + far - dot32(near[:, :DK], far)
        parts = split(enter)
        attended = local_ref[h] + dot_split(split(link_ref[h]), parts)
        scale = lax.rsqrt(jnp.mean(attended * attended, axis=1, keepdims=True) + 1e-05)
        normed = attended * scale * gain
        lanes = slice(h * DK, (h + 1) * DK)
        for p in range(wins * cores):
            heads_ref[p // cores, p % cores, :, lanes] = normed[p * piece : (p + 1) * piece].astype(
                BF16
            )
        uw = uw_ref[h]
        corrected = (uw[:, :DK] - dot_split(split(uw[:, DK:]), parts)) * ks_ref[h]
        for r in range(REQS):
            owned = (ends[r] - 1 >= first) & (ends[r] - 1 <= last)
            carried = owned & (ends[r] - meta[r] < first)
            member = (seg == r) & owned
            high, less = split(jnp.where(member, corrected, 0.0))
            final = dot(kb_ref[h], high, TN) + dot(kb_ref[h], less, TN)
            final = final + jnp.where(carried, enter, 0.0)
            spot = (r * heads + h) * DK
            pay_ref[spot : spot + DK, :] = final.astype(BF16)
    base = REQS * heads * DK
    for b in range(edge_ref.shape[0]):
        pay_ref[base + b * EDGE_ROWS : base + (b + 1) * EDGE_ROWS, :] = edge_ref[b]
    order = [lax.rem(win + k, wins) for k in range(wins)]
    w = w_ref[...]
    mine = jnp.concatenate([heads_ref[o, core] for o in order], axis=0)
    own_ref[...] = dot(mine, w)
    theirs = jnp.concatenate([heads_ref[o, cores - 1 - core] for o in order], axis=0)
    other_ref[...] = dot(theirs, w).astype(BF16)


def pair_kernel(own_ref, got_ref, keep_ref, *send_refs):
    piece = keep_ref.shape[0]
    keep_ref[...] = own_ref[:piece] + got_ref[:piece].astype(F32)
    for k, ref in enumerate(send_refs):
        part = slice((k + 1) * piece, (k + 2) * piece)
        ref[...] = (own_ref[part] + got_ref[part].astype(F32)).astype(BF16)


def norm_kernel(hidden_ref, gain_ref, pay_ref, came_ref, keep_ref, *refs):
    *got, stream_ref, normed_ref, sum_ref = refs
    total = keep_ref[...]
    for ref in got:
        total = total + ref[...].astype(F32)
    total = hidden_ref[...].astype(F32) + total
    stream_ref[...] = total.astype(BF16)
    scale = lax.rsqrt(jnp.mean(total * total, axis=1, keepdims=True) + 1e-05)
    normed_ref[...] = (total * scale * gain_ref[...]).astype(BF16)
    sum_ref[...] = pay_ref[...] + came_ref[...]


def columns_kernel(meta, mine_ref, peer_ref, *refs):
    *piece_refs, cols_ref = refs
    wins, rows, width = cols_ref.shape
    mine, peer = mine_ref[...], peer_ref[...]
    lower = jnp.where(meta[6] == 0, mine, peer)
    upper = jnp.where(meta[6] == 0, peer, mine)
    for k in range(wins):
        cols_ref[k, : rows // 2] = lower[:, k * width : (k + 1) * width]
        cols_ref[k, rows // 2 :] = upper[:, k * width : (k + 1) * width]
    for k, ref in enumerate(piece_refs):
        ref[...] = cols_ref[lax.rem(meta[5] + k, wins)]


def body(qkv_in, conv_w, beta_logits, lengths, out_gain, w_out, hidden_in, norm_gain, w_qkv):
    rows = qkv_in.shape[0]
    width = qkv_in.shape[2]
    heads = width // DK
    model = w_out.shape[1]
    n_seq, wins, cores = (lax.axis_size(a) for a in ("seq", "win", "wout"))
    piece = rows // (wins * cores)
    seq, win, core = (lax.axis_index(a).astype(jnp.int32) for a in ("seq", "win", "wout"))
    meta = jnp.concatenate([lengths, jnp.stack([seq * rows, win, core, core])])
    x = qkv_in.transpose(1, 0, 2)
    halo = shift(x[:, rows - HALO :], "seq", 1)
    act, lead, parts, taps, beta = call(
        conv_kernel,
        [
            out((3, rows, width), BF16),
            out((3, HALO, width), BF16),
            out((3, EDGE_ROWS, width), BF16),
            out((3, CONV, width), F32),
            out((heads, rows), F32),
        ],
        "conv",
        10**8,
        meta, *(in_hbm(a) for a in (x, conv_w, beta_logits)),
        scratch=[pltpu.VMEM((3, rows, width), BF16), pltpu.SemaphoreType.DMA((3,))],
        hbm=3,
    )
    maps, uw, local, link, kb, ks, edges = call(
        prep_kernel,
        [
            out((heads, DK, 2 * DK), BF16),
            out((heads, rows, 2 * DK), F32),
            out((heads, rows, DK), F32),
            out((heads, rows, DK), F32),
            out((heads, rows, DK), BF16),
            out((heads, rows, 1), F32),
            out((3 * heads, EDGE_ROWS, DK), BF16),
        ],
        "prep",
        2 * 10**9,
        meta, act, lead, parts, taps, beta, halo,
    )

    def sent(value, steps):
        return shift(value, "seq", steps) if steps < n_seq else jnp.zeros_like(value)

    near = [sent(maps, k) for k in range(1, 5)]
    wide, send, tail = call(
        window_kernel,
        [
            out((heads, DK, 2 * DK), F32),
            out((heads, DK, 2 * DK), BF16),
            out((heads, DK, DK), BF16),
        ],
        "window",
        10**8,
        *near,
        smem=0,
    )
    far = [sent(send, 4), sent(send, 8), sent(tail, 12)]
    state_rows = REQS * heads * DK
    pay_rows = state_rows + 3 * heads * EDGE_ROWS
    own, other, payload = call(
        attend_kernel,
        [
            out((wins * piece, model), F32),
            out((wins * piece, model), BF16),
            out((pay_rows, DK), BF16),
        ],
        "attend",
        10**9,
        meta, wide, *far, uw, local, link, kb, ks, edges, out_gain.reshape(1, DK), w_out,
        scratch=[pltpu.VMEM((wins, cores, piece, width), BF16)],
    )
    got = rotate(other, "wout", 1)
    bits = [1 << b for b in reversed(range((n_seq - 1).bit_length()))]
    came = exchange(payload, "seq", bits[0])
    sums = call(
        pair_kernel,
        [out((piece, model), F32)] + [out((piece, model), BF16)] * (wins - 1),
        "pair",
        10**6,
        own, got,
        smem=0,
    )
    reduced = [rotate(sums[k], "win", k) for k in range(1, wins)]
    stream_out, normed, payload = call(
        norm_kernel,
        [out((piece, model), BF16), out((piece, model), BF16), out((pay_rows, DK), BF16)],
        "norm",
        10**6,
        hidden_in, norm_gain.reshape(1, model), payload, came, sums[0], *reduced,
        smem=0,
    )
    peer = rotate(normed, "wout", 1)
    came = exchange(payload, "seq", bits[1])
    cols = call(
        columns_kernel,
        [out((2 * piece, model // wins), BF16)] * wins,
        "columns",
        10**6,
        meta, normed, peer,
        scratch=[pltpu.VMEM((wins, 2 * piece, model // wins), BF16)],
    )
    blocks = [cols[0]] + [rotate(cols[k], "win", k) for k in range(1, wins)]
    *blocks, payload = lax.optimization_barrier((*blocks, payload + came))

    def partial(k):
        return jnp.dot(blocks[(wins - k) % wins], w_qkv, preferred_element_type=F32)

    arrived = [rotate(partial(k).astype(BF16), "win", k) for k in range(1, wins)]
    total = partial(0)
    for part in arrived:
        total = total + part.astype(F32)
    projected = total.astype(BF16)

    for bit in bits[2:]:
        payload = payload + exchange(payload, "seq", bit)
    final_states = payload[:state_rows].astype(F32).reshape(REQS, heads, DK, DK)
    edges = payload[state_rows:].reshape(3 * heads, EDGE_ROWS, DK)[:, : REQS * (CONV - 1)]
    conv_edges = edges.transpose(1, 0, 2).reshape(REQS, CONV - 1, 3, width)
    return (projected, stream_out, final_states, conv_edges)


def solution(mesh):
    return jax.shard_map(
        body,
        mesh=mesh,
        in_specs=(
            P("seq", None, ("win", "wout")),
            P(None, None, ("win", "wout")),
            P(("win", "wout"), "seq"),
            P(),
            P(),
            P(("win", "wout"), None),
            P(("seq", "win", "wout"), None),
            P(),
            P("win", "wout"),
        ),
        out_specs=(
            P(("seq", "win"), "wout"),
            P(("seq", "win", "wout"), None),
            P(None, ("win", "wout"), None, None),
            P(None, None, None, ("win", "wout")),
        ),
        check_vma=False,
    )
```

```python
import functools

import jax
import jax.numpy as jnp
from jax import lax
from jax.experimental import pallas as pl
from jax.experimental.pallas import tpu as pltpu
from jax.sharding import PartitionSpec as P

DK = 128
CONV = 4
REQS = 4
HALO = 16
ROW = 4
EDGE_ROWS = 16
INTERPRET = False
F32 = jnp.float32
BF16 = jnp.bfloat16
NN = ((1,), (0,))
NT = ((1,), (1,))
TN = ((0,), (0,))
VMEM = pl.BlockSpec(memory_space=pltpu.VMEM)
SMEM = pl.BlockSpec(memory_space=pltpu.SMEM)
HBM = pl.BlockSpec(memory_space=pltpu.HBM)


def shift(value, axis, steps):
    count = lax.axis_size(axis)
    return lax.ppermute(value, axis, [(s, s + steps) for s in range(max(0, count - steps))])


def rotate(value, axis, steps):
    count = lax.axis_size(axis)
    return lax.ppermute(value, axis, [(s, (s + steps) % count) for s in range(count)])


def row_rotate(value, steps):
    count = lax.axis_size("seq")
    pairs = [(s, s // ROW * ROW + (s + steps) % ROW) for s in range(count)]
    return lax.ppermute(value, "seq", pairs)


def exchange(value, axis, bit):
    return lax.ppermute(value, axis, [(s, s ^ bit) for s in range(lax.axis_size(axis))])


def dot(left, right, dims=NN):
    return lax.dot_general(left, right, (dims, ((), ())), preferred_element_type=F32)


def split(value):
    high = value.astype(BF16)
    return high, (value - high.astype(F32)).astype(BF16)


def dot_split(left, right, dims=NN):
    lh, ll = left
    rh, rl = right
    return dot(lh, rh, dims) + (dot(lh, rl, dims) + dot(ll, rh, dims))


def dot32(left, right, dims=NN):
    return dot_split(split(left), split(right), dims)


def call(kernel, outs, name, flops, *args, scratch=(), smem=1, hbm=0):
    size = sum(a.size * a.dtype.itemsize for a in args) + sum(
        o.size * o.dtype.itemsize for o in outs
    )
    return pl.pallas_call(
        kernel,
        out_shape=outs,
        in_specs=[SMEM] * smem + [HBM] * hbm + [VMEM] * (len(args) - smem - hbm),
        out_specs=[VMEM] * len(outs),
        scratch_shapes=list(scratch),
        name=name,
        interpret=INTERPRET,
        cost_estimate=pl.CostEstimate(flops=flops, bytes_accessed=size, transcendentals=0),
        compiler_params=pltpu.CompilerParams(vmem_limit_bytes=40 * 1024 * 1024),
    )(*args)


def in_hbm(value):
    return value if INTERPRET else pltpu.with_memory_space_constraint(value, pltpu.HBM)


def out(shape, dtype):
    return jax.ShapeDtypeStruct(shape, dtype)


def request_ends(meta):
    ends = [meta[0]]
    for r in range(1, REQS):
        ends.append(ends[-1] + meta[r])
    return ends


def seg_of(pos, ends):
    total = jnp.where(pos >= ends[0], 1, 0)
    for r in range(1, REQS):
        total = total + jnp.where(pos >= ends[r], 1, 0)
    return total


def start_of(pos, ends):
    begin = jnp.where(pos >= ends[0], ends[0], 0)
    for r in range(1, REQS):
        begin = jnp.maximum(begin, jnp.where(pos >= ends[r], ends[r], 0))
    return begin


def iota(shape, dim):
    return lax.broadcasted_iota(jnp.int32, shape, dim)


def conv_rows(ext, taps, pos, begin):
    pre = ext[HALO:] * taps[CONV - 1 : CONV]
    for back in range(1, CONV):
        moved = pltpu.roll(ext, back, 0)[HALO:]
        ok = jnp.where(pos - back >= begin, 1.0, 0.0).astype(F32)
        pre = pre + moved * taps[CONV - 1 - back : CONV - back] * ok
    return (pre / (1.0 + jnp.exp(-pre))).astype(BF16)


def edge_select(meta, ends, first, last, ext_pos):
    edge_id = iota((EDGE_ROWS, 1), 0)
    wanted = jnp.full((EDGE_ROWS, 1), -1, jnp.int32)
    for r in range(REQS):
        begin = ends[r] - meta[r]
        owned = (ends[r] - 1 >= first) & (ends[r] - 1 <= last)
        for i in range(CONV - 1):
            spot = ends[r] - (CONV - 1) + i
            good = owned & (spot >= begin)
            wanted = jnp.where(edge_id == i * REQS + r, jnp.where(good, spot, -1), wanted)
    return jnp.where((ext_pos == wanted) & (ext_pos >= 0), 1.0, 0.0).astype(BF16)


def conv_kernel(
    meta, x_hbm, taps_hbm, beta_hbm,
    act_ref, head_ref, edge_ref, taps_ref, beta_ref, x_ref, sems,
):
    copies = [
        pltpu.make_async_copy(x_hbm, x_ref, sems.at[0]),
        pltpu.make_async_copy(taps_hbm, taps_ref, sems.at[1]),
        pltpu.make_async_copy(beta_hbm, beta_ref, sems.at[2]),
    ]
    for copy in copies:
        copy.start()
    for copy in copies:
        copy.wait()
    rows = x_ref.shape[1]
    ends = request_ends(meta)
    first = meta[4]
    pos = first + iota((rows, 1), 0)
    begin = start_of(pos, ends)
    select = edge_select(
        meta, ends, first, first + rows - 1, first + iota((EDGE_ROWS, rows), 1)
    )
    for c in range(3):
        x = x_ref[c]
        edge_ref[c] = dot(select, x).astype(BF16)
        head_ref[c] = x[:HALO]
        wide = x.astype(F32)
        act_ref[c, HALO:] = conv_rows(wide, taps_ref[c], pos[HALO:], begin[HALO:])
        act_ref[c, :HALO] = jnp.zeros((HALO, x.shape[1]), BF16)


def prep_kernel(
    meta, act_ref, head_ref, part_ref, taps_ref, beta_ref, halo_ref,
    map_ref, uw_ref, local_ref, link_ref, kb_ref, ks_ref, edge_ref,
):
    rows = act_ref.shape[1]
    heads = act_ref.shape[2] // DK
    half = rows // 2
    ends = request_ends(meta)
    first = meta[4]
    pos = first + iota((rows, 1), 0)
    pos_r = first + iota((1, rows), 1)
    seg = seg_of(pos, ends)
    seg_r = seg_of(pos_r, ends)
    begin = start_of(pos, ends)
    coupled = jnp.where(begin < first, 1.0, 0.0).astype(F32)
    last = first + rows - 1
    last_seg = seg_of(last, ends)
    last_link = start_of(last, ends) < first
    in_last = jnp.where(seg == last_seg, 1.0, 0.0).astype(F32)
    select = edge_select(meta, ends, first, last, first - HALO + iota((EDGE_ROWS, HALO), 1))

    planes = []
    for c in range(3):
        halo = halo_ref[c]
        picked = part_ref[c] + dot(select, halo).astype(BF16)
        for b in range(heads):
            edge_ref[c * heads + b] = picked[:, b * DK : (b + 1) * DK]
        ext = jnp.concatenate([halo, head_ref[c]], axis=0).astype(F32)
        lead = conv_rows(ext, taps_ref[c], pos[:HALO], begin[:HALO])
        planes.append(jnp.concatenate([lead, act_ref[c, HALO:]], axis=0))

    row_id = iota((rows, rows), 0)
    col_id = iota((rows, rows), 1)
    same = seg == seg_r
    strict = same & (row_id > col_id)
    causal = same & (row_id >= col_id)
    diag = row_id == col_id
    row_h = iota((half, half), 0)
    col_h = iota((half, half), 1)
    eye_h = jnp.where(row_h == col_h, 1.0, 0.0).astype(F32)

    def as_row(column):
        return jnp.sum(jnp.where(diag, column, 0.0), axis=0, keepdims=True)

    def as_column(row):
        return jnp.sum(jnp.where(diag, row, 0.0), axis=1, keepdims=True)

    state = []
    for h in range(heads):
        lanes = slice(h * DK, (h + 1) * DK)
        qb, kb, vb = (planes[c][:, lanes] for c in range(3))
        q32, k32, v32 = (t.astype(F32) for t in (qb, kb, vb))
        qs = lax.rsqrt(jnp.sum(q32 * q32, axis=1, keepdims=True) + 1e-06)
        ks = lax.rsqrt(jnp.sum(k32 * k32, axis=1, keepdims=True) + 1e-06)
        ks_row = as_row(ks)
        beta = as_column(1.0 / (1.0 + jnp.exp(-beta_ref[h : h + 1, :])))
        system = jnp.where(strict, dot(kb, kb, NT) * (beta * ks) * ks_row, 0.0)
        scores = jnp.where(causal, dot(qb, kb, NT) * qs * ks_row, 0.0)
        targets = jnp.concatenate([beta * v32, (beta * coupled * ks) * k32], axis=1)
        state.append((q32 * qs, kb, ks, system, scores, targets))

    blocks = []
    for h in range(heads):
        system = state[h][3]
        for d in range(2):
            blocks.append(system[d * half : (d + 1) * half, d * half : (d + 1) * half])
    inverses = []
    low = ((row_h ^ col_h) == 1) & (row_h > col_h)
    for a in blocks:
        inverses.append(eye_h - jnp.where(low, a, 0.0))
    level = 1
    while (2 << level) <= half:
        low = (((row_h >> level) ^ (col_h >> level)) == 1) & (row_h > col_h)
        parts = [split(x) for x in inverses]
        inner = [dot_split(split(jnp.where(low, a, 0.0)), p) for a, p in zip(blocks, parts)]
        inverses = [x - dot_split(p, split(t)) for x, p, t in zip(inverses, parts, inner)]
        level += 1

    for h in range(heads):
        q32, kb, ks, system, scores, targets = state[h]
        top = dot32(inverses[2 * h], targets[:half])
        rest = targets[half:] - dot32(system[half:, :half], top)
        uw = jnp.concatenate([top, dot32(inverses[2 * h + 1], rest)], axis=0)
        uw_ref[h] = uw
        mixed = dot32(scores, uw)
        local_ref[h] = mixed[:, :DK]
        link_ref[h] = coupled * q32 - mixed[:, DK:]
        kb_ref[h] = kb
        ks_ref[h] = ks
        scaled = jnp.concatenate([uw[:, DK:] * ks, uw[:, :DK] * (ks * in_last)], axis=1)
        high, less = split(scaled)
        fold = dot(kb, high, TN) + dot(kb, less, TN)
        eye_k = jnp.where(iota((DK, DK), 0) == iota((DK, DK), 1), 1.0, 0.0).astype(F32)
        map_ref[h, :, :DK] = jnp.where(last_link, fold[:, :DK], eye_k).astype(BF16)
        map_ref[h, :, DK:] = fold[:, DK:].astype(BF16)


def joined(newer, older):
    return newer + older - dot32(newer[:, :DK], older)


def row_kernel(meta, own_ref, *refs):
    *came, prefix_ref, send_ref, maps_ref = refs
    here = meta[7]
    maps_ref[here] = own_ref[...]
    for k, ref in enumerate(came):
        maps_ref[lax.rem(here + ROW - 1 - k, ROW)] = ref[...]
    for h in range(own_ref.shape[0]):
        maps = [maps_ref[i, h] for i in range(ROW)]
        wide = [m.astype(F32) for m in maps]
        first = wide[1] + wide[0] - dot(maps[1][:, :DK], maps[0])
        second = wide[3] + wide[2] - dot(maps[3][:, :DK], maps[2])
        send_ref[h] = joined(second, first).astype(BF16)
        third = joined(wide[2], first)
        prefix = jnp.where(here == 1, wide[0], jnp.where(here == 2, first, third))
        prefix_ref[h] = jnp.where(here == 0, 0.0, prefix)


def join_kernel(near_ref, far_ref, wide_ref, tail_ref):
    for h in range(near_ref.shape[0]):
        near, far = near_ref[h], far_ref[h]
        both = near.astype(F32) + far.astype(F32) - dot(near[:, :DK], far)
        wide_ref[h] = both
        tail_ref[h] = both[:, DK:].astype(BF16)


def attend_kernel(
    meta, prefix_ref, wide_ref, tail_ref, uw_ref, local_ref, link_ref, kb_ref, ks_ref,
    edge_ref, gain_ref, w_ref, own_ref, other_ref, pay_ref, heads_ref,
):
    heads, rows, _ = local_ref.shape
    wins, cores, piece, _ = heads_ref.shape
    ends = request_ends(meta)
    first, win, core = meta[4], meta[5], meta[6]
    last = first + rows - 1
    seg = seg_of(first + iota((rows, 1), 0), ends)
    gain = gain_ref[...]
    for h in range(heads):
        wide, prefix, tail = wide_ref[h], prefix_ref[h], tail_ref[h].astype(F32)
        ahead = wide[:, DK:] + tail - dot32(wide[:, :DK], tail)
        enter = prefix[:, DK:] + ahead - dot32(prefix[:, :DK], ahead)
        parts = split(enter)
        attended = local_ref[h] + dot_split(split(link_ref[h]), parts)
        scale = lax.rsqrt(jnp.mean(attended * attended, axis=1, keepdims=True) + 1e-05)
        normed = attended * scale * gain
        lanes = slice(h * DK, (h + 1) * DK)
        for p in range(wins * cores):
            heads_ref[p // cores, p % cores, :, lanes] = normed[p * piece : (p + 1) * piece].astype(
                BF16
            )
        uw = uw_ref[h]
        corrected = (uw[:, :DK] - dot_split(split(uw[:, DK:]), parts)) * ks_ref[h]
        for r in range(REQS):
            owned = (ends[r] - 1 >= first) & (ends[r] - 1 <= last)
            carried = owned & (ends[r] - meta[r] < first)
            member = (seg == r) & owned
            high, less = split(jnp.where(member, corrected, 0.0))
            final = dot(kb_ref[h], high, TN) + dot(kb_ref[h], less, TN)
            final = final + jnp.where(carried, enter, 0.0)
            spot = (r * heads + h) * DK
            pay_ref[spot : spot + DK, :] = final.astype(BF16)
    base = REQS * heads * DK
    for b in range(edge_ref.shape[0]):
        pay_ref[base + b * EDGE_ROWS : base + (b + 1) * EDGE_ROWS, :] = edge_ref[b]
    order = [lax.rem(win + k, wins) for k in range(wins)]
    w = w_ref[...]
    mine = jnp.concatenate([heads_ref[o, core] for o in order], axis=0)
    own_ref[...] = dot(mine, w)
    theirs = jnp.concatenate([heads_ref[o, cores - 1 - core] for o in order], axis=0)
    other_ref[...] = dot(theirs, w).astype(BF16)


def pair_kernel(own_ref, got_ref, keep_ref, *send_refs):
    piece = keep_ref.shape[0]
    keep_ref[...] = own_ref[:piece] + got_ref[:piece].astype(F32)
    for k, ref in enumerate(send_refs):
        part = slice((k + 1) * piece, (k + 2) * piece)
        ref[...] = (own_ref[part] + got_ref[part].astype(F32)).astype(BF16)


def norm_kernel(hidden_ref, gain_ref, pay_ref, came_ref, keep_ref, *refs):
    *got, stream_ref, normed_ref, sum_ref = refs
    total = keep_ref[...]
    for ref in got:
        total = total + ref[...].astype(F32)
    total = hidden_ref[...].astype(F32) + total
    stream_ref[...] = total.astype(BF16)
    scale = lax.rsqrt(jnp.mean(total * total, axis=1, keepdims=True) + 1e-05)
    normed_ref[...] = (total * scale * gain_ref[...]).astype(BF16)
    sum_ref[...] = pay_ref[...] + came_ref[...]


def columns_kernel(meta, mine_ref, peer_ref, *refs):
    *piece_refs, cols_ref = refs
    wins, rows, width = cols_ref.shape
    mine, peer = mine_ref[...], peer_ref[...]
    lower = jnp.where(meta[6] == 0, mine, peer)
    upper = jnp.where(meta[6] == 0, peer, mine)
    for k in range(wins):
        cols_ref[k, : rows // 2] = lower[:, k * width : (k + 1) * width]
        cols_ref[k, rows // 2 :] = upper[:, k * width : (k + 1) * width]
    for k, ref in enumerate(piece_refs):
        ref[...] = cols_ref[lax.rem(meta[5] + k, wins)]


def finish_kernel(pay_ref, came_ref, state_ref, edge_ref):
    rows = state_ref.shape[0]
    state_ref[...] = (pay_ref[:rows] + came_ref[:rows]).astype(F32)
    heads = edge_ref.shape[3] // DK
    for b in range(3 * heads):
        part = slice(rows + b * EDGE_ROWS, rows + (b + 1) * EDGE_ROWS)
        edges = pay_ref[part].astype(F32) + came_ref[part].astype(F32)
        lanes = slice(b % heads * DK, (b % heads + 1) * DK)
        for i in range(CONV - 1):
            edge_ref[i, b // heads, :, lanes] = edges[i * REQS : (i + 1) * REQS].astype(BF16)


def body(qkv_in, conv_w, beta_logits, lengths, out_gain, w_out, hidden_in, norm_gain, w_qkv):
    rows = qkv_in.shape[0]
    width = qkv_in.shape[2]
    heads = width // DK
    model = w_out.shape[1]
    n_seq, wins, cores = (lax.axis_size(a) for a in ("seq", "win", "wout"))
    piece = rows // (wins * cores)
    seq, win, core = (lax.axis_index(a).astype(jnp.int32) for a in ("seq", "win", "wout"))
    meta = jnp.concatenate([lengths, jnp.stack([seq * rows, win, core, seq % ROW])])
    x = qkv_in.transpose(1, 0, 2)
    halo = shift(x[:, rows - HALO :], "seq", 1)
    act, lead, parts, taps, beta = call(
        conv_kernel,
        [
            out((3, rows, width), BF16),
            out((3, HALO, width), BF16),
            out((3, EDGE_ROWS, width), BF16),
            out((3, CONV, width), F32),
            out((heads, rows), F32),
        ],
        "conv",
        10**8,
        meta, *(in_hbm(a) for a in (x, conv_w, beta_logits)),
        scratch=[pltpu.VMEM((3, rows, width), BF16), pltpu.SemaphoreType.DMA((3,))],
        hbm=3,
    )
    maps, uw, local, link, kb, ks, edges = call(
        prep_kernel,
        [
            out((heads, DK, 2 * DK), BF16),
            out((heads, rows, 2 * DK), F32),
            out((heads, rows, DK), F32),
            out((heads, rows, DK), F32),
            out((heads, rows, DK), BF16),
            out((heads, rows, 1), F32),
            out((3 * heads, EDGE_ROWS, DK), BF16),
        ],
        "prep",
        2 * 10**9,
        meta, act, lead, parts, taps, beta, halo,
    )

    came = [row_rotate(maps, k) for k in range(1, ROW)]
    prefix, total = call(
        row_kernel,
        [out((heads, DK, 2 * DK), F32), out((heads, DK, 2 * DK), BF16)],
        "row",
        10**8,
        meta, maps, *came,
        scratch=[pltpu.VMEM((ROW, heads, DK, 2 * DK), BF16)],
    )
    wide, tail = call(
        join_kernel,
        [out((heads, DK, 2 * DK), F32), out((heads, DK, DK), BF16)],
        "join",
        10**8,
        shift(total, "seq", ROW), shift(total, "seq", 2 * ROW),
        smem=0,
    )
    tail = shift(tail, "seq", 2 * ROW)
    state_rows = REQS * heads * DK
    pay_rows = state_rows + 3 * heads * EDGE_ROWS
    own, other, payload = call(
        attend_kernel,
        [
            out((wins * piece, model), F32),
            out((wins * piece, model), BF16),
            out((pay_rows, DK), BF16),
        ],
        "attend",
        10**9,
        meta, prefix, wide, tail, uw, local, link, kb, ks, edges, out_gain.reshape(1, DK), w_out,
        scratch=[pltpu.VMEM((wins, cores, piece, width), BF16)],
    )
    got = rotate(other, "wout", 1)
    bits = [1 << b for b in reversed(range((n_seq - 1).bit_length()))]
    came = exchange(payload, "seq", bits[0])
    sums = call(
        pair_kernel,
        [out((piece, model), F32)] + [out((piece, model), BF16)] * (wins - 1),
        "pair",
        10**6,
        own, got,
        smem=0,
    )
    reduced = [rotate(sums[k], "win", k) for k in range(1, wins)]
    stream_out, normed, payload = call(
        norm_kernel,
        [out((piece, model), BF16), out((piece, model), BF16), out((pay_rows, DK), BF16)],
        "norm",
        10**6,
        hidden_in, norm_gain.reshape(1, model), payload, came, sums[0], *reduced,
        smem=0,
    )
    peer = rotate(normed, "wout", 1)
    came = exchange(payload, "seq", bits[1])
    cols = call(
        columns_kernel,
        [out((2 * piece, model // wins), BF16)] * wins,
        "columns",
        10**6,
        meta, normed, peer,
        scratch=[pltpu.VMEM((wins, 2 * piece, model // wins), BF16)],
    )
    blocks = [cols[0]] + [rotate(cols[k], "win", k) for k in range(1, wins)]
    *blocks, payload = lax.optimization_barrier((*blocks, payload + came))

    def partial(k):
        return jnp.dot(blocks[(wins - k) % wins], w_qkv, preferred_element_type=F32)

    arrived = [rotate(partial(k).astype(BF16), "win", k) for k in range(1, wins)]
    total = partial(0)
    for part in arrived:
        total = total + part.astype(F32)
    projected = total.astype(BF16)

    for bit in bits[2:-1]:
        payload = payload + exchange(payload, "seq", bit)
    final_states, conv_edges = call(
        finish_kernel,
        [out((state_rows, DK), F32), out((CONV - 1, 3, REQS, width), BF16)],
        "finish",
        10**6,
        payload, exchange(payload, "seq", bits[-1]),
        smem=0,
    )
    final_states = final_states.reshape(REQS, heads, DK, DK)
    conv_edges = conv_edges.transpose(2, 0, 1, 3)
    return (projected, stream_out, final_states, conv_edges)


def solution(mesh):
    return jax.shard_map(
        body,
        mesh=mesh,
        in_specs=(
            P("seq", None, ("win", "wout")),
            P(None, None, ("win", "wout")),
            P(("win", "wout"), "seq"),
            P(),
            P(),
            P(("win", "wout"), None),
            P(("seq", "win", "wout"), None),
            P(),
            P("win", "wout"),
        ),
        out_specs=(
            P(("seq", "win"), "wout"),
            P(("seq", "win", "wout"), None),
            P(None, ("win", "wout"), None, None),
            P(None, None, None, ("win", "wout")),
        ),
        check_vma=False,
    )
```

```python
import functools

import jax
import jax.numpy as jnp
from jax import lax
from jax.experimental import pallas as pl
from jax.experimental.pallas import tpu as pltpu
from jax.sharding import PartitionSpec as P

DK = 128
CONV = 4
REQS = 4
HALO = 16
ROW = 4
EDGE_ROWS = 16
INTERPRET = False
F32 = jnp.float32
BF16 = jnp.bfloat16
NN = ((1,), (0,))
NT = ((1,), (1,))
TN = ((0,), (0,))
VMEM = pl.BlockSpec(memory_space=pltpu.VMEM)
SMEM = pl.BlockSpec(memory_space=pltpu.SMEM)
HBM = pl.BlockSpec(memory_space=pltpu.HBM)


def shift(value, axis, steps):
    count = lax.axis_size(axis)
    return lax.ppermute(value, axis, [(s, s + steps) for s in range(max(0, count - steps))])


def rotate(value, axis, steps):
    count = lax.axis_size(axis)
    return lax.ppermute(value, axis, [(s, (s + steps) % count) for s in range(count)])


def exchange(value, axis, bit):
    return lax.ppermute(value, axis, [(s, s ^ bit) for s in range(lax.axis_size(axis))])


def dot(left, right, dims=NN):
    return lax.dot_general(left, right, (dims, ((), ())), preferred_element_type=F32)


def split(value):
    high = value.astype(BF16)
    return high, (value - high.astype(F32)).astype(BF16)


def dot_split(left, right, dims=NN):
    lh, ll = left
    rh, rl = right
    return dot(lh, rh, dims) + (dot(lh, rl, dims) + dot(ll, rh, dims))


def dot32(left, right, dims=NN):
    return dot_split(split(left), split(right), dims)


def call(kernel, outs, name, flops, *args, scratch=(), smem=1, hbm=0):
    size = sum(a.size * a.dtype.itemsize for a in args) + sum(
        o.size * o.dtype.itemsize for o in outs
    )
    return pl.pallas_call(
        kernel,
        out_shape=outs,
        in_specs=[SMEM] * smem + [HBM] * hbm + [VMEM] * (len(args) - smem - hbm),
        out_specs=[VMEM] * len(outs),
        scratch_shapes=list(scratch),
        name=name,
        interpret=INTERPRET,
        cost_estimate=pl.CostEstimate(flops=flops, bytes_accessed=size, transcendentals=0),
        compiler_params=pltpu.CompilerParams(vmem_limit_bytes=40 * 1024 * 1024),
    )(*args)


def in_hbm(value):
    return value if INTERPRET else pltpu.with_memory_space_constraint(value, pltpu.HBM)


def out(shape, dtype):
    return jax.ShapeDtypeStruct(shape, dtype)


def request_ends(meta):
    ends = [meta[0]]
    for r in range(1, REQS):
        ends.append(ends[-1] + meta[r])
    return ends


def seg_of(pos, ends):
    total = jnp.where(pos >= ends[0], 1, 0)
    for r in range(1, REQS):
        total = total + jnp.where(pos >= ends[r], 1, 0)
    return total


def start_of(pos, ends):
    begin = jnp.where(pos >= ends[0], ends[0], 0)
    for r in range(1, REQS):
        begin = jnp.maximum(begin, jnp.where(pos >= ends[r], ends[r], 0))
    return begin


def iota(shape, dim):
    return lax.broadcasted_iota(jnp.int32, shape, dim)


def conv_rows(ext, taps, pos, begin):
    pre = ext[HALO:] * taps[CONV - 1 : CONV]
    for back in range(1, CONV):
        moved = pltpu.roll(ext, back, 0)[HALO:]
        ok = jnp.where(pos - back >= begin, 1.0, 0.0).astype(F32)
        pre = pre + moved * taps[CONV - 1 - back : CONV - back] * ok
    return (pre / (1.0 + jnp.exp(-pre))).astype(BF16)


def edge_select(meta, ends, first, last, ext_pos):
    edge_id = iota((EDGE_ROWS, 1), 0)
    wanted = jnp.full((EDGE_ROWS, 1), -1, jnp.int32)
    for r in range(REQS):
        begin = ends[r] - meta[r]
        owned = (ends[r] - 1 >= first) & (ends[r] - 1 <= last)
        for i in range(CONV - 1):
            spot = ends[r] - (CONV - 1) + i
            good = owned & (spot >= begin)
            wanted = jnp.where(edge_id == i * REQS + r, jnp.where(good, spot, -1), wanted)
    return jnp.where((ext_pos == wanted) & (ext_pos >= 0), 1.0, 0.0).astype(BF16)


def conv_kernel(
    meta, x_hbm, taps_hbm, beta_hbm,
    act_ref, head_ref, edge_ref, taps_ref, beta_ref, x_ref, sems,
):
    copies = [
        pltpu.make_async_copy(x_hbm, x_ref, sems.at[0]),
        pltpu.make_async_copy(taps_hbm, taps_ref, sems.at[1]),
        pltpu.make_async_copy(beta_hbm, beta_ref, sems.at[2]),
    ]
    for copy in copies:
        copy.start()
    for copy in copies:
        copy.wait()
    rows = x_ref.shape[1]
    ends = request_ends(meta)
    first = meta[4]
    pos = first + iota((rows, 1), 0)
    begin = start_of(pos, ends)
    select = edge_select(
        meta, ends, first, first + rows - 1, first + iota((EDGE_ROWS, rows), 1)
    )
    for c in range(3):
        x = x_ref[c]
        edge_ref[c] = dot(select, x).astype(BF16)
        head_ref[c] = x[:HALO]
        wide = x.astype(F32)
        act_ref[c, HALO:] = conv_rows(wide, taps_ref[c], pos[HALO:], begin[HALO:])
        act_ref[c, :HALO] = jnp.zeros((HALO, x.shape[1]), BF16)


def prep_kernel(
    meta, act_ref, head_ref, part_ref, taps_ref, beta_ref, halo_ref,
    map_ref, uw_ref, local_ref, link_ref, kb_ref, ks_ref, edge_ref,
):
    rows = act_ref.shape[1]
    heads = act_ref.shape[2] // DK
    half = rows // 2
    ends = request_ends(meta)
    first = meta[4]
    pos = first + iota((rows, 1), 0)
    pos_r = first + iota((1, rows), 1)
    seg = seg_of(pos, ends)
    seg_r = seg_of(pos_r, ends)
    begin = start_of(pos, ends)
    coupled = jnp.where(begin < first, 1.0, 0.0).astype(F32)
    last = first + rows - 1
    last_seg = seg_of(last, ends)
    last_link = start_of(last, ends) < first
    in_last = jnp.where(seg == last_seg, 1.0, 0.0).astype(F32)
    select = edge_select(meta, ends, first, last, first - HALO + iota((EDGE_ROWS, HALO), 1))

    planes = []
    for c in range(3):
        halo = halo_ref[c]
        picked = part_ref[c] + dot(select, halo).astype(BF16)
        for b in range(heads):
            edge_ref[c * heads + b] = picked[:, b * DK : (b + 1) * DK]
        ext = jnp.concatenate([halo, head_ref[c]], axis=0).astype(F32)
        lead = conv_rows(ext, taps_ref[c], pos[:HALO], begin[:HALO])
        planes.append(jnp.concatenate([lead, act_ref[c, HALO:]], axis=0))

    row_id = iota((rows, rows), 0)
    col_id = iota((rows, rows), 1)
    same = seg == seg_r
    strict = same & (row_id > col_id)
    causal = same & (row_id >= col_id)
    diag = row_id == col_id
    row_h = iota((half, half), 0)
    col_h = iota((half, half), 1)
    eye_h = jnp.where(row_h == col_h, 1.0, 0.0).astype(F32)

    def as_row(column):
        return jnp.sum(jnp.where(diag, column, 0.0), axis=0, keepdims=True)

    def as_column(row):
        return jnp.sum(jnp.where(diag, row, 0.0), axis=1, keepdims=True)

    state = []
    for h in range(heads):
        lanes = slice(h * DK, (h + 1) * DK)
        qb, kb, vb = (planes[c][:, lanes] for c in range(3))
        q32, k32, v32 = (t.astype(F32) for t in (qb, kb, vb))
        qs = lax.rsqrt(jnp.sum(q32 * q32, axis=1, keepdims=True) + 1e-06)
        ks = lax.rsqrt(jnp.sum(k32 * k32, axis=1, keepdims=True) + 1e-06)
        ks_row = as_row(ks)
        beta = as_column(1.0 / (1.0 + jnp.exp(-beta_ref[h : h + 1, :])))
        system = jnp.where(strict, dot(kb, kb, NT) * (beta * ks) * ks_row, 0.0)
        scores = jnp.where(causal, dot(qb, kb, NT) * qs * ks_row, 0.0)
        targets = jnp.concatenate([beta * v32, (beta * coupled * ks) * k32], axis=1)
        state.append((q32 * qs, kb, ks, system, scores, targets))

    blocks = []
    for h in range(heads):
        system = state[h][3]
        for d in range(2):
            blocks.append(system[d * half : (d + 1) * half, d * half : (d + 1) * half])
    inverses = []
    low = ((row_h ^ col_h) == 1) & (row_h > col_h)
    for a in blocks:
        inverses.append(eye_h - jnp.where(low, a, 0.0))
    level = 1
    while (2 << level) <= half:
        low = (((row_h >> level) ^ (col_h >> level)) == 1) & (row_h > col_h)
        parts = [split(x) for x in inverses]
        inner = [dot_split(split(jnp.where(low, a, 0.0)), p) for a, p in zip(blocks, parts)]
        inverses = [x - dot_split(p, split(t)) for x, p, t in zip(inverses, parts, inner)]
        level += 1

    for h in range(heads):
        q32, kb, ks, system, scores, targets = state[h]
        top = dot32(inverses[2 * h], targets[:half])
        rest = targets[half:] - dot32(system[half:, :half], top)
        uw = jnp.concatenate([top, dot32(inverses[2 * h + 1], rest)], axis=0)
        uw_ref[h] = uw
        mixed = dot32(scores, uw)
        local_ref[h] = mixed[:, :DK]
        link_ref[h] = coupled * q32 - mixed[:, DK:]
        kb_ref[h] = kb
        ks_ref[h] = ks
        scaled = jnp.concatenate([uw[:, DK:] * ks, uw[:, :DK] * (ks * in_last)], axis=1)
        high, less = split(scaled)
        fold = dot(kb, high, TN) + dot(kb, less, TN)
        eye_k = jnp.where(iota((DK, DK), 0) == iota((DK, DK), 1), 1.0, 0.0).astype(F32)
        map_ref[h, :, :DK] = jnp.where(last_link, fold[:, :DK], eye_k).astype(BF16)
        map_ref[h, :, DK:] = fold[:, DK:].astype(BF16)


def joined(newer, older):
    return newer.astype(F32) + older.astype(F32) - dot(newer[:, :DK], older)


def twin_kernel(meta, own_ref, came_ref, twin_ref):
    odd = lax.rem(meta[7], 2) == 1
    for h in range(own_ref.shape[0]):
        own, came = own_ref[h], came_ref[h]
        newer = jnp.where(odd, own, came)
        older = jnp.where(odd, came, own)
        twin_ref[h] = joined(newer, older).astype(BF16)


def row_kernel(meta, own_ref, came_ref, twin_ref, other_ref, prefix_ref, total_ref):
    here = meta[7]
    late = here >= ROW // 2
    odd = lax.rem(here, 2) == 1
    for h in range(own_ref.shape[0]):
        twin, other = twin_ref[h], other_ref[h]
        older = jnp.where(late, other, twin)
        total_ref[h] = joined(jnp.where(late, twin, other), older).astype(BF16)
        step = jnp.where(odd, came_ref[h], jnp.zeros_like(twin))
        prefix_ref[h] = joined(step, jnp.where(late, other, jnp.zeros_like(twin)))


def join_kernel(total_ref, near_ref, both_ref, tail_ref):
    for h in range(total_ref.shape[0]):
        both = joined(total_ref[h], near_ref[h]).astype(BF16)
        both_ref[h] = both
        tail_ref[h] = both[:, DK:]


def quarter_of(here):
    return lax.rem((here + 1) // 2, 2) * 2 + here // 2


def attend_kernel(
    meta, prefix_ref, wide_ref, tail_ref, uw_ref, local_ref, link_ref, kb_ref, ks_ref,
    edge_ref, gain_ref, w_ref, own_ref, other_ref, keep_ref, give_ref, heads_ref, pay_ref,
):
    heads, rows, _ = local_ref.shape
    wins, cores, piece, _ = heads_ref.shape
    ends = request_ends(meta)
    first, win, core = meta[4], meta[5], meta[6]
    last = first + rows - 1
    seg = seg_of(first + iota((rows, 1), 0), ends)
    gain = gain_ref[...]
    for h in range(heads):
        wide, prefix, tail = wide_ref[h], prefix_ref[h], tail_ref[h]
        ahead = wide[:, DK:].astype(F32) + tail.astype(F32) - dot(wide[:, :DK], tail)
        enter = prefix[:, DK:] + ahead - dot32(prefix[:, :DK], ahead)
        parts = split(enter)
        attended = local_ref[h] + dot_split(split(link_ref[h]), parts)
        scale = lax.rsqrt(jnp.mean(attended * attended, axis=1, keepdims=True) + 1e-05)
        normed = attended * scale * gain
        lanes = slice(h * DK, (h + 1) * DK)
        for p in range(wins * cores):
            heads_ref[p // cores, p % cores, :, lanes] = normed[p * piece : (p + 1) * piece].astype(
                BF16
            )
        uw = uw_ref[h]
        corrected = (uw[:, :DK] - dot_split(split(uw[:, DK:]), parts)) * ks_ref[h]
        for r in range(REQS):
            owned = (ends[r] - 1 >= first) & (ends[r] - 1 <= last)
            carried = owned & (ends[r] - meta[r] < first)
            member = (seg == r) & owned
            high, less = split(jnp.where(member, corrected, 0.0))
            final = dot(kb_ref[h], high, TN) + dot(kb_ref[h], less, TN)
            final = final + jnp.where(carried, enter, 0.0)
            spot = (r * heads + h) * DK
            pay_ref[spot : spot + DK, :] = final.astype(BF16)
    base = REQS * heads * DK
    for b in range(edge_ref.shape[0]):
        pay_ref[base + b * EDGE_ROWS : base + (b + 1) * EDGE_ROWS, :] = edge_ref[b]
    used = base + edge_ref.shape[0] * EDGE_ROWS
    pay_ref[used:, :] = jnp.zeros((pay_ref.shape[0] - used, DK), BF16)
    quarter = keep_ref.shape[0] // 2
    mine = quarter_of(meta[7])
    twin = quarter_of(meta[7] + 1 - 2 * lax.rem(meta[7], 2))
    for ref, spot in ((keep_ref, mine), (give_ref, twin)):
        for part, which in enumerate((spot, spot + 1 - 2 * lax.rem(spot, 2))):
            start = pl.multiple_of(which * quarter, EDGE_ROWS)
            ref[part * quarter : (part + 1) * quarter] = pay_ref[pl.ds(start, quarter), :]
    order = [lax.rem(win + k, wins) for k in range(wins)]
    w = w_ref[...]
    mine = jnp.concatenate([heads_ref[o, core] for o in order], axis=0)
    own_ref[...] = dot(mine, w)
    theirs = jnp.concatenate([heads_ref[o, cores - 1 - core] for o in order], axis=0)
    other_ref[...] = dot(theirs, w).astype(BF16)


def pair_kernel(own_ref, got_ref, pay_ref, came_ref, keep_ref, *refs):
    *send_refs, quarter_ref, give_ref = refs
    piece = keep_ref.shape[0]
    keep_ref[...] = own_ref[:piece] + got_ref[:piece].astype(F32)
    for k, ref in enumerate(send_refs):
        part = slice((k + 1) * piece, (k + 2) * piece)
        ref[...] = (own_ref[part] + got_ref[part].astype(F32)).astype(BF16)
    quarter = quarter_ref.shape[0]
    quarter_ref[...] = pay_ref[:quarter] + came_ref[:quarter]
    give_ref[...] = pay_ref[quarter:] + came_ref[quarter:]


def norm_kernel(hidden_ref, gain_ref, pay_ref, came_ref, keep_ref, *refs):
    *got, stream_ref, normed_ref, sum_ref = refs
    total = keep_ref[...]
    for ref in got:
        total = total + ref[...].astype(F32)
    total = hidden_ref[...].astype(F32) + total
    stream_ref[...] = total.astype(BF16)
    scale = lax.rsqrt(jnp.mean(total * total, axis=1, keepdims=True) + 1e-05)
    normed_ref[...] = (total * scale * gain_ref[...]).astype(BF16)
    sum_ref[...] = pay_ref[...] + came_ref[...]


def columns_kernel(meta, mine_ref, peer_ref, *refs):
    *piece_refs, cols_ref = refs
    wins, rows, width = cols_ref.shape
    mine, peer = mine_ref[...], peer_ref[...]
    lower = jnp.where(meta[6] == 0, mine, peer)
    upper = jnp.where(meta[6] == 0, peer, mine)
    for k in range(wins):
        cols_ref[k, : rows // 2] = lower[:, k * width : (k + 1) * width]
        cols_ref[k, rows // 2 :] = upper[:, k * width : (k + 1) * width]
    for k, ref in enumerate(piece_refs):
        ref[...] = cols_ref[lax.rem(meta[5] + k, wins)]


def finish_kernel(meta, q0_ref, q1_ref, q3_ref, q2_ref, state_ref, edge_ref, pay_ref):
    here = meta[7]
    quarter = q0_ref.shape[0]
    flip = 1 - 2 * lax.rem(here, 2)
    for ref, place in (
        (q0_ref, here),
        (q1_ref, here + flip),
        (q3_ref, ROW - 1 - here),
        (q2_ref, ROW - 1 - here - flip),
    ):
        start = pl.multiple_of(quarter_of(place) * quarter, EDGE_ROWS)
        pay_ref[pl.ds(start, quarter), :] = ref[...]
    rows = state_ref.shape[0]
    state_ref[...] = pay_ref[:rows].astype(F32)
    heads = edge_ref.shape[3] // DK
    for b in range(3 * heads):
        edges = pay_ref[rows + b * EDGE_ROWS : rows + (b + 1) * EDGE_ROWS].astype(F32)
        lanes = slice(b % heads * DK, (b % heads + 1) * DK)
        for i in range(CONV - 1):
            edge_ref[i, b // heads, :, lanes] = edges[i * REQS : (i + 1) * REQS].astype(BF16)


def body(qkv_in, conv_w, beta_logits, lengths, out_gain, w_out, hidden_in, norm_gain, w_qkv):
    rows = qkv_in.shape[0]
    width = qkv_in.shape[2]
    heads = width // DK
    model = w_out.shape[1]
    n_seq, wins, cores = (lax.axis_size(a) for a in ("seq", "win", "wout"))
    piece = rows // (wins * cores)
    seq, win, core = (lax.axis_index(a).astype(jnp.int32) for a in ("seq", "win", "wout"))
    meta = jnp.concatenate([lengths, jnp.stack([seq * rows, win, core, seq % ROW])])
    x = qkv_in.transpose(1, 0, 2)
    halo = shift(x[:, rows - HALO :], "seq", 1)
    act, lead, parts, taps, beta = call(
        conv_kernel,
        [
            out((3, rows, width), BF16),
            out((3, HALO, width), BF16),
            out((3, EDGE_ROWS, width), BF16),
            out((3, CONV, width), F32),
            out((heads, rows), F32),
        ],
        "conv",
        10**8,
        meta, *(in_hbm(a) for a in (x, conv_w, beta_logits)),
        scratch=[pltpu.VMEM((3, rows, width), BF16), pltpu.SemaphoreType.DMA((3,))],
        hbm=3,
    )
    maps, uw, local, link, kb, ks, edges = call(
        prep_kernel,
        [
            out((heads, DK, 2 * DK), BF16),
            out((heads, rows, 2 * DK), F32),
            out((heads, rows, DK), F32),
            out((heads, rows, DK), F32),
            out((heads, rows, DK), BF16),
            out((heads, rows, 1), F32),
            out((3 * heads, EDGE_ROWS, DK), BF16),
        ],
        "prep",
        2 * 10**9,
        meta, act, lead, parts, taps, beta, halo,
    )

    maps_out = out((heads, DK, 2 * DK), BF16)
    came = exchange(maps, "seq", 1)
    (twin,) = call(twin_kernel, [maps_out], "twin", 10**8, meta, maps, came)
    prefix, total = call(
        row_kernel,
        [out((heads, DK, 2 * DK), F32), maps_out],
        "row",
        10**8,
        meta, maps, came, twin, exchange(twin, "seq", ROW - 1),
    )
    both, tail = call(
        join_kernel,
        [maps_out, out((heads, DK, DK), BF16)],
        "join",
        10**8,
        total, shift(total, "seq", ROW),
        smem=0,
    )
    tail = shift(tail, "seq", 3 * ROW)
    wide = shift(both, "seq", ROW)
    state_rows = REQS * heads * DK
    grain = ROW * EDGE_ROWS
    pay_rows = -(-(state_rows + 3 * heads * EDGE_ROWS) // grain) * grain
    half, quarter = out((pay_rows // 2, DK), BF16), out((pay_rows // 4, DK), BF16)
    own, other, keep, give = call(
        attend_kernel,
        [
            out((wins * piece, model), F32),
            out((wins * piece, model), BF16),
            half,
            half,
        ],
        "attend",
        10**9,
        meta, prefix, wide, tail, uw, local, link, kb, ks, edges, out_gain.reshape(1, DK), w_out,
        scratch=[
            pltpu.VMEM((wins, cores, piece, width), BF16),
            pltpu.VMEM((pay_rows, DK), BF16),
        ],
    )
    got = rotate(other, "wout", 1)
    *sums, payload, give = call(
        pair_kernel,
        [out((piece, model), F32)] + [out((piece, model), BF16)] * (wins - 1) + [quarter] * 2,
        "pair",
        10**6,
        own, got, keep, exchange(give, "seq", 1),
        smem=0,
    )
    came = exchange(give, "seq", ROW - 1)
    reduced = [rotate(sums[k], "win", k) for k in range(1, wins)]
    stream_out, normed, payload = call(
        norm_kernel,
        [out((piece, model), BF16), out((piece, model), BF16), quarter],
        "norm",
        10**6,
        hidden_in, norm_gain.reshape(1, model), payload, came, sums[0], *reduced,
        smem=0,
    )
    peer = rotate(normed, "wout", 1)
    bits = [ROW << b for b in reversed(range((n_seq // ROW - 1).bit_length()))]
    came = exchange(payload, "seq", bits[0])
    cols = call(
        columns_kernel,
        [out((2 * piece, model // wins), BF16)] * wins,
        "columns",
        10**6,
        meta, normed, peer,
        scratch=[pltpu.VMEM((wins, 2 * piece, model // wins), BF16)],
    )
    blocks = [cols[0]] + [rotate(cols[k], "win", k) for k in range(1, wins)]
    *blocks, payload = lax.optimization_barrier((*blocks, payload + came))

    def partial(k):
        return jnp.dot(blocks[(wins - k) % wins], w_qkv, preferred_element_type=F32)

    arrived = [rotate(partial(k).astype(BF16), "win", k) for k in range(1, wins)]
    total = partial(0)
    for part in arrived:
        total = total + part.astype(F32)
    projected = total.astype(BF16)

    for bit in bits[1:]:
        payload = payload + exchange(payload, "seq", bit)
    across = exchange(payload, "seq", ROW - 1)
    final_states, conv_edges = call(
        finish_kernel,
        [out((state_rows, DK), F32), out((CONV - 1, 3, REQS, width), BF16)],
        "finish",
        10**6,
        meta, payload, exchange(payload, "seq", 1), across, exchange(across, "seq", 1),
        scratch=[pltpu.VMEM((pay_rows, DK), BF16)],
    )
    final_states = final_states.reshape(REQS, heads, DK, DK)
    conv_edges = conv_edges.transpose(2, 0, 1, 3)
    return (projected, stream_out, final_states, conv_edges)


def solution(mesh):
    return jax.shard_map(
        body,
        mesh=mesh,
        in_specs=(
            P("seq", None, ("win", "wout")),
            P(None, None, ("win", "wout")),
            P(("win", "wout"), "seq"),
            P(),
            P(),
            P(("win", "wout"), None),
            P(("seq", "win", "wout"), None),
            P(),
            P("win", "wout"),
        ),
        out_specs=(
            P(("seq", "win"), "wout"),
            P(("seq", "win", "wout"), None),
            P(None, ("win", "wout"), None, None),
            P(None, None, None, ("win", "wout")),
        ),
        check_vma=False,
    )
```

```python
import functools

import jax
import jax.numpy as jnp
from jax import lax
from jax.experimental import pallas as pl
from jax.experimental.pallas import tpu as pltpu
from jax.sharding import PartitionSpec as P

DK = 128
CONV = 4
REQS = 4
HALO = 16
ROW = 4
EDGE_ROWS = 16
INTERPRET = False
F32 = jnp.float32
BF16 = jnp.bfloat16
NN = ((1,), (0,))
NT = ((1,), (1,))
TN = ((0,), (0,))
VMEM = pl.BlockSpec(memory_space=pltpu.VMEM)
SMEM = pl.BlockSpec(memory_space=pltpu.SMEM)
HBM = pl.BlockSpec(memory_space=pltpu.HBM)


def shift(value, axis, steps):
    count = lax.axis_size(axis)
    return lax.ppermute(value, axis, [(s, s + steps) for s in range(max(0, count - steps))])


def rotate(value, axis, steps):
    count = lax.axis_size(axis)
    return lax.ppermute(value, axis, [(s, (s + steps) % count) for s in range(count)])


def row_rotate(value, steps):
    count = lax.axis_size("seq")
    pairs = [(s, s // ROW * ROW + (s + steps) % ROW) for s in range(count)]
    return lax.ppermute(value, "seq", pairs)


def exchange(value, axis, bit):
    return lax.ppermute(value, axis, [(s, s ^ bit) for s in range(lax.axis_size(axis))])


def dot(left, right, dims=NN):
    return lax.dot_general(left, right, (dims, ((), ())), preferred_element_type=F32)


def split(value):
    high = value.astype(BF16)
    return high, (value - high.astype(F32)).astype(BF16)


def dot_split(left, right, dims=NN):
    lh, ll = left
    rh, rl = right
    return dot(lh, rh, dims) + (dot(lh, rl, dims) + dot(ll, rh, dims))


def dot32(left, right, dims=NN):
    return dot_split(split(left), split(right), dims)


def call(kernel, outs, name, flops, *args, scratch=(), smem=1, hbm=0):
    size = sum(a.size * a.dtype.itemsize for a in args) + sum(
        o.size * o.dtype.itemsize for o in outs
    )
    return pl.pallas_call(
        kernel,
        out_shape=outs,
        in_specs=[SMEM] * smem + [HBM] * hbm + [VMEM] * (len(args) - smem - hbm),
        out_specs=[VMEM] * len(outs),
        scratch_shapes=list(scratch),
        name=name,
        interpret=INTERPRET,
        cost_estimate=pl.CostEstimate(flops=flops, bytes_accessed=size, transcendentals=0),
        compiler_params=pltpu.CompilerParams(vmem_limit_bytes=40 * 1024 * 1024),
    )(*args)


def in_hbm(value):
    return value if INTERPRET else pltpu.with_memory_space_constraint(value, pltpu.HBM)


def out(shape, dtype):
    return jax.ShapeDtypeStruct(shape, dtype)


def request_ends(meta):
    ends = [meta[0]]
    for r in range(1, REQS):
        ends.append(ends[-1] + meta[r])
    return ends


def seg_of(pos, ends):
    total = jnp.where(pos >= ends[0], 1, 0)
    for r in range(1, REQS):
        total = total + jnp.where(pos >= ends[r], 1, 0)
    return total


def start_of(pos, ends):
    begin = jnp.where(pos >= ends[0], ends[0], 0)
    for r in range(1, REQS):
        begin = jnp.maximum(begin, jnp.where(pos >= ends[r], ends[r], 0))
    return begin


def iota(shape, dim):
    return lax.broadcasted_iota(jnp.int32, shape, dim)


def conv_rows(ext, taps, pos, begin):
    pre = ext[HALO:] * taps[CONV - 1 : CONV]
    for back in range(1, CONV):
        moved = pltpu.roll(ext, back, 0)[HALO:]
        ok = jnp.where(pos - back >= begin, 1.0, 0.0).astype(F32)
        pre = pre + moved * taps[CONV - 1 - back : CONV - back] * ok
    return (pre / (1.0 + jnp.exp(-pre))).astype(BF16)


def edge_select(meta, ends, first, last, ext_pos):
    edge_id = iota((EDGE_ROWS, 1), 0)
    wanted = jnp.full((EDGE_ROWS, 1), -1, jnp.int32)
    for r in range(REQS):
        begin = ends[r] - meta[r]
        owned = (ends[r] - 1 >= first) & (ends[r] - 1 <= last)
        for i in range(CONV - 1):
            spot = ends[r] - (CONV - 1) + i
            good = owned & (spot >= begin)
            wanted = jnp.where(edge_id == i * REQS + r, jnp.where(good, spot, -1), wanted)
    return jnp.where((ext_pos == wanted) & (ext_pos >= 0), 1.0, 0.0).astype(BF16)


def conv_kernel(
    meta, x_hbm, taps_hbm, beta_hbm,
    act_ref, head_ref, edge_ref, taps_ref, beta_ref, x_ref, sems,
):
    copies = [
        pltpu.make_async_copy(x_hbm, x_ref, sems.at[0]),
        pltpu.make_async_copy(taps_hbm, taps_ref, sems.at[1]),
        pltpu.make_async_copy(beta_hbm, beta_ref, sems.at[2]),
    ]
    for copy in copies:
        copy.start()
    for copy in copies:
        copy.wait()
    rows = x_ref.shape[1]
    ends = request_ends(meta)
    first = meta[4]
    pos = first + iota((rows, 1), 0)
    begin = start_of(pos, ends)
    select = edge_select(
        meta, ends, first, first + rows - 1, first + iota((EDGE_ROWS, rows), 1)
    )
    for c in range(3):
        x = x_ref[c]
        edge_ref[c] = dot(select, x).astype(BF16)
        head_ref[c] = x[:HALO]
        wide = x.astype(F32)
        act_ref[c, HALO:] = conv_rows(wide, taps_ref[c], pos[HALO:], begin[HALO:])
        act_ref[c, :HALO] = jnp.zeros((HALO, x.shape[1]), BF16)


def prep_kernel(
    meta, act_ref, head_ref, part_ref, taps_ref, beta_ref, halo_ref,
    map_ref, uw_ref, local_ref, link_ref, kb_ref, ks_ref, edge_ref,
):
    rows = act_ref.shape[1]
    heads = act_ref.shape[2] // DK
    half = rows // 2
    ends = request_ends(meta)
    first = meta[4]
    pos = first + iota((rows, 1), 0)
    pos_r = first + iota((1, rows), 1)
    seg = seg_of(pos, ends)
    seg_r = seg_of(pos_r, ends)
    begin = start_of(pos, ends)
    coupled = jnp.where(begin < first, 1.0, 0.0).astype(F32)
    last = first + rows - 1
    last_seg = seg_of(last, ends)
    last_link = start_of(last, ends) < first
    in_last = jnp.where(seg == last_seg, 1.0, 0.0).astype(F32)
    select = edge_select(meta, ends, first, last, first - HALO + iota((EDGE_ROWS, HALO), 1))

    planes = []
    for c in range(3):
        halo = halo_ref[c]
        picked = part_ref[c] + dot(select, halo).astype(BF16)
        for b in range(heads):
            edge_ref[c * heads + b] = picked[:, b * DK : (b + 1) * DK]
        ext = jnp.concatenate([halo, head_ref[c]], axis=0).astype(F32)
        lead = conv_rows(ext, taps_ref[c], pos[:HALO], begin[:HALO])
        planes.append(jnp.concatenate([lead, act_ref[c, HALO:]], axis=0))

    row_id = iota((rows, rows), 0)
    col_id = iota((rows, rows), 1)
    same = seg == seg_r
    strict = same & (row_id > col_id)
    causal = same & (row_id >= col_id)
    diag = row_id == col_id
    row_h = iota((half, half), 0)
    col_h = iota((half, half), 1)
    eye_h = jnp.where(row_h == col_h, 1.0, 0.0).astype(F32)

    def as_row(column):
        return jnp.sum(jnp.where(diag, column, 0.0), axis=0, keepdims=True)

    def as_column(row):
        return jnp.sum(jnp.where(diag, row, 0.0), axis=1, keepdims=True)

    state = []
    for h in range(heads):
        lanes = slice(h * DK, (h + 1) * DK)
        qb, kb, vb = (planes[c][:, lanes] for c in range(3))
        q32, k32, v32 = (t.astype(F32) for t in (qb, kb, vb))
        qs = lax.rsqrt(jnp.sum(q32 * q32, axis=1, keepdims=True) + 1e-06)
        ks = lax.rsqrt(jnp.sum(k32 * k32, axis=1, keepdims=True) + 1e-06)
        ks_row = as_row(ks)
        beta = as_column(1.0 / (1.0 + jnp.exp(-beta_ref[h : h + 1, :])))
        system = jnp.where(strict, dot(kb, kb, NT) * (beta * ks) * ks_row, 0.0)
        scores = jnp.where(causal, dot(qb, kb, NT) * qs * ks_row, 0.0)
        targets = jnp.concatenate([beta * v32, (beta * coupled * ks) * k32], axis=1)
        state.append((q32 * qs, kb, ks, system, scores, targets))

    blocks = []
    for h in range(heads):
        system = state[h][3]
        for d in range(2):
            blocks.append(system[d * half : (d + 1) * half, d * half : (d + 1) * half])
    inverses = []
    low = ((row_h ^ col_h) == 1) & (row_h > col_h)
    for a in blocks:
        inverses.append(eye_h - jnp.where(low, a, 0.0))
    level = 1
    while (2 << level) <= half:
        low = (((row_h >> level) ^ (col_h >> level)) == 1) & (row_h > col_h)
        parts = [split(x) for x in inverses]
        inner = [dot_split(split(jnp.where(low, a, 0.0)), p) for a, p in zip(blocks, parts)]
        inverses = [x - dot_split(p, split(t)) for x, p, t in zip(inverses, parts, inner)]
        level += 1

    for h in range(heads):
        q32, kb, ks, system, scores, targets = state[h]
        top = dot32(inverses[2 * h], targets[:half])
        rest = targets[half:] - dot32(system[half:, :half], top)
        uw = jnp.concatenate([top, dot32(inverses[2 * h + 1], rest)], axis=0)
        uw_ref[h] = uw
        mixed = dot32(scores, uw)
        local_ref[h] = mixed[:, :DK]
        link_ref[h] = coupled * q32 - mixed[:, DK:]
        kb_ref[h] = kb
        ks_ref[h] = ks
        scaled = jnp.concatenate([uw[:, DK:] * ks, uw[:, :DK] * (ks * in_last)], axis=1)
        high, less = split(scaled)
        fold = dot(kb, high, TN) + dot(kb, less, TN)
        eye_k = jnp.where(iota((DK, DK), 0) == iota((DK, DK), 1), 1.0, 0.0).astype(F32)
        map_ref[h, :, :DK] = jnp.where(last_link, fold[:, :DK], eye_k).astype(BF16)
        map_ref[h, :, DK:] = fold[:, DK:].astype(BF16)


def joined(newer, older):
    return newer.astype(F32) + older.astype(F32) - dot(newer[:, :DK], older)


def twin_kernel(meta, own_ref, came_ref, twin_ref):
    odd = lax.rem(meta[7], 2) == 1
    for h in range(own_ref.shape[0]):
        own, came = own_ref[h], came_ref[h]
        newer = jnp.where(odd, own, came)
        older = jnp.where(odd, came, own)
        twin_ref[h] = joined(newer, older).astype(BF16)


def row_kernel(meta, own_ref, came_ref, twin_ref, other_ref, prefix_ref, total_ref):
    here = meta[7]
    late = here >= ROW // 2
    odd = lax.rem(here, 2) == 1
    for h in range(own_ref.shape[0]):
        twin, other = twin_ref[h], other_ref[h]
        older = jnp.where(late, other, twin)
        total_ref[h] = joined(jnp.where(late, twin, other), older).astype(BF16)
        step = jnp.where(odd, came_ref[h], jnp.zeros_like(twin))
        prefix_ref[h] = joined(step, jnp.where(late, other, jnp.zeros_like(twin)))


def join_kernel(total_ref, near_ref, both_ref, tail_ref):
    for h in range(total_ref.shape[0]):
        both = joined(total_ref[h], near_ref[h]).astype(BF16)
        both_ref[h] = both
        tail_ref[h] = both[:, DK:]


def quarter_of(here):
    return lax.rem((here + 1) // 2, 2) * 2 + here // 2


def attend_kernel(
    meta, prefix_ref, wide_ref, tail_ref, uw_ref, local_ref, link_ref, kb_ref, ks_ref,
    edge_ref, gain_ref, w_ref, own_ref, other_ref, keep_ref, give_ref, heads_ref, pay_ref,
):
    heads, rows, _ = local_ref.shape
    wins, cores, piece, _ = heads_ref.shape
    ends = request_ends(meta)
    first, win, core = meta[4], meta[5], meta[6]
    last = first + rows - 1
    seg = seg_of(first + iota((rows, 1), 0), ends)
    gain = gain_ref[...]
    for h in range(heads):
        wide, prefix, tail = wide_ref[h], prefix_ref[h], tail_ref[h]
        ahead = wide[:, DK:].astype(F32) + tail.astype(F32) - dot(wide[:, :DK], tail)
        enter = prefix[:, DK:] + ahead - dot32(prefix[:, :DK], ahead)
        parts = split(enter)
        attended = local_ref[h] + dot_split(split(link_ref[h]), parts)
        scale = lax.rsqrt(jnp.mean(attended * attended, axis=1, keepdims=True) + 1e-05)
        normed = attended * scale * gain
        lanes = slice(h * DK, (h + 1) * DK)
        for p in range(wins * cores):
            heads_ref[p // cores, p % cores, :, lanes] = normed[p * piece : (p + 1) * piece].astype(
                BF16
            )
        uw = uw_ref[h]
        corrected = (uw[:, :DK] - dot_split(split(uw[:, DK:]), parts)) * ks_ref[h]
        for r in range(REQS):
            owned = (ends[r] - 1 >= first) & (ends[r] - 1 <= last)
            carried = owned & (ends[r] - meta[r] < first)
            member = (seg == r) & owned
            high, less = split(jnp.where(member, corrected, 0.0))
            final = dot(kb_ref[h], high, TN) + dot(kb_ref[h], less, TN)
            final = final + jnp.where(carried, enter, 0.0)
            spot = (r * heads + h) * DK
            pay_ref[spot : spot + DK, :] = final.astype(BF16)
    base = REQS * heads * DK
    for b in range(edge_ref.shape[0]):
        pay_ref[base + b * EDGE_ROWS : base + (b + 1) * EDGE_ROWS, :] = edge_ref[b]
    used = base + edge_ref.shape[0] * EDGE_ROWS
    pay_ref[used:, :] = jnp.zeros((pay_ref.shape[0] - used, DK), BF16)
    quarter = keep_ref.shape[0] // 2
    mine = quarter_of(meta[7])
    twin = quarter_of(meta[7] + 1 - 2 * lax.rem(meta[7], 2))
    for ref, spot in ((keep_ref, mine), (give_ref, twin)):
        for part, which in enumerate((spot, spot + 1 - 2 * lax.rem(spot, 2))):
            start = pl.multiple_of(which * quarter, EDGE_ROWS)
            ref[part * quarter : (part + 1) * quarter] = pay_ref[pl.ds(start, quarter), :]
    order = [lax.rem(win + k, wins) for k in range(wins)]
    w = w_ref[...]
    mine = jnp.concatenate([heads_ref[o, core] for o in order], axis=0)
    own_ref[...] = dot(mine, w)
    theirs = jnp.concatenate([heads_ref[o, cores - 1 - core] for o in order], axis=0)
    other_ref[...] = dot(theirs, w).astype(BF16)


def pair_kernel(own_ref, got_ref, pay_ref, came_ref, keep_ref, *refs):
    *send_refs, quarter_ref, give_ref = refs
    piece = keep_ref.shape[0]
    keep_ref[...] = own_ref[:piece] + got_ref[:piece].astype(F32)
    for k, ref in enumerate(send_refs):
        part = slice((k + 1) * piece, (k + 2) * piece)
        ref[...] = (own_ref[part] + got_ref[part].astype(F32)).astype(BF16)
    quarter = quarter_ref.shape[0]
    quarter_ref[...] = pay_ref[:quarter] + came_ref[:quarter]
    give_ref[...] = pay_ref[quarter:] + came_ref[quarter:]


def norm_kernel(hidden_ref, gain_ref, pay_ref, came_ref, keep_ref, *refs):
    *got, stream_ref, normed_ref, sum_ref = refs
    total = keep_ref[...]
    for ref in got:
        total = total + ref[...].astype(F32)
    total = hidden_ref[...].astype(F32) + total
    stream_ref[...] = total.astype(BF16)
    scale = lax.rsqrt(jnp.mean(total * total, axis=1, keepdims=True) + 1e-05)
    normed_ref[...] = (total * scale * gain_ref[...]).astype(BF16)
    sum_ref[...] = pay_ref[...] + came_ref[...]


def columns_kernel(meta, mine_ref, peer_ref, *refs):
    full_ref, *piece_refs, cols_ref = refs
    wins, rows, width = cols_ref.shape
    mine, peer = mine_ref[...], peer_ref[...]
    lower = jnp.where(meta[6] == 0, mine, peer)
    upper = jnp.where(meta[6] == 0, peer, mine)
    full_ref[: rows // 2] = lower
    full_ref[rows // 2 :] = upper
    for k in range(wins):
        cols_ref[k, : rows // 2] = lower[:, k * width : (k + 1) * width]
        cols_ref[k, rows // 2 :] = upper[:, k * width : (k + 1) * width]
    for k, ref in enumerate(piece_refs):
        ref[...] = cols_ref[lax.rem(meta[5] + k, wins)]


def last_kernel(done_ref, own_ref, *refs):
    *came, all_ref = refs
    direct = done_ref.shape[1]
    all_ref[:, :direct] = done_ref[...]
    total = own_ref[...]
    for ref in came:
        total = total + ref[...].astype(F32)
    all_ref[:, direct:] = total.astype(BF16)


def finish_kernel(meta, *refs):
    *quarters, state_ref, edge_ref, pay_ref = refs
    for k, ref in enumerate(quarters):
        quarter = ref.shape[0]
        place = lax.rem(meta[7] + ROW - k, ROW)
        start = pl.multiple_of(quarter_of(place) * quarter, EDGE_ROWS)
        pay_ref[pl.ds(start, quarter), :] = ref[...]
    rows = state_ref.shape[0]
    state_ref[...] = pay_ref[:rows].astype(F32)
    heads = edge_ref.shape[3] // DK
    for b in range(3 * heads):
        edges = pay_ref[rows + b * EDGE_ROWS : rows + (b + 1) * EDGE_ROWS].astype(F32)
        lanes = slice(b % heads * DK, (b % heads + 1) * DK)
        for i in range(CONV - 1):
            edge_ref[i, b // heads, :, lanes] = edges[i * REQS : (i + 1) * REQS].astype(BF16)


def body(qkv_in, conv_w, beta_logits, lengths, out_gain, w_out, hidden_in, norm_gain, w_qkv):
    rows = qkv_in.shape[0]
    width = qkv_in.shape[2]
    heads = width // DK
    model = w_out.shape[1]
    n_seq, wins, cores = (lax.axis_size(a) for a in ("seq", "win", "wout"))
    piece = rows // (wins * cores)
    seq, win, core = (lax.axis_index(a).astype(jnp.int32) for a in ("seq", "win", "wout"))
    meta = jnp.concatenate([lengths, jnp.stack([seq * rows, win, core, seq % ROW])])
    direct = w_qkv.shape[1] // 3
    gathered = lax.all_gather(w_qkv[:, :direct], "win", axis=0, tiled=True)
    x = qkv_in.transpose(1, 0, 2)
    halo = shift(x[:, rows - HALO :], "seq", 1)
    act, lead, parts, taps, beta = call(
        conv_kernel,
        [
            out((3, rows, width), BF16),
            out((3, HALO, width), BF16),
            out((3, EDGE_ROWS, width), BF16),
            out((3, CONV, width), F32),
            out((heads, rows), F32),
        ],
        "conv",
        10**8,
        meta, *(in_hbm(a) for a in (x, conv_w, beta_logits)),
        scratch=[pltpu.VMEM((3, rows, width), BF16), pltpu.SemaphoreType.DMA((3,))],
        hbm=3,
    )
    maps, uw, local, link, kb, ks, edges = call(
        prep_kernel,
        [
            out((heads, DK, 2 * DK), BF16),
            out((heads, rows, 2 * DK), F32),
            out((heads, rows, DK), F32),
            out((heads, rows, DK), F32),
            out((heads, rows, DK), BF16),
            out((heads, rows, 1), F32),
            out((3 * heads, EDGE_ROWS, DK), BF16),
        ],
        "prep",
        2 * 10**9,
        meta, act, lead, parts, taps, beta, halo,
    )

    maps_out = out((heads, DK, 2 * DK), BF16)
    came = exchange(maps, "seq", 1)
    (twin,) = call(twin_kernel, [maps_out], "twin", 10**8, meta, maps, came)
    prefix, total = call(
        row_kernel,
        [out((heads, DK, 2 * DK), F32), maps_out],
        "row",
        10**8,
        meta, maps, came, twin, exchange(twin, "seq", ROW - 1),
    )
    both, tail = call(
        join_kernel,
        [maps_out, out((heads, DK, DK), BF16)],
        "join",
        10**8,
        total, shift(total, "seq", ROW),
        smem=0,
    )
    tail = shift(tail, "seq", 3 * ROW)
    wide = shift(both, "seq", ROW)
    state_rows = REQS * heads * DK
    grain = ROW * EDGE_ROWS
    pay_rows = -(-(state_rows + 3 * heads * EDGE_ROWS) // grain) * grain
    half, quarter = out((pay_rows // 2, DK), BF16), out((pay_rows // 4, DK), BF16)
    own, other, keep, give = call(
        attend_kernel,
        [
            out((wins * piece, model), F32),
            out((wins * piece, model), BF16),
            half,
            half,
        ],
        "attend",
        10**9,
        meta, prefix, wide, tail, uw, local, link, kb, ks, edges, out_gain.reshape(1, DK), w_out,
        scratch=[
            pltpu.VMEM((wins, cores, piece, width), BF16),
            pltpu.VMEM((pay_rows, DK), BF16),
        ],
    )
    got = rotate(other, "wout", 1)
    *sums, payload, give = call(
        pair_kernel,
        [out((piece, model), F32)] + [out((piece, model), BF16)] * (wins - 1) + [quarter] * 2,
        "pair",
        10**6,
        own, got, keep, exchange(give, "seq", 1),
        smem=0,
    )
    came = exchange(give, "seq", ROW - 1)
    reduced = [rotate(sums[k], "win", k) for k in range(1, wins)]
    stream_out, normed, payload = call(
        norm_kernel,
        [out((piece, model), BF16), out((piece, model), BF16), quarter],
        "norm",
        10**6,
        hidden_in, norm_gain.reshape(1, model), payload, came, sums[0], *reduced,
        smem=0,
    )
    peer = rotate(normed, "wout", 1)
    lines = n_seq // ROW
    bits = [b for b in (4, 2, 1) if 2 * b <= lines]
    came = exchange(payload, "seq", bits[0] * ROW)
    full, *cols = call(
        columns_kernel,
        [out((2 * piece, model), BF16)] + [out((2 * piece, model // wins), BF16)] * wins,
        "columns",
        10**6,
        meta, normed, peer,
        scratch=[pltpu.VMEM((wins, 2 * piece, model // wins), BF16)],
    )
    blocks = [cols[0]] + [rotate(cols[k], "win", k) for k in range(1, wins)]
    finished = jnp.dot(full, gathered, preferred_element_type=F32).astype(BF16)
    finished, came = lax.optimization_barrier((finished, came))
    *blocks, payload = lax.optimization_barrier((*blocks, payload + came))

    def partial(k):
        return jnp.dot(blocks[(wins - k) % wins], w_qkv[:, direct:], preferred_element_type=F32)

    parts = [partial(k).astype(BF16) for k in range(1, wins)]
    *parts, payload = lax.optimization_barrier((*parts, payload))
    arrived = [rotate(part, "win", k + 1) for k, part in enumerate(parts)]
    (projected,) = call(
        last_kernel,
        [out((2 * piece, w_qkv.shape[1]), BF16)],
        "last",
        10**10,
        finished, partial(0), *arrived,
        smem=0,
    )

    if lines == 8:
        turns = [rotate(payload, "seq", steps * ROW) for steps in (1, 7, 2)]
        payload = payload + (turns[0] + turns[1]) + turns[2]
    else:
        for bit in bits[1:]:
            payload = payload + exchange(payload, "seq", bit * ROW)
    quarters = [payload] + [row_rotate(payload, k) for k in range(1, ROW)]
    projected, *quarters = lax.optimization_barrier((projected, *quarters))
    final_states, conv_edges = call(
        finish_kernel,
        [out((state_rows, DK), F32), out((CONV - 1, 3, REQS, width), BF16)],
        "finish",
        10**6,
        meta, *quarters,
        scratch=[pltpu.VMEM((pay_rows, DK), BF16)],
    )
    final_states = final_states.reshape(REQS, heads, DK, DK)
    conv_edges = conv_edges.transpose(2, 0, 1, 3)
    return (projected, stream_out, final_states, conv_edges)


def solution(mesh):
    return jax.shard_map(
        body,
        mesh=mesh,
        in_specs=(
            P("seq", None, ("win", "wout")),
            P(None, None, ("win", "wout")),
            P(("win", "wout"), "seq"),
            P(),
            P(),
            P(("win", "wout"), None),
            P(("seq", "win", "wout"), None),
            P(),
            P("win", "wout"),
        ),
        out_specs=(
            P(("seq", "win"), "wout"),
            P(("seq", "win", "wout"), None),
            P(None, ("win", "wout"), None, None),
            P(None, None, None, ("win", "wout")),
        ),
        check_vma=False,
    )
```

```python
import functools

import jax
import jax.numpy as jnp
from jax import lax
from jax.experimental import pallas as pl
from jax.experimental.pallas import tpu as pltpu
from jax.sharding import PartitionSpec as P

DK = 128
CONV = 4
REQS = 4
HALO = 16
ROW = 4
EDGE_ROWS = 16
INTERPRET = False
F32 = jnp.float32
BF16 = jnp.bfloat16
NN = ((1,), (0,))
NT = ((1,), (1,))
TN = ((0,), (0,))
VMEM = pl.BlockSpec(memory_space=pltpu.VMEM)
SMEM = pl.BlockSpec(memory_space=pltpu.SMEM)
HBM = pl.BlockSpec(memory_space=pltpu.HBM)


def shift(value, axis, steps):
    count = lax.axis_size(axis)
    return lax.ppermute(value, axis, [(s, s + steps) for s in range(max(0, count - steps))])


def rotate(value, axis, steps):
    count = lax.axis_size(axis)
    return lax.ppermute(value, axis, [(s, (s + steps) % count) for s in range(count)])


def row_rotate(value, steps):
    count = lax.axis_size("seq")
    pairs = [(s, s // ROW * ROW + (s + steps) % ROW) for s in range(count)]
    return lax.ppermute(value, "seq", pairs)


def exchange(value, axis, bit):
    return lax.ppermute(value, axis, [(s, s ^ bit) for s in range(lax.axis_size(axis))])


def dot(left, right, dims=NN):
    return lax.dot_general(left, right, (dims, ((), ())), preferred_element_type=F32)


def split(value):
    high = value.astype(BF16)
    return high, (value - high.astype(F32)).astype(BF16)


def dot_split(left, right, dims=NN):
    lh, ll = left
    rh, rl = right
    return dot(lh, rh, dims) + (dot(lh, rl, dims) + dot(ll, rh, dims))


def dot32(left, right, dims=NN):
    return dot_split(split(left), split(right), dims)


def call(kernel, outs, name, flops, *args, scratch=(), smem=1, hbm=0):
    size = sum(a.size * a.dtype.itemsize for a in args) + sum(
        o.size * o.dtype.itemsize for o in outs
    )
    return pl.pallas_call(
        kernel,
        out_shape=outs,
        in_specs=[SMEM] * smem + [HBM] * hbm + [VMEM] * (len(args) - smem - hbm),
        out_specs=[VMEM] * len(outs),
        scratch_shapes=list(scratch),
        name=name,
        interpret=INTERPRET,
        cost_estimate=pl.CostEstimate(flops=flops, bytes_accessed=size, transcendentals=0),
        compiler_params=pltpu.CompilerParams(vmem_limit_bytes=40 * 1024 * 1024),
    )(*args)


def in_hbm(value):
    return value if INTERPRET else pltpu.with_memory_space_constraint(value, pltpu.HBM)


def out(shape, dtype):
    return jax.ShapeDtypeStruct(shape, dtype)


def request_ends(meta):
    ends = [meta[0]]
    for r in range(1, REQS):
        ends.append(ends[-1] + meta[r])
    return ends


def seg_of(pos, ends):
    total = jnp.where(pos >= ends[0], 1, 0)
    for r in range(1, REQS):
        total = total + jnp.where(pos >= ends[r], 1, 0)
    return total


def start_of(pos, ends):
    begin = jnp.where(pos >= ends[0], ends[0], 0)
    for r in range(1, REQS):
        begin = jnp.maximum(begin, jnp.where(pos >= ends[r], ends[r], 0))
    return begin


def iota(shape, dim):
    return lax.broadcasted_iota(jnp.int32, shape, dim)


def conv_rows(ext, taps, pos, begin):
    pre = ext[HALO:] * taps[CONV - 1 : CONV]
    for back in range(1, CONV):
        moved = pltpu.roll(ext, back, 0)[HALO:]
        ok = jnp.where(pos - back >= begin, 1.0, 0.0).astype(F32)
        pre = pre + moved * taps[CONV - 1 - back : CONV - back] * ok
    return (pre / (1.0 + jnp.exp(-pre))).astype(BF16)


def edge_select(meta, ends, first, last, ext_pos):
    edge_id = iota((EDGE_ROWS, 1), 0)
    wanted = jnp.full((EDGE_ROWS, 1), -1, jnp.int32)
    for r in range(REQS):
        begin = ends[r] - meta[r]
        owned = (ends[r] - 1 >= first) & (ends[r] - 1 <= last)
        for i in range(CONV - 1):
            spot = ends[r] - (CONV - 1) + i
            good = owned & (spot >= begin)
            wanted = jnp.where(edge_id == i * REQS + r, jnp.where(good, spot, -1), wanted)
    return jnp.where((ext_pos == wanted) & (ext_pos >= 0), 1.0, 0.0).astype(BF16)


def conv_kernel(
    meta, x_hbm, taps_hbm, beta_hbm,
    act_ref, head_ref, edge_ref, taps_ref, beta_ref, x_ref, sems,
):
    copies = [
        pltpu.make_async_copy(x_hbm, x_ref, sems.at[0]),
        pltpu.make_async_copy(taps_hbm, taps_ref, sems.at[1]),
        pltpu.make_async_copy(beta_hbm, beta_ref, sems.at[2]),
    ]
    for copy in copies:
        copy.start()
    for copy in copies:
        copy.wait()
    rows = x_ref.shape[1]
    ends = request_ends(meta)
    first = meta[4]
    pos = first + iota((rows, 1), 0)
    begin = start_of(pos, ends)
    select = edge_select(
        meta, ends, first, first + rows - 1, first + iota((EDGE_ROWS, rows), 1)
    )
    for c in range(3):
        x = x_ref[c]
        edge_ref[c] = dot(select, x).astype(BF16)
        head_ref[c] = x[:HALO]
        wide = x.astype(F32)
        act_ref[c, HALO:] = conv_rows(wide, taps_ref[c], pos[HALO:], begin[HALO:])
        act_ref[c, :HALO] = jnp.zeros((HALO, x.shape[1]), BF16)


def prep_kernel(
    meta, act_ref, head_ref, part_ref, taps_ref, beta_ref, halo_ref,
    map_ref, uw_ref, local_ref, link_ref, kb_ref, ks_ref, edge_ref,
):
    rows = act_ref.shape[1]
    heads = act_ref.shape[2] // DK
    half = rows // 2
    ends = request_ends(meta)
    first = meta[4]
    pos = first + iota((rows, 1), 0)
    pos_r = first + iota((1, rows), 1)
    seg = seg_of(pos, ends)
    seg_r = seg_of(pos_r, ends)
    begin = start_of(pos, ends)
    coupled = jnp.where(begin < first, 1.0, 0.0).astype(F32)
    last = first + rows - 1
    last_seg = seg_of(last, ends)
    last_link = start_of(last, ends) < first
    in_last = jnp.where(seg == last_seg, 1.0, 0.0).astype(F32)
    select = edge_select(meta, ends, first, last, first - HALO + iota((EDGE_ROWS, HALO), 1))

    planes = []
    for c in range(3):
        halo = halo_ref[c]
        picked = part_ref[c] + dot(select, halo).astype(BF16)
        for b in range(heads):
            edge_ref[c * heads + b] = picked[:, b * DK : (b + 1) * DK]
        ext = jnp.concatenate([halo, head_ref[c]], axis=0).astype(F32)
        lead = conv_rows(ext, taps_ref[c], pos[:HALO], begin[:HALO])
        planes.append(jnp.concatenate([lead, act_ref[c, HALO:]], axis=0))

    row_id = iota((rows, rows), 0)
    col_id = iota((rows, rows), 1)
    same = seg == seg_r
    strict = same & (row_id > col_id)
    causal = same & (row_id >= col_id)
    diag = row_id == col_id
    row_h = iota((half, half), 0)
    col_h = iota((half, half), 1)
    eye_h = jnp.where(row_h == col_h, 1.0, 0.0).astype(F32)

    def as_row(column):
        return jnp.sum(jnp.where(diag, column, 0.0), axis=0, keepdims=True)

    def as_column(row):
        return jnp.sum(jnp.where(diag, row, 0.0), axis=1, keepdims=True)

    state = []
    for h in range(heads):
        lanes = slice(h * DK, (h + 1) * DK)
        qb, kb, vb = (planes[c][:, lanes] for c in range(3))
        q32, k32, v32 = (t.astype(F32) for t in (qb, kb, vb))
        qs = lax.rsqrt(jnp.sum(q32 * q32, axis=1, keepdims=True) + 1e-06)
        ks = lax.rsqrt(jnp.sum(k32 * k32, axis=1, keepdims=True) + 1e-06)
        ks_row = as_row(ks)
        beta = as_column(1.0 / (1.0 + jnp.exp(-beta_ref[h : h + 1, :])))
        system = jnp.where(strict, dot(kb, kb, NT) * (beta * ks) * ks_row, 0.0)
        scores = jnp.where(causal, dot(qb, kb, NT) * qs * ks_row, 0.0)
        targets = jnp.concatenate([beta * v32, (beta * coupled * ks) * k32], axis=1)
        state.append((q32 * qs, kb, ks, system, scores, targets))

    blocks = []
    for h in range(heads):
        system = state[h][3]
        for d in range(2):
            blocks.append(system[d * half : (d + 1) * half, d * half : (d + 1) * half])
    inverses = []
    low = ((row_h ^ col_h) == 1) & (row_h > col_h)
    for a in blocks:
        inverses.append(eye_h - jnp.where(low, a, 0.0))
    level = 1
    while (2 << level) <= half:
        low = (((row_h >> level) ^ (col_h >> level)) == 1) & (row_h > col_h)
        parts = [split(x) for x in inverses]
        inner = [dot_split(split(jnp.where(low, a, 0.0)), p) for a, p in zip(blocks, parts)]
        inverses = [x - dot_split(p, split(t)) for x, p, t in zip(inverses, parts, inner)]
        level += 1

    for h in range(heads):
        q32, kb, ks, system, scores, targets = state[h]
        top = dot32(inverses[2 * h], targets[:half])
        rest = targets[half:] - dot32(system[half:, :half], top)
        uw = jnp.concatenate([top, dot32(inverses[2 * h + 1], rest)], axis=0)
        uw_ref[h] = uw
        mixed = dot32(scores, uw)
        local_ref[h] = mixed[:, :DK]
        link_ref[h] = coupled * q32 - mixed[:, DK:]
        kb_ref[h] = kb
        ks_ref[h] = ks
        scaled = jnp.concatenate([uw[:, DK:] * ks, uw[:, :DK] * (ks * in_last)], axis=1)
        high, less = split(scaled)
        fold = dot(kb, high, TN) + dot(kb, less, TN)
        eye_k = jnp.where(iota((DK, DK), 0) == iota((DK, DK), 1), 1.0, 0.0).astype(F32)
        map_ref[h, :, :DK] = jnp.where(last_link, fold[:, :DK], eye_k).astype(BF16)
        map_ref[h, :, DK:] = fold[:, DK:].astype(BF16)


def joined(newer, older):
    return newer.astype(F32) + older.astype(F32) - dot(newer[:, :DK], older)


def twin_kernel(meta, own_ref, came_ref, twin_ref):
    odd = lax.rem(meta[7], 2) == 1
    for h in range(own_ref.shape[0]):
        own, came = own_ref[h], came_ref[h]
        newer = jnp.where(odd, own, came)
        older = jnp.where(odd, came, own)
        twin_ref[h] = joined(newer, older).astype(BF16)


def row_kernel(
    meta, own_ref, came_ref, twin_ref, other_ref, below_ref, cross_ref,
    prefix_ref, both_ref, tail_ref,
):
    here = meta[7]
    late = here >= ROW // 2
    odd = lax.rem(here, 2) == 1
    for h in range(own_ref.shape[0]):
        totals = []
        for same_ref, far_ref in ((twin_ref, other_ref), (below_ref, cross_ref)):
            same, far = same_ref[h], far_ref[h]
            newer = jnp.where(late, same, far)
            totals.append(joined(newer, jnp.where(late, far, same)).astype(BF16))
        both = joined(*totals).astype(BF16)
        both_ref[h] = both
        tail_ref[h] = both[:, DK:]
        other = other_ref[h]
        step = jnp.where(odd, came_ref[h], jnp.zeros_like(other))
        prefix_ref[h] = joined(step, jnp.where(late, other, jnp.zeros_like(other)))


def quarter_of(here):
    return lax.rem((here + 1) // 2, 2) * 2 + here // 2


def attend_kernel(
    meta, prefix_ref, wide_ref, tail_ref, uw_ref, local_ref, link_ref, kb_ref, ks_ref,
    edge_ref, gain_ref, w_ref, own_ref, other_ref, keep_ref, give_ref, heads_ref, pay_ref,
):
    heads, rows, _ = local_ref.shape
    wins, cores, piece, _ = heads_ref.shape
    ends = request_ends(meta)
    first, win, core = meta[4], meta[5], meta[6]
    last = first + rows - 1
    seg = seg_of(first + iota((rows, 1), 0), ends)
    gain = gain_ref[...]
    for h in range(heads):
        wide, prefix, tail = wide_ref[h], prefix_ref[h], tail_ref[h]
        ahead = wide[:, DK:].astype(F32) + tail.astype(F32) - dot(wide[:, :DK], tail)
        enter = prefix[:, DK:] + ahead - dot32(prefix[:, :DK], ahead)
        parts = split(enter)
        attended = local_ref[h] + dot_split(split(link_ref[h]), parts)
        scale = lax.rsqrt(jnp.mean(attended * attended, axis=1, keepdims=True) + 1e-05)
        normed = attended * scale * gain
        lanes = slice(h * DK, (h + 1) * DK)
        for p in range(wins * cores):
            heads_ref[p // cores, p % cores, :, lanes] = normed[p * piece : (p + 1) * piece].astype(
                BF16
            )
        uw = uw_ref[h]
        corrected = (uw[:, :DK] - dot_split(split(uw[:, DK:]), parts)) * ks_ref[h]
        for r in range(REQS):
            owned = (ends[r] - 1 >= first) & (ends[r] - 1 <= last)
            carried = owned & (ends[r] - meta[r] < first)
            member = (seg == r) & owned
            high, less = split(jnp.where(member, corrected, 0.0))
            final = dot(kb_ref[h], high, TN) + dot(kb_ref[h], less, TN)
            final = final + jnp.where(carried, enter, 0.0)
            spot = (r * heads + h) * DK
            pay_ref[spot : spot + DK, :] = final.astype(BF16)
    base = REQS * heads * DK
    for b in range(edge_ref.shape[0]):
        pay_ref[base + b * EDGE_ROWS : base + (b + 1) * EDGE_ROWS, :] = edge_ref[b]
    used = base + edge_ref.shape[0] * EDGE_ROWS
    pay_ref[used:, :] = jnp.zeros((pay_ref.shape[0] - used, DK), BF16)
    quarter = keep_ref.shape[0] // 2
    mine = quarter_of(meta[7])
    twin = quarter_of(meta[7] + 1 - 2 * lax.rem(meta[7], 2))
    for ref, spot in ((keep_ref, mine), (give_ref, twin)):
        for part, which in enumerate((spot, spot + 1 - 2 * lax.rem(spot, 2))):
            start = pl.multiple_of(which * quarter, EDGE_ROWS)
            ref[part * quarter : (part + 1) * quarter] = pay_ref[pl.ds(start, quarter), :]
    order = [lax.rem(win + k, wins) for k in range(wins)]
    w = w_ref[...]
    mine = jnp.concatenate([heads_ref[o, core] for o in order], axis=0)
    own_ref[...] = dot(mine, w)
    theirs = jnp.concatenate([heads_ref[o, cores - 1 - core] for o in order], axis=0)
    other_ref[...] = dot(theirs, w).astype(BF16)


def pair_kernel(own_ref, got_ref, keep_ref, *send_refs):
    piece = keep_ref.shape[0]
    keep_ref[...] = own_ref[:piece] + got_ref[:piece].astype(F32)
    for k, ref in enumerate(send_refs):
        part = slice((k + 1) * piece, (k + 2) * piece)
        ref[...] = (own_ref[part] + got_ref[part].astype(F32)).astype(BF16)


def halve_kernel(pay_ref, came_ref, quarter_ref, give_ref):
    quarter = quarter_ref.shape[0]
    quarter_ref[...] = pay_ref[:quarter] + came_ref[:quarter]
    give_ref[...] = pay_ref[quarter:] + came_ref[quarter:]


def norm_kernel(hidden_ref, gain_ref, keep_ref, *refs):
    *got, stream_ref, normed_ref = refs
    total = keep_ref[...]
    for ref in got:
        total = total + ref[...].astype(F32)
    total = hidden_ref[...].astype(F32) + total
    stream_ref[...] = total.astype(BF16)
    scale = lax.rsqrt(jnp.mean(total * total, axis=1, keepdims=True) + 1e-05)
    normed_ref[...] = (total * scale * gain_ref[...]).astype(BF16)


def columns_kernel(meta, mine_ref, peer_ref, pay_ref, came_ref, sum_ref, *refs):
    *piece_refs, cols_ref = refs
    wins, rows, width = cols_ref.shape
    mine, peer = mine_ref[...], peer_ref[...]
    lower = jnp.where(meta[6] == 0, mine, peer)
    upper = jnp.where(meta[6] == 0, peer, mine)
    for k in range(wins):
        cols_ref[k, : rows // 2] = lower[:, k * width : (k + 1) * width]
        cols_ref[k, rows // 2 :] = upper[:, k * width : (k + 1) * width]
    for k, ref in enumerate(piece_refs):
        ref[...] = cols_ref[lax.rem(meta[5] + k, wins)]
    sum_ref[...] = pay_ref[...] + came_ref[...]


def last_kernel(own_ref, *refs):
    *came, all_ref = refs
    total = own_ref[...]
    for ref in came:
        total = total + ref[...].astype(F32)
    all_ref[...] = total.astype(BF16)


def finish_kernel(meta, *refs):
    *quarters, state_ref, edge_ref, pay_ref = refs
    for k, ref in enumerate(quarters):
        quarter = ref.shape[0]
        place = lax.rem(meta[7] + ROW - k, ROW)
        start = pl.multiple_of(quarter_of(place) * quarter, EDGE_ROWS)
        pay_ref[pl.ds(start, quarter), :] = ref[...]
    rows = state_ref.shape[0]
    state_ref[...] = pay_ref[:rows].astype(F32)
    heads = edge_ref.shape[3] // DK
    for b in range(3 * heads):
        edges = pay_ref[rows + b * EDGE_ROWS : rows + (b + 1) * EDGE_ROWS].astype(F32)
        lanes = slice(b % heads * DK, (b % heads + 1) * DK)
        for i in range(CONV - 1):
            edge_ref[i, b // heads, :, lanes] = edges[i * REQS : (i + 1) * REQS].astype(BF16)


def body(qkv_in, conv_w, beta_logits, lengths, out_gain, w_out, hidden_in, norm_gain, w_qkv):
    rows = qkv_in.shape[0]
    width = qkv_in.shape[2]
    heads = width // DK
    model = w_out.shape[1]
    n_seq, wins, cores = (lax.axis_size(a) for a in ("seq", "win", "wout"))
    piece = rows // (wins * cores)
    seq, win, core = (lax.axis_index(a).astype(jnp.int32) for a in ("seq", "win", "wout"))
    meta = jnp.concatenate([lengths, jnp.stack([seq * rows, win, core, seq % ROW])])
    x = qkv_in.transpose(1, 0, 2)
    halo = shift(x[:, rows - HALO :], "seq", 1)
    act, lead, parts, taps, beta = call(
        conv_kernel,
        [
            out((3, rows, width), BF16),
            out((3, HALO, width), BF16),
            out((3, EDGE_ROWS, width), BF16),
            out((3, CONV, width), F32),
            out((heads, rows), F32),
        ],
        "conv",
        10**8,
        meta, *(in_hbm(a) for a in (x, conv_w, beta_logits)),
        scratch=[pltpu.VMEM((3, rows, width), BF16), pltpu.SemaphoreType.DMA((3,))],
        hbm=3,
    )
    maps, uw, local, link, kb, ks, edges = call(
        prep_kernel,
        [
            out((heads, DK, 2 * DK), BF16),
            out((heads, rows, 2 * DK), F32),
            out((heads, rows, DK), F32),
            out((heads, rows, DK), F32),
            out((heads, rows, DK), BF16),
            out((heads, rows, 1), F32),
            out((3 * heads, EDGE_ROWS, DK), BF16),
        ],
        "prep",
        2 * 10**9,
        meta, act, lead, parts, taps, beta, halo,
    )

    maps_out = out((heads, DK, 2 * DK), BF16)
    came = exchange(maps, "seq", 1)
    (twin,) = call(twin_kernel, [maps_out], "twin", 10**8, meta, maps, came)
    cross = lax.ppermute(
        twin, "seq", [(s, (s ^ (ROW - 1)) + ROW) for s in range(n_seq - ROW)]
    )
    prefix, both, tail = call(
        row_kernel,
        [out((heads, DK, 2 * DK), F32), maps_out, out((heads, DK, DK), BF16)],
        "row",
        10**8,
        meta, maps, came, twin, exchange(twin, "seq", ROW - 1), shift(twin, "seq", ROW), cross,
    )
    tail = shift(tail, "seq", 3 * ROW)
    wide = shift(both, "seq", ROW)
    state_rows = REQS * heads * DK
    grain = ROW * EDGE_ROWS
    pay_rows = -(-(state_rows + 3 * heads * EDGE_ROWS) // grain) * grain
    half, quarter = out((pay_rows // 2, DK), BF16), out((pay_rows // 4, DK), BF16)
    own, other, keep, give = call(
        attend_kernel,
        [
            out((wins * piece, model), F32),
            out((wins * piece, model), BF16),
            half,
            half,
        ],
        "attend",
        10**9,
        meta, prefix, wide, tail, uw, local, link, kb, ks, edges, out_gain.reshape(1, DK), w_out,
        scratch=[
            pltpu.VMEM((wins, cores, piece, width), BF16),
            pltpu.VMEM((pay_rows, DK), BF16),
        ],
    )
    got = rotate(other, "wout", 1)
    sums = call(
        pair_kernel,
        [out((piece, model), F32)] + [out((piece, model), BF16)] * (wins - 1),
        "pair",
        10**6,
        own, got,
        smem=0,
    )
    came = exchange(give, "seq", 1)
    reduced = [rotate(sums[k], "win", k) for k in range(1, wins)]
    payload, give = call(
        halve_kernel,
        [quarter] * 2,
        "halve",
        10**6,
        keep, came,
        smem=0,
    )
    stream_out, normed = call(
        norm_kernel,
        [out((piece, model), BF16)] * 2,
        "norm",
        10**6,
        hidden_in, norm_gain.reshape(1, model), sums[0], *reduced,
        smem=0,
    )
    peer = rotate(normed, "wout", 1)
    payload, *cols = call(
        columns_kernel,
        [quarter] + [out((2 * piece, model // wins), BF16)] * wins,
        "columns",
        10**6,
        meta, normed, peer, payload, exchange(give, "seq", ROW - 1),
        scratch=[pltpu.VMEM((wins, 2 * piece, model // wins), BF16)],
    )
    lines = n_seq // ROW
    bits = [b for b in (4, 2, 1) if 2 * b <= lines]
    came = exchange(payload, "seq", bits[0] * ROW)
    blocks = [cols[0]] + [rotate(cols[k], "win", k) for k in range(1, wins)]
    *blocks, payload = lax.optimization_barrier((*blocks, payload + came))

    def partial(k):
        return jnp.dot(blocks[(wins - k) % wins], w_qkv, preferred_element_type=F32)

    parts = [partial(k).astype(BF16) for k in range(1, wins)]
    *parts, payload = lax.optimization_barrier((*parts, payload))
    arrived = [rotate(part, "win", k + 1) for k, part in enumerate(parts)]
    (projected,) = call(
        last_kernel,
        [out((2 * piece, w_qkv.shape[1]), BF16)],
        "last",
        10**10,
        partial(0), *arrived,
        smem=0,
    )

    if lines == 8:
        turns = [rotate(payload, "seq", steps * ROW) for steps in (1, 7, 2)]
        payload = payload + (turns[0] + turns[1]) + turns[2]
    else:
        for bit in bits[1:]:
            payload = payload + exchange(payload, "seq", bit * ROW)
    quarters = [payload] + [row_rotate(payload, k) for k in range(1, ROW)]
    projected, *quarters = lax.optimization_barrier((projected, *quarters))
    final_states, conv_edges = call(
        finish_kernel,
        [out((state_rows, DK), F32), out((CONV - 1, 3, REQS, width), BF16)],
        "finish",
        10**6,
        meta, *quarters,
        scratch=[pltpu.VMEM((pay_rows, DK), BF16)],
    )
    final_states = final_states.reshape(REQS, heads, DK, DK)
    conv_edges = conv_edges.transpose(2, 0, 1, 3)
    return (projected, stream_out, final_states, conv_edges)


def solution(mesh):
    return jax.shard_map(
        body,
        mesh=mesh,
        in_specs=(
            P("seq", None, ("win", "wout")),
            P(None, None, ("win", "wout")),
            P(("win", "wout"), "seq"),
            P(),
            P(),
            P(("win", "wout"), None),
            P(("seq", "win", "wout"), None),
            P(),
            P("win", "wout"),
        ),
        out_specs=(
            P(("seq", "win"), "wout"),
            P(("seq", "win", "wout"), None),
            P(None, ("win", "wout"), None, None),
            P(None, None, None, ("win", "wout")),
        ),
        check_vma=False,
    )
```

```python
import functools

import jax
import jax.numpy as jnp
from jax import lax
from jax.experimental import pallas as pl
from jax.experimental.pallas import tpu as pltpu
from jax.sharding import PartitionSpec as P

DK = 128
CONV = 4
REQS = 4
HALO = 16
ROW = 4
EDGE_ROWS = 16
INTERPRET = False
F32 = jnp.float32
BF16 = jnp.bfloat16
NN = ((1,), (0,))
NT = ((1,), (1,))
TN = ((0,), (0,))
VMEM = pl.BlockSpec(memory_space=pltpu.VMEM)
SMEM = pl.BlockSpec(memory_space=pltpu.SMEM)
HBM = pl.BlockSpec(memory_space=pltpu.HBM)


def shift(value, axis, steps):
    count = lax.axis_size(axis)
    return lax.ppermute(value, axis, [(s, s + steps) for s in range(max(0, count - steps))])


def rotate(value, axis, steps):
    count = lax.axis_size(axis)
    return lax.ppermute(value, axis, [(s, (s + steps) % count) for s in range(count)])


def row_rotate(value, steps):
    count = lax.axis_size("seq")
    pairs = [(s, s // ROW * ROW + (s + steps) % ROW) for s in range(count)]
    return lax.ppermute(value, "seq", pairs)


def exchange(value, axis, bit):
    return lax.ppermute(value, axis, [(s, s ^ bit) for s in range(lax.axis_size(axis))])


def dot(left, right, dims=NN):
    return lax.dot_general(left, right, (dims, ((), ())), preferred_element_type=F32)


def split(value):
    high = value.astype(BF16)
    return high, (value - high.astype(F32)).astype(BF16)


def dot_split(left, right, dims=NN):
    lh, ll = left
    rh, rl = right
    return dot(lh, rh, dims) + (dot(lh, rl, dims) + dot(ll, rh, dims))


def dot32(left, right, dims=NN):
    return dot_split(split(left), split(right), dims)


def call(kernel, outs, name, flops, *args, scratch=(), smem=1, hbm=0):
    size = sum(a.size * a.dtype.itemsize for a in args) + sum(
        o.size * o.dtype.itemsize for o in outs
    )
    return pl.pallas_call(
        kernel,
        out_shape=outs,
        in_specs=[SMEM] * smem + [HBM] * hbm + [VMEM] * (len(args) - smem - hbm),
        out_specs=[VMEM] * len(outs),
        scratch_shapes=list(scratch),
        name=name,
        interpret=INTERPRET,
        cost_estimate=pl.CostEstimate(flops=flops, bytes_accessed=size, transcendentals=0),
        compiler_params=pltpu.CompilerParams(vmem_limit_bytes=40 * 1024 * 1024),
    )(*args)


def in_hbm(value):
    return value if INTERPRET else pltpu.with_memory_space_constraint(value, pltpu.HBM)


def out(shape, dtype):
    return jax.ShapeDtypeStruct(shape, dtype)


def request_ends(meta):
    ends = [meta[0]]
    for r in range(1, REQS):
        ends.append(ends[-1] + meta[r])
    return ends


def seg_of(pos, ends):
    total = jnp.where(pos >= ends[0], 1, 0)
    for r in range(1, REQS):
        total = total + jnp.where(pos >= ends[r], 1, 0)
    return total


def start_of(pos, ends):
    begin = jnp.where(pos >= ends[0], ends[0], 0)
    for r in range(1, REQS):
        begin = jnp.maximum(begin, jnp.where(pos >= ends[r], ends[r], 0))
    return begin


def iota(shape, dim):
    return lax.broadcasted_iota(jnp.int32, shape, dim)


def conv_rows(ext, taps, pos, begin):
    pre = ext[HALO:] * taps[CONV - 1 : CONV]
    for back in range(1, CONV):
        moved = pltpu.roll(ext, back, 0)[HALO:]
        ok = jnp.where(pos - back >= begin, 1.0, 0.0).astype(F32)
        pre = pre + moved * taps[CONV - 1 - back : CONV - back] * ok
    return (pre / (1.0 + jnp.exp(-pre))).astype(BF16)


def edge_select(meta, ends, first, last, ext_pos):
    edge_id = iota((EDGE_ROWS, 1), 0)
    wanted = jnp.full((EDGE_ROWS, 1), -1, jnp.int32)
    for r in range(REQS):
        begin = ends[r] - meta[r]
        owned = (ends[r] - 1 >= first) & (ends[r] - 1 <= last)
        for i in range(CONV - 1):
            spot = ends[r] - (CONV - 1) + i
            good = owned & (spot >= begin)
            wanted = jnp.where(edge_id == r * CONV + i, jnp.where(good, spot, -1), wanted)
    return jnp.where((ext_pos == wanted) & (ext_pos >= 0), 1.0, 0.0).astype(BF16)


def conv_kernel(
    meta, x_hbm, taps_hbm, beta_hbm,
    act_ref, head_ref, edge_ref, taps_ref, beta_ref, x_ref, sems,
):
    copies = [
        pltpu.make_async_copy(x_hbm, x_ref, sems.at[0]),
        pltpu.make_async_copy(taps_hbm, taps_ref, sems.at[1]),
        pltpu.make_async_copy(beta_hbm, beta_ref, sems.at[2]),
    ]
    for copy in copies:
        copy.start()
    for copy in copies:
        copy.wait()
    rows = x_ref.shape[1]
    ends = request_ends(meta)
    first = meta[4]
    pos = first + iota((rows, 1), 0)
    begin = start_of(pos, ends)
    select = edge_select(
        meta, ends, first, first + rows - 1, first + iota((EDGE_ROWS, rows), 1)
    )
    for c in range(3):
        x = x_ref[c]
        edge_ref[c] = dot(select, x).astype(BF16)
        head_ref[c] = x[:HALO]
        wide = x.astype(F32)
        act_ref[c, HALO:] = conv_rows(wide, taps_ref[c], pos[HALO:], begin[HALO:])
        act_ref[c, :HALO] = jnp.zeros((HALO, x.shape[1]), BF16)


def prep_kernel(
    meta, act_ref, head_ref, part_ref, taps_ref, beta_ref, halo_ref,
    map_ref, uw_ref, local_ref, link_ref, kb_ref, ks_ref, edge_ref,
):
    rows = act_ref.shape[1]
    heads = act_ref.shape[2] // DK
    half = rows // 2
    ends = request_ends(meta)
    first = meta[4]
    pos = first + iota((rows, 1), 0)
    pos_r = first + iota((1, rows), 1)
    seg = seg_of(pos, ends)
    seg_r = seg_of(pos_r, ends)
    begin = start_of(pos, ends)
    coupled = jnp.where(begin < first, 1.0, 0.0).astype(F32)
    last = first + rows - 1
    last_seg = seg_of(last, ends)
    last_link = start_of(last, ends) < first
    in_last = jnp.where(seg == last_seg, 1.0, 0.0).astype(F32)
    select = edge_select(meta, ends, first, last, first - HALO + iota((EDGE_ROWS, HALO), 1))
    edge_ref[...] = jnp.zeros_like(edge_ref)

    planes = []
    for c in range(3):
        halo = halo_ref[c]
        picked = part_ref[c] + dot(select, halo).astype(BF16)
        picked = picked.astype(F32)
        for r in range(REQS):
            edge_ref[r, c * CONV : (c + 1) * CONV] = picked[r * CONV : (r + 1) * CONV]
        ext = jnp.concatenate([halo, head_ref[c]], axis=0).astype(F32)
        lead = conv_rows(ext, taps_ref[c], pos[:HALO], begin[:HALO])
        planes.append(jnp.concatenate([lead, act_ref[c, HALO:]], axis=0))

    row_id = iota((rows, rows), 0)
    col_id = iota((rows, rows), 1)
    same = seg == seg_r
    strict = same & (row_id > col_id)
    causal = same & (row_id >= col_id)
    diag = row_id == col_id
    row_h = iota((half, half), 0)
    col_h = iota((half, half), 1)
    eye_h = jnp.where(row_h == col_h, 1.0, 0.0).astype(F32)

    def as_row(column):
        return jnp.sum(jnp.where(diag, column, 0.0), axis=0, keepdims=True)

    def as_column(row):
        return jnp.sum(jnp.where(diag, row, 0.0), axis=1, keepdims=True)

    state = []
    for h in range(heads):
        lanes = slice(h * DK, (h + 1) * DK)
        qb, kb, vb = (planes[c][:, lanes] for c in range(3))
        q32, k32, v32 = (t.astype(F32) for t in (qb, kb, vb))
        qs = lax.rsqrt(jnp.sum(q32 * q32, axis=1, keepdims=True) + 1e-06)
        ks = lax.rsqrt(jnp.sum(k32 * k32, axis=1, keepdims=True) + 1e-06)
        ks_row = as_row(ks)
        beta = as_column(1.0 / (1.0 + jnp.exp(-beta_ref[h : h + 1, :])))
        system = jnp.where(strict, dot(kb, kb, NT) * (beta * ks) * ks_row, 0.0)
        scores = jnp.where(causal, dot(qb, kb, NT) * qs * ks_row, 0.0)
        targets = jnp.concatenate([beta * v32, (beta * coupled * ks) * k32], axis=1)
        state.append((q32 * qs, kb, ks, system, scores, targets))

    blocks = []
    for h in range(heads):
        system = state[h][3]
        for d in range(2):
            blocks.append(system[d * half : (d + 1) * half, d * half : (d + 1) * half])
    inverses = []
    low = ((row_h ^ col_h) == 1) & (row_h > col_h)
    for a in blocks:
        inverses.append(eye_h - jnp.where(low, a, 0.0))
    level = 1
    while (2 << level) <= half:
        low = (((row_h >> level) ^ (col_h >> level)) == 1) & (row_h > col_h)
        parts = [split(x) for x in inverses]
        inner = [dot_split(split(jnp.where(low, a, 0.0)), p) for a, p in zip(blocks, parts)]
        inverses = [x - dot_split(p, split(t)) for x, p, t in zip(inverses, parts, inner)]
        level += 1

    for h in range(heads):
        q32, kb, ks, system, scores, targets = state[h]
        top = dot32(inverses[2 * h], targets[:half])
        rest = targets[half:] - dot32(system[half:, :half], top)
        uw = jnp.concatenate([top, dot32(inverses[2 * h + 1], rest)], axis=0)
        uw_ref[h] = uw
        mixed = dot32(scores, uw)
        local_ref[h] = mixed[:, :DK]
        link_ref[h] = coupled * q32 - mixed[:, DK:]
        kb_ref[h] = kb
        ks_ref[h] = ks
        scaled = jnp.concatenate([uw[:, DK:] * ks, uw[:, :DK] * (ks * in_last)], axis=1)
        high, less = split(scaled)
        fold = dot(kb, high, TN) + dot(kb, less, TN)
        eye_k = jnp.where(iota((DK, DK), 0) == iota((DK, DK), 1), 1.0, 0.0).astype(F32)
        map_ref[h, :, :DK] = jnp.where(last_link, fold[:, :DK], eye_k).astype(BF16)
        map_ref[h, :, DK:] = fold[:, DK:].astype(BF16)


def joined(newer, older):
    return newer.astype(F32) + older.astype(F32) - dot(newer[:, :DK], older)


def twin_kernel(meta, own_ref, came_ref, twin_ref):
    odd = lax.rem(meta[7], 2) == 1
    for h in range(own_ref.shape[0]):
        own, came = own_ref[h], came_ref[h]
        newer = jnp.where(odd, own, came)
        older = jnp.where(odd, came, own)
        twin_ref[h] = joined(newer, older).astype(BF16)


def row_kernel(
    meta, own_ref, came_ref, twin_ref, other_ref, below_ref, cross_ref,
    prefix_ref, both_ref, tail_ref,
):
    here = meta[7]
    late = here >= ROW // 2
    odd = lax.rem(here, 2) == 1
    for h in range(own_ref.shape[0]):
        totals = []
        for same_ref, far_ref in ((twin_ref, other_ref), (below_ref, cross_ref)):
            same, far = same_ref[h], far_ref[h]
            newer = jnp.where(late, same, far)
            totals.append(joined(newer, jnp.where(late, far, same)).astype(BF16))
        both = joined(*totals).astype(BF16)
        both_ref[h] = both
        tail_ref[h] = both[:, DK:]
        other = other_ref[h]
        step = jnp.where(odd, came_ref[h], jnp.zeros_like(other))
        prefix_ref[h] = joined(step, jnp.where(late, other, jnp.zeros_like(other)))


def ends_kernel(meta, uw_ref, kb_ref, ks_ref, prefix_ref, edge_ref, *piece_refs):
    heads, rows, _ = uw_ref.shape
    ends = request_ends(meta)
    first = meta[4]
    pos = first + iota((rows, 1), 0)
    seg = seg_of(pos, ends)
    eye = jnp.where(iota((DK, DK), 0) == iota((DK, DK), 1), 1.0, 0.0).astype(F32)
    for k, ref in enumerate(piece_refs):
        r = lax.rem(meta[7] + k, REQS)
        end = ends[0]
        for i in range(1, REQS):
            end = jnp.where(r == i, ends[i], end)
        owned = (end - 1 >= first) & (end - 1 <= first + rows - 1)
        carried = jnp.where(end - meta[r] < first, 1.0, 0.0)
        ref[heads * DK :] = edge_ref[r].astype(BF16)

        @pl.when(owned)
        def _():
            for h in range(heads):
                scaled = jnp.where(seg == r, uw_ref[h] * ks_ref[h], 0.0)
                high, less = split(scaled)
                fold = dot(kb_ref[h], high, TN) + dot(kb_ref[h], less, TN)
                link = carried * eye - fold[:, DK:]
                prefix = prefix_ref[h]
                both = dot32(link, prefix)
                ref[h * DK : (h + 1) * DK, :DK] = (link - both[:, :DK]).astype(BF16)
                ref[h * DK : (h + 1) * DK, DK:] = (both[:, DK:] + fold[:, :DK]).astype(BF16)

        @pl.when(jnp.logical_not(owned))
        def _():
            ref[: heads * DK] = jnp.zeros((heads * DK, 2 * DK), BF16)


def state_kernel(ahead_ref, *refs):
    *piece_refs, pay_ref = refs
    maps = piece_refs[0][...]
    for ref in piece_refs[1:]:
        maps = maps + ref[...]
    heads = ahead_ref.shape[0]
    for h in range(heads):
        mine = maps[h * DK : (h + 1) * DK]
        high, less = split(ahead_ref[h])
        final = dot(mine[:, :DK], high) + dot(mine[:, :DK], less) + mine[:, DK:].astype(F32)
        pay_ref[h * DK : (h + 1) * DK] = final.astype(BF16)
        base = heads * DK + h * EDGE_ROWS
        pay_ref[base : base + EDGE_ROWS] = maps[heads * DK :, h * DK : (h + 1) * DK]


def sum_kernel(pay_ref, came_ref, sum_ref):
    sum_ref[...] = pay_ref[...] + came_ref[...]


def attend_kernel(
    meta, prefix_ref, wide_ref, tail_ref, local_ref, link_ref, gain_ref, w_ref,
    own_ref, other_ref, ahead_ref, heads_ref,
):
    heads, rows, _ = local_ref.shape
    wins, cores, piece, _ = heads_ref.shape
    win, core = meta[5], meta[6]
    gain = gain_ref[...]
    for h in range(heads):
        wide, prefix, tail = wide_ref[h], prefix_ref[h], tail_ref[h]
        ahead = wide[:, DK:].astype(F32) + tail.astype(F32) - dot(wide[:, :DK], tail)
        enter = prefix[:, DK:] + ahead - dot32(prefix[:, :DK], ahead)
        parts = split(enter)
        attended = local_ref[h] + dot_split(split(link_ref[h]), parts)
        scale = lax.rsqrt(jnp.mean(attended * attended, axis=1, keepdims=True) + 1e-05)
        normed = attended * scale * gain
        lanes = slice(h * DK, (h + 1) * DK)
        for p in range(wins * cores):
            heads_ref[p // cores, p % cores, :, lanes] = normed[p * piece : (p + 1) * piece].astype(
                BF16
            )
        ahead_ref[h] = ahead
    order = [lax.rem(win + k, wins) for k in range(wins)]
    w = w_ref[...]
    mine = jnp.concatenate([heads_ref[o, core] for o in order], axis=0)
    own_ref[...] = dot(mine, w)
    theirs = jnp.concatenate([heads_ref[o, cores - 1 - core] for o in order], axis=0)
    other_ref[...] = dot(theirs, w).astype(BF16)


def pair_kernel(own_ref, got_ref, keep_ref, *send_refs):
    piece = keep_ref.shape[0]
    keep_ref[...] = own_ref[:piece] + got_ref[:piece].astype(F32)
    for k, ref in enumerate(send_refs):
        part = slice((k + 1) * piece, (k + 2) * piece)
        ref[...] = (own_ref[part] + got_ref[part].astype(F32)).astype(BF16)


def norm_kernel(hidden_ref, gain_ref, keep_ref, *refs):
    *got, stream_ref, normed_ref = refs
    total = keep_ref[...]
    for ref in got:
        total = total + ref[...].astype(F32)
    total = hidden_ref[...].astype(F32) + total
    stream_ref[...] = total.astype(BF16)
    scale = lax.rsqrt(jnp.mean(total * total, axis=1, keepdims=True) + 1e-05)
    normed_ref[...] = (total * scale * gain_ref[...]).astype(BF16)


def columns_kernel(meta, mine_ref, peer_ref, *refs):
    *piece_refs, cols_ref = refs
    wins, rows, width = cols_ref.shape
    mine, peer = mine_ref[...], peer_ref[...]
    lower = jnp.where(meta[6] == 0, mine, peer)
    upper = jnp.where(meta[6] == 0, peer, mine)
    for k in range(wins):
        cols_ref[k, : rows // 2] = lower[:, k * width : (k + 1) * width]
        cols_ref[k, rows // 2 :] = upper[:, k * width : (k + 1) * width]
    for k, ref in enumerate(piece_refs):
        ref[...] = cols_ref[lax.rem(meta[5] + k, wins)]


def last_kernel(own_ref, *refs):
    *came, all_ref = refs
    total = own_ref[...]
    for ref in came:
        total = total + ref[...].astype(F32)
    all_ref[...] = total.astype(BF16)


def finish_kernel(meta, *refs):
    *quarters, state_ref, edge_ref, pay_ref = refs
    for k, ref in enumerate(quarters):
        pay_ref[lax.rem(meta[7] + REQS - k, REQS)] = ref[...]
    reqs, rows, _ = state_ref.shape
    heads = rows // DK
    for r in range(reqs):
        state_ref[r] = pay_ref[r, :rows].astype(F32)
    for h in range(heads):
        base = rows + h * EDGE_ROWS
        edges = [pay_ref[r, base : base + EDGE_ROWS].astype(F32) for r in range(reqs)]
        for c in range(3):
            for i in range(CONV - 1):
                spot = c * CONV + i
                lines = jnp.concatenate([e[spot : spot + 1] for e in edges], axis=0)
                edge_ref[i, c, :, h * DK : (h + 1) * DK] = lines.astype(BF16)


def body(qkv_in, conv_w, beta_logits, lengths, out_gain, w_out, hidden_in, norm_gain, w_qkv):
    rows = qkv_in.shape[0]
    width = qkv_in.shape[2]
    heads = width // DK
    model = w_out.shape[1]
    n_seq, wins, cores = (lax.axis_size(a) for a in ("seq", "win", "wout"))
    piece = rows // (wins * cores)
    seq, win, core = (lax.axis_index(a).astype(jnp.int32) for a in ("seq", "win", "wout"))
    meta = jnp.concatenate([lengths, jnp.stack([seq * rows, win, core, seq % ROW])])
    x = qkv_in.transpose(1, 0, 2)
    halo = shift(x[:, rows - HALO :], "seq", 1)
    act, lead, parts, taps, beta = call(
        conv_kernel,
        [
            out((3, rows, width), BF16),
            out((3, HALO, width), BF16),
            out((3, EDGE_ROWS, width), BF16),
            out((3, CONV, width), F32),
            out((heads, rows), F32),
        ],
        "conv",
        10**8,
        meta, *(in_hbm(a) for a in (x, conv_w, beta_logits)),
        scratch=[pltpu.VMEM((3, rows, width), BF16), pltpu.SemaphoreType.DMA((3,))],
        hbm=3,
    )
    maps, uw, local, link, kb, ks, edges = call(
        prep_kernel,
        [
            out((heads, DK, 2 * DK), BF16),
            out((heads, rows, 2 * DK), F32),
            out((heads, rows, DK), F32),
            out((heads, rows, DK), F32),
            out((heads, rows, DK), BF16),
            out((heads, rows, 1), F32),
            out((REQS, EDGE_ROWS, width), F32),
        ],
        "prep",
        2 * 10**9,
        meta, act, lead, parts, taps, beta, halo,
    )

    maps_out = out((heads, DK, 2 * DK), BF16)
    came = exchange(maps, "seq", 1)
    (twin,) = call(twin_kernel, [maps_out], "twin", 10**8, meta, maps, came)
    cross = lax.ppermute(
        twin, "seq", [(s, (s ^ (ROW - 1)) + ROW) for s in range(n_seq - ROW)]
    )
    prefix, both, tail = call(
        row_kernel,
        [out((heads, DK, 2 * DK), F32), maps_out, out((heads, DK, DK), BF16)],
        "row",
        10**8,
        meta, maps, came, twin, exchange(twin, "seq", ROW - 1), shift(twin, "seq", ROW), cross,
    )
    tail = shift(tail, "seq", 3 * ROW)
    wide = shift(both, "seq", ROW)
    piece_rows = heads * DK + EDGE_ROWS
    quarter = out((heads * (DK + EDGE_ROWS), DK), BF16)
    pieces = call(
        ends_kernel,
        [out((piece_rows, 2 * DK), BF16)] * ROW,
        "ends",
        10**8,
        meta, uw, kb, ks, prefix, edges,
    )
    pieces = [pieces[0]] + [row_rotate(pieces[k], k) for k in range(1, ROW)]
    own, other, ahead = call(
        attend_kernel,
        [
            out((wins * piece, model), F32),
            out((wins * piece, model), BF16),
            out((heads, DK, DK), F32),
        ],
        "attend",
        10**9,
        meta, prefix, wide, tail, local, link, out_gain.reshape(1, DK), w_out,
        scratch=[pltpu.VMEM((wins, cores, piece, width), BF16)],
    )
    got = rotate(other, "wout", 1)
    (payload,) = call(state_kernel, [quarter], "state", 10**10, ahead, *pieces, smem=0)
    own, payload = lax.optimization_barrier((own, payload))
    sums = call(
        pair_kernel,
        [out((piece, model), F32)] + [out((piece, model), BF16)] * (wins - 1),
        "pair",
        10**6,
        own, got,
        smem=0,
    )
    reduced = [rotate(sums[k], "win", k) for k in range(1, wins)]
    lines = n_seq // ROW
    bits = [b for b in (4, 2, 1) if 2 * b <= lines]
    came = exchange(payload, "seq", bits[0] * ROW)
    stream_out, normed = call(
        norm_kernel,
        [out((piece, model), BF16)] * 2,
        "norm",
        10**6,
        hidden_in, norm_gain.reshape(1, model), sums[0], *reduced,
        smem=0,
    )
    peer = rotate(normed, "wout", 1)
    (payload,) = call(sum_kernel, [quarter], "sum", 10**10, payload, came, smem=0)
    normed, payload = lax.optimization_barrier((normed, payload))
    cols = call(
        columns_kernel,
        [out((2 * piece, model // wins), BF16)] * wins,
        "columns",
        10**6,
        meta, normed, peer,
        scratch=[pltpu.VMEM((wins, 2 * piece, model // wins), BF16)],
    )
    blocks = [cols[0]] + [rotate(cols[k], "win", k) for k in range(1, wins)]

    def partial(k):
        return jnp.dot(blocks[(wins - k) % wins], w_qkv, preferred_element_type=F32)

    parts = [partial(k).astype(BF16) for k in range(1, wins)]
    arrived = [rotate(part, "win", k + 1) for k, part in enumerate(parts)]
    (projected,) = call(
        last_kernel,
        [out((2 * piece, w_qkv.shape[1]), BF16)],
        "last",
        10**10,
        partial(0), *arrived,
        smem=0,
    )

    if lines == 8:
        turns = [rotate(payload, "seq", steps * ROW) for steps in (1, 7, 2)]
        payload = payload + (turns[0] + turns[1]) + turns[2]
    else:
        for bit in bits[1:]:
            payload = payload + exchange(payload, "seq", bit * ROW)
    quarters = [payload] + [row_rotate(payload, k) for k in range(1, ROW)]
    projected, *quarters = lax.optimization_barrier((projected, *quarters))
    final_states, conv_edges = call(
        finish_kernel,
        [out((REQS, heads * DK, DK), F32), out((CONV - 1, 3, REQS, width), BF16)],
        "finish",
        10**6,
        meta, *quarters,
        scratch=[pltpu.VMEM((REQS, *quarter.shape), BF16)],
    )
    final_states = final_states.reshape(REQS, heads, DK, DK)
    conv_edges = conv_edges.transpose(2, 0, 1, 3)
    return (projected, stream_out, final_states, conv_edges)


def solution(mesh):
    return jax.shard_map(
        body,
        mesh=mesh,
        in_specs=(
            P("seq", None, ("win", "wout")),
            P(None, None, ("win", "wout")),
            P(("win", "wout"), "seq"),
            P(),
            P(),
            P(("win", "wout"), None),
            P(("seq", "win", "wout"), None),
            P(),
            P("win", "wout"),
        ),
        out_specs=(
            P(("seq", "win"), "wout"),
            P(("seq", "win", "wout"), None),
            P(None, ("win", "wout"), None, None),
            P(None, None, None, ("win", "wout")),
        ),
        check_vma=False,
    )
```

```python
import functools

import jax
import jax.numpy as jnp
from jax import lax
from jax.experimental import pallas as pl
from jax.experimental.pallas import tpu as pltpu
from jax.sharding import PartitionSpec as P

DK = 128
CONV = 4
REQS = 4
HALO = 16
ROW = 4
EDGE_ROWS = 16
INTERPRET = False
F32 = jnp.float32
BF16 = jnp.bfloat16
NN = ((1,), (0,))
NT = ((1,), (1,))
TN = ((0,), (0,))
VMEM = pl.BlockSpec(memory_space=pltpu.VMEM)
SMEM = pl.BlockSpec(memory_space=pltpu.SMEM)
HBM = pl.BlockSpec(memory_space=pltpu.HBM)


def shift(value, axis, steps):
    count = lax.axis_size(axis)
    return lax.ppermute(value, axis, [(s, s + steps) for s in range(max(0, count - steps))])


def rotate(value, axis, steps):
    count = lax.axis_size(axis)
    return lax.ppermute(value, axis, [(s, (s + steps) % count) for s in range(count)])


def row_rotate(value, steps):
    count = lax.axis_size("seq")
    pairs = [(s, s // ROW * ROW + (s + steps) % ROW) for s in range(count)]
    return lax.ppermute(value, "seq", pairs)


def exchange(value, axis, bit):
    return lax.ppermute(value, axis, [(s, s ^ bit) for s in range(lax.axis_size(axis))])


def dot(left, right, dims=NN):
    return lax.dot_general(left, right, (dims, ((), ())), preferred_element_type=F32)


def split(value):
    high = value.astype(BF16)
    return high, (value - high.astype(F32)).astype(BF16)


def dot_split(left, right, dims=NN):
    lh, ll = left
    rh, rl = right
    return dot(lh, rh, dims) + (dot(lh, rl, dims) + dot(ll, rh, dims))


def dot32(left, right, dims=NN):
    return dot_split(split(left), split(right), dims)


def call(kernel, outs, name, flops, *args, scratch=(), smem=1, hbm=0):
    size = sum(a.size * a.dtype.itemsize for a in args) + sum(
        o.size * o.dtype.itemsize for o in outs
    )
    return pl.pallas_call(
        kernel,
        out_shape=outs,
        in_specs=[SMEM] * smem + [HBM] * hbm + [VMEM] * (len(args) - smem - hbm),
        out_specs=[VMEM] * len(outs),
        scratch_shapes=list(scratch),
        name=name,
        interpret=INTERPRET,
        cost_estimate=pl.CostEstimate(flops=flops, bytes_accessed=size, transcendentals=0),
        compiler_params=pltpu.CompilerParams(vmem_limit_bytes=40 * 1024 * 1024),
    )(*args)


def in_hbm(value):
    return value if INTERPRET else pltpu.with_memory_space_constraint(value, pltpu.HBM)


def out(shape, dtype):
    return jax.ShapeDtypeStruct(shape, dtype)


def request_ends(meta):
    ends = [meta[0]]
    for r in range(1, REQS):
        ends.append(ends[-1] + meta[r])
    return ends


def seg_of(pos, ends):
    total = jnp.where(pos >= ends[0], 1, 0)
    for r in range(1, REQS):
        total = total + jnp.where(pos >= ends[r], 1, 0)
    return total


def start_of(pos, ends):
    begin = jnp.where(pos >= ends[0], ends[0], 0)
    for r in range(1, REQS):
        begin = jnp.maximum(begin, jnp.where(pos >= ends[r], ends[r], 0))
    return begin


def iota(shape, dim):
    return lax.broadcasted_iota(jnp.int32, shape, dim)


def conv_rows(ext, taps, pos, begin):
    pre = ext[HALO:] * taps[CONV - 1 : CONV]
    for back in range(1, CONV):
        moved = pltpu.roll(ext, back, 0)[HALO:]
        ok = jnp.where(pos - back >= begin, 1.0, 0.0).astype(F32)
        pre = pre + moved * taps[CONV - 1 - back : CONV - back] * ok
    return (pre / (1.0 + jnp.exp(-pre))).astype(BF16)


def edge_select(meta, ends, first, last, ext_pos):
    edge_id = iota((EDGE_ROWS, 1), 0)
    wanted = jnp.full((EDGE_ROWS, 1), -1, jnp.int32)
    for r in range(REQS):
        begin = ends[r] - meta[r]
        owned = (ends[r] - 1 >= first) & (ends[r] - 1 <= last)
        for i in range(CONV - 1):
            spot = ends[r] - (CONV - 1) + i
            good = owned & (spot >= begin)
            wanted = jnp.where(edge_id == r * CONV + i, jnp.where(good, spot, -1), wanted)
    return jnp.where((ext_pos == wanted) & (ext_pos >= 0), 1.0, 0.0).astype(BF16)


def conv_kernel(
    meta, x_hbm, taps_hbm, beta_hbm,
    act_ref, head_ref, edge_ref, taps_ref, beta_ref, x_ref, sems,
):
    copies = [
        pltpu.make_async_copy(x_hbm, x_ref, sems.at[0]),
        pltpu.make_async_copy(taps_hbm, taps_ref, sems.at[1]),
        pltpu.make_async_copy(beta_hbm, beta_ref, sems.at[2]),
    ]
    for copy in copies:
        copy.start()
    for copy in copies:
        copy.wait()
    rows = x_ref.shape[1]
    ends = request_ends(meta)
    first = meta[4]
    pos = first + iota((rows, 1), 0)
    begin = start_of(pos, ends)
    select = edge_select(
        meta, ends, first, first + rows - 1, first + iota((EDGE_ROWS, rows), 1)
    )
    for c in range(3):
        x = x_ref[c]
        edge_ref[c] = dot(select, x).astype(BF16)
        head_ref[c] = x[:HALO]
        wide = x.astype(F32)
        act_ref[c, HALO:] = conv_rows(wide, taps_ref[c], pos[HALO:], begin[HALO:])
        act_ref[c, :HALO] = jnp.zeros((HALO, x.shape[1]), BF16)


def prep_kernel(
    meta, act_ref, head_ref, part_ref, taps_ref, beta_ref, halo_ref,
    map_ref, uw_ref, local_ref, link_ref, kb_ref, ks_ref, edge_ref,
):
    rows = act_ref.shape[1]
    heads = act_ref.shape[2] // DK
    half = rows // 2
    ends = request_ends(meta)
    first = meta[4]
    pos = first + iota((rows, 1), 0)
    pos_r = first + iota((1, rows), 1)
    seg = seg_of(pos, ends)
    seg_r = seg_of(pos_r, ends)
    begin = start_of(pos, ends)
    coupled = jnp.where(begin < first, 1.0, 0.0).astype(F32)
    last = first + rows - 1
    last_seg = seg_of(last, ends)
    last_link = start_of(last, ends) < first
    in_last = jnp.where(seg == last_seg, 1.0, 0.0).astype(F32)
    select = edge_select(meta, ends, first, last, first - HALO + iota((EDGE_ROWS, HALO), 1))
    edge_ref[...] = jnp.zeros_like(edge_ref)

    planes = []
    for c in range(3):
        halo = halo_ref[c]
        picked = part_ref[c] + dot(select, halo).astype(BF16)
        picked = picked.astype(F32)
        for r in range(REQS):
            edge_ref[r, c * CONV : (c + 1) * CONV] = picked[r * CONV : (r + 1) * CONV]
        ext = jnp.concatenate([halo, head_ref[c]], axis=0).astype(F32)
        lead = conv_rows(ext, taps_ref[c], pos[:HALO], begin[:HALO])
        planes.append(jnp.concatenate([lead, act_ref[c, HALO:]], axis=0))

    row_id = iota((rows, rows), 0)
    col_id = iota((rows, rows), 1)
    same = seg == seg_r
    strict = same & (row_id > col_id)
    causal = same & (row_id >= col_id)
    diag = row_id == col_id
    row_h = iota((half, half), 0)
    col_h = iota((half, half), 1)
    eye_h = jnp.where(row_h == col_h, 1.0, 0.0).astype(F32)

    def as_row(column):
        return jnp.sum(jnp.where(diag, column, 0.0), axis=0, keepdims=True)

    def as_column(row):
        return jnp.sum(jnp.where(diag, row, 0.0), axis=1, keepdims=True)

    state = []
    for h in range(heads):
        lanes = slice(h * DK, (h + 1) * DK)
        qb, kb, vb = (planes[c][:, lanes] for c in range(3))
        q32, k32, v32 = (t.astype(F32) for t in (qb, kb, vb))
        qs = lax.rsqrt(jnp.sum(q32 * q32, axis=1, keepdims=True) + 1e-06)
        ks = lax.rsqrt(jnp.sum(k32 * k32, axis=1, keepdims=True) + 1e-06)
        ks_row = as_row(ks)
        beta = as_column(1.0 / (1.0 + jnp.exp(-beta_ref[h : h + 1, :])))
        system = jnp.where(strict, dot(kb, kb, NT) * (beta * ks) * ks_row, 0.0)
        scores = jnp.where(causal, dot(qb, kb, NT) * qs * ks_row, 0.0)
        targets = jnp.concatenate([beta * v32, (beta * coupled * ks) * k32], axis=1)
        state.append((q32 * qs, kb, ks, system, scores, targets))

    blocks = []
    for h in range(heads):
        system = state[h][3]
        for d in range(2):
            blocks.append(system[d * half : (d + 1) * half, d * half : (d + 1) * half])
    inverses = []
    low = ((row_h ^ col_h) == 1) & (row_h > col_h)
    for a in blocks:
        inverses.append(eye_h - jnp.where(low, a, 0.0))
    level = 1
    while (2 << level) <= half:
        low = (((row_h >> level) ^ (col_h >> level)) == 1) & (row_h > col_h)
        parts = [split(x) for x in inverses]
        inner = [dot_split(split(jnp.where(low, a, 0.0)), p) for a, p in zip(blocks, parts)]
        inverses = [x - dot_split(p, split(t)) for x, p, t in zip(inverses, parts, inner)]
        level += 1

    for h in range(heads):
        q32, kb, ks, system, scores, targets = state[h]
        top = dot32(inverses[2 * h], targets[:half])
        rest = targets[half:] - dot32(system[half:, :half], top)
        uw = jnp.concatenate([top, dot32(inverses[2 * h + 1], rest)], axis=0)
        uw_ref[h] = uw
        mixed = dot32(scores, uw)
        local_ref[h] = mixed[:, :DK]
        link_ref[h] = coupled * q32 - mixed[:, DK:]
        kb_ref[h] = kb
        ks_ref[h] = ks
        scaled = jnp.concatenate([uw[:, DK:] * ks, uw[:, :DK] * (ks * in_last)], axis=1)
        high, less = split(scaled)
        fold = dot(kb, high, TN) + dot(kb, less, TN)
        eye_k = jnp.where(iota((DK, DK), 0) == iota((DK, DK), 1), 1.0, 0.0).astype(F32)
        map_ref[h, :, :DK] = jnp.where(last_link, fold[:, :DK], eye_k).astype(BF16)
        map_ref[h, :, DK:] = fold[:, DK:].astype(BF16)


def joined(newer, older):
    return newer.astype(F32) + older.astype(F32) - dot(newer[:, :DK], older)


def twin_kernel(meta, own_ref, came_ref, twin_ref):
    odd = lax.rem(meta[7], 2) == 1
    for h in range(own_ref.shape[0]):
        own, came = own_ref[h], came_ref[h]
        newer = jnp.where(odd, own, came)
        older = jnp.where(odd, came, own)
        twin_ref[h] = joined(newer, older).astype(BF16)


def row_kernel(
    meta, own_ref, came_ref, twin_ref, other_ref, below_ref, cross_ref,
    prefix_ref, both_ref, tail_ref,
):
    here = meta[7]
    late = here >= ROW // 2
    odd = lax.rem(here, 2) == 1
    for h in range(own_ref.shape[0]):
        totals = []
        for same_ref, far_ref in ((twin_ref, other_ref), (below_ref, cross_ref)):
            same, far = same_ref[h], far_ref[h]
            newer = jnp.where(late, same, far)
            totals.append(joined(newer, jnp.where(late, far, same)).astype(BF16))
        both = joined(*totals).astype(BF16)
        both_ref[h] = both
        tail_ref[h] = both[:, DK:]
        other = other_ref[h]
        step = jnp.where(odd, came_ref[h], jnp.zeros_like(other))
        prefix_ref[h] = joined(step, jnp.where(late, other, jnp.zeros_like(other)))


def ends_kernel(meta, uw_ref, kb_ref, ks_ref, prefix_ref, edge_ref, *piece_refs):
    heads, rows, _ = uw_ref.shape
    ends = request_ends(meta)
    first = meta[4]
    pos = first + iota((rows, 1), 0)
    seg = seg_of(pos, ends)
    eye = jnp.where(iota((DK, DK), 0) == iota((DK, DK), 1), 1.0, 0.0).astype(F32)
    for k, ref in enumerate(piece_refs):
        r = lax.rem(meta[7] + k, REQS)
        end = ends[0]
        for i in range(1, REQS):
            end = jnp.where(r == i, ends[i], end)
        owned = (end - 1 >= first) & (end - 1 <= first + rows - 1)
        carried = jnp.where(end - meta[r] < first, 1.0, 0.0)
        ref[heads * DK :] = edge_ref[r].astype(BF16)

        @pl.when(owned)
        def _():
            for h in range(heads):
                scaled = jnp.where(seg == r, uw_ref[h] * ks_ref[h], 0.0)
                high, less = split(scaled)
                fold = dot(kb_ref[h], high, TN) + dot(kb_ref[h], less, TN)
                link = carried * eye - fold[:, DK:]
                prefix = prefix_ref[h]
                both = dot32(link, prefix)
                ref[h * DK : (h + 1) * DK, :DK] = (link - both[:, :DK]).astype(BF16)
                ref[h * DK : (h + 1) * DK, DK:] = (both[:, DK:] + fold[:, :DK]).astype(BF16)

        @pl.when(jnp.logical_not(owned))
        def _():
            ref[: heads * DK] = jnp.zeros((heads * DK, 2 * DK), BF16)


def state_kernel(ahead_ref, *refs):
    *piece_refs, pay_ref = refs
    maps = piece_refs[0][...]
    for ref in piece_refs[1:]:
        maps = maps + ref[...]
    heads = ahead_ref.shape[0]
    for h in range(heads):
        mine = maps[h * DK : (h + 1) * DK]
        high, less = split(ahead_ref[h])
        final = dot(mine[:, :DK], high) + dot(mine[:, :DK], less) + mine[:, DK:].astype(F32)
        pay_ref[h * DK : (h + 1) * DK] = final.astype(BF16)
        base = heads * DK + h * EDGE_ROWS
        pay_ref[base : base + EDGE_ROWS] = maps[heads * DK :, h * DK : (h + 1) * DK]


def sum_kernel(pay_ref, came_ref, sum_ref):
    sum_ref[...] = pay_ref[...] + came_ref[...]


def attend_kernel(
    meta, prefix_ref, wide_ref, tail_ref, local_ref, link_ref, gain_ref, w_ref,
    own_ref, other_ref, ahead_ref, heads_ref,
):
    heads, rows, _ = local_ref.shape
    wins, cores, piece, _ = heads_ref.shape
    win, core = meta[5], meta[6]
    gain = gain_ref[...]
    for h in range(heads):
        wide, prefix, tail = wide_ref[h], prefix_ref[h], tail_ref[h]
        ahead = wide[:, DK:].astype(F32) + tail.astype(F32) - dot(wide[:, :DK], tail)
        enter = prefix[:, DK:] + ahead - dot32(prefix[:, :DK], ahead)
        parts = split(enter)
        attended = local_ref[h] + dot_split(split(link_ref[h]), parts)
        scale = lax.rsqrt(jnp.mean(attended * attended, axis=1, keepdims=True) + 1e-05)
        normed = attended * scale * gain
        lanes = slice(h * DK, (h + 1) * DK)
        for p in range(wins * cores):
            heads_ref[p // cores, p % cores, :, lanes] = normed[p * piece : (p + 1) * piece].astype(
                BF16
            )
        ahead_ref[h] = ahead
    order = [lax.rem(win + k, wins) for k in range(wins)]
    w = w_ref[...]
    mine = jnp.concatenate([heads_ref[o, core] for o in order], axis=0)
    own_ref[...] = dot(mine, w)
    theirs = jnp.concatenate([heads_ref[o, cores - 1 - core] for o in order], axis=0)
    other_ref[...] = dot(theirs, w).astype(BF16)


def pair_kernel(own_ref, got_ref, keep_ref, *send_refs):
    piece = keep_ref.shape[0]
    keep_ref[...] = own_ref[:piece] + got_ref[:piece].astype(F32)
    for k, ref in enumerate(send_refs):
        part = slice((k + 1) * piece, (k + 2) * piece)
        ref[...] = (own_ref[part] + got_ref[part].astype(F32)).astype(BF16)


def norm_kernel(hidden_ref, gain_ref, keep_ref, *refs):
    *got, stream_ref, normed_ref = refs
    total = keep_ref[...]
    for ref in got:
        total = total + ref[...].astype(F32)
    total = hidden_ref[...].astype(F32) + total
    stream_ref[...] = total.astype(BF16)
    scale = lax.rsqrt(jnp.mean(total * total, axis=1, keepdims=True) + 1e-05)
    normed_ref[...] = (total * scale * gain_ref[...]).astype(BF16)


def columns_kernel(meta, mine_ref, peer_ref, *refs):
    *piece_refs, cols_ref = refs
    wins, rows, width = cols_ref.shape
    mine, peer = mine_ref[...], peer_ref[...]
    lower = jnp.where(meta[6] == 0, mine, peer)
    upper = jnp.where(meta[6] == 0, peer, mine)
    for k in range(wins):
        cols_ref[k, : rows // 2] = lower[:, k * width : (k + 1) * width]
        cols_ref[k, rows // 2 :] = upper[:, k * width : (k + 1) * width]
    for k, ref in enumerate(piece_refs):
        ref[...] = cols_ref[lax.rem(meta[5] + k, wins)]


def last_kernel(own_ref, *refs):
    *came, all_ref = refs
    total = own_ref[...]
    for ref in came:
        total = total + ref[...].astype(F32)
    all_ref[...] = total.astype(BF16)


def finish_kernel(meta, *refs):
    *quarters, state_ref, edge_ref, pay_ref = refs
    for k, ref in enumerate(quarters):
        pay_ref[lax.rem(meta[7] + REQS - k, REQS)] = ref[...]
    reqs, rows, _ = state_ref.shape
    heads = rows // DK
    for r in range(reqs):
        state_ref[r] = pay_ref[r, :rows].astype(F32)
    for h in range(heads):
        base = rows + h * EDGE_ROWS
        edges = [pay_ref[r, base : base + EDGE_ROWS].astype(F32) for r in range(reqs)]
        for c in range(3):
            for i in range(CONV - 1):
                spot = c * CONV + i
                lines = jnp.concatenate([e[spot : spot + 1] for e in edges], axis=0)
                edge_ref[i, c, :, h * DK : (h + 1) * DK] = lines.astype(BF16)


def body(qkv_in, conv_w, beta_logits, lengths, out_gain, w_out, hidden_in, norm_gain, w_qkv):
    rows = qkv_in.shape[0]
    width = qkv_in.shape[2]
    heads = width // DK
    model = w_out.shape[1]
    n_seq, wins, cores = (lax.axis_size(a) for a in ("seq", "win", "wout"))
    piece = rows // (wins * cores)
    seq, win, core = (lax.axis_index(a).astype(jnp.int32) for a in ("seq", "win", "wout"))
    meta = jnp.concatenate([lengths, jnp.stack([seq * rows, win, core, seq % ROW])])
    x = qkv_in.transpose(1, 0, 2)
    halo = shift(x[:, rows - HALO :], "seq", 1)
    act, lead, parts, taps, beta = call(
        conv_kernel,
        [
            out((3, rows, width), BF16),
            out((3, HALO, width), BF16),
            out((3, EDGE_ROWS, width), BF16),
            out((3, CONV, width), F32),
            out((heads, rows), F32),
        ],
        "conv",
        10**8,
        meta, *(in_hbm(a) for a in (x, conv_w, beta_logits)),
        scratch=[pltpu.VMEM((3, rows, width), BF16), pltpu.SemaphoreType.DMA((3,))],
        hbm=3,
    )
    maps, uw, local, link, kb, ks, edges = call(
        prep_kernel,
        [
            out((heads, DK, 2 * DK), BF16),
            out((heads, rows, 2 * DK), F32),
            out((heads, rows, DK), F32),
            out((heads, rows, DK), F32),
            out((heads, rows, DK), BF16),
            out((heads, rows, 1), F32),
            out((REQS, EDGE_ROWS, width), F32),
        ],
        "prep",
        2 * 10**9,
        meta, act, lead, parts, taps, beta, halo,
    )

    maps_out = out((heads, DK, 2 * DK), BF16)
    came = exchange(maps, "seq", 1)
    (twin,) = call(twin_kernel, [maps_out], "twin", 10**8, meta, maps, came)
    cross = lax.ppermute(
        twin, "seq", [(s, (s ^ (ROW - 1)) + ROW) for s in range(n_seq - ROW)]
    )
    prefix, both, tail = call(
        row_kernel,
        [out((heads, DK, 2 * DK), F32), maps_out, out((heads, DK, DK), BF16)],
        "row",
        10**8,
        meta, maps, came, twin, exchange(twin, "seq", ROW - 1), shift(twin, "seq", ROW), cross,
    )
    tail = shift(tail, "seq", 3 * ROW)
    wide = shift(both, "seq", ROW)
    piece_rows = heads * DK + EDGE_ROWS
    quarter = out((heads * (DK + EDGE_ROWS), DK), BF16)
    pieces = call(
        ends_kernel,
        [out((piece_rows, 2 * DK), BF16)] * ROW,
        "ends",
        10**8,
        meta, uw, kb, ks, prefix, edges,
    )
    pieces = [pieces[0]] + [row_rotate(pieces[k], k) for k in range(1, ROW)]
    own, other, ahead = call(
        attend_kernel,
        [
            out((wins * piece, model), F32),
            out((wins * piece, model), BF16),
            out((heads, DK, DK), F32),
        ],
        "attend",
        10**9,
        meta, prefix, wide, tail, local, link, out_gain.reshape(1, DK), w_out,
        scratch=[pltpu.VMEM((wins, cores, piece, width), BF16)],
    )
    got = rotate(other, "wout", 1)
    (payload,) = call(state_kernel, [quarter], "state", 10**10, ahead, *pieces, smem=0)
    own, payload = lax.optimization_barrier((own, payload))
    sums = call(
        pair_kernel,
        [out((piece, model), F32)] + [out((piece, model), BF16)] * (wins - 1),
        "pair",
        10**6,
        own, got,
        smem=0,
    )
    reduced = [rotate(sums[k], "win", k) for k in range(1, wins)]
    lines = n_seq // ROW
    bits = [b for b in (4, 2, 1) if 2 * b <= lines]
    came = exchange(payload, "seq", bits[0] * ROW)
    stream_out, normed = call(
        norm_kernel,
        [out((piece, model), BF16)] * 2,
        "norm",
        10**6,
        hidden_in, norm_gain.reshape(1, model), sums[0], *reduced,
        smem=0,
    )
    peer = rotate(normed, "wout", 1)
    (payload,) = call(sum_kernel, [quarter], "sum", 10**10, payload, came, smem=0)
    normed, payload = lax.optimization_barrier((normed, payload))
    cols = call(
        columns_kernel,
        [out((2 * piece, model // wins), BF16)] * wins,
        "columns",
        10**6,
        meta, normed, peer,
        scratch=[pltpu.VMEM((wins, 2 * piece, model // wins), BF16)],
    )
    blocks = [cols[0]] + [rotate(cols[k], "win", k) for k in range(1, wins)]

    def partial(k):
        return jnp.dot(blocks[(wins - k) % wins], w_qkv, preferred_element_type=F32)

    parts = [partial(k).astype(BF16) for k in range(1, wins)]
    arrived = [rotate(part, "win", k + 1) for k, part in enumerate(parts)]
    if lines == 8:
        turns = [rotate(payload, "seq", steps * ROW) for steps in (1, 7, 2)]
        payload = payload + (turns[0] + turns[1]) + turns[2]
    else:
        for bit in bits[1:]:
            payload = payload + exchange(payload, "seq", bit * ROW)
    quarters = [payload] + [row_rotate(payload, k) for k in range(1, ROW)]
    *arrived, payload = lax.optimization_barrier((*arrived, quarters[1]))
    quarters[1] = payload
    (projected,) = call(
        last_kernel,
        [out((2 * piece, w_qkv.shape[1]), BF16)],
        "last",
        10**10,
        partial(0), *arrived,
        smem=0,
    )

    final_states, conv_edges = call(
        finish_kernel,
        [out((REQS, heads * DK, DK), F32), out((CONV - 1, 3, REQS, width), BF16)],
        "finish",
        10**6,
        meta, *quarters,
        scratch=[pltpu.VMEM((REQS, *quarter.shape), BF16)],
    )
    final_states = final_states.reshape(REQS, heads, DK, DK)
    conv_edges = conv_edges.transpose(2, 0, 1, 3)
    return (projected, stream_out, final_states, conv_edges)


def solution(mesh):
    return jax.shard_map(
        body,
        mesh=mesh,
        in_specs=(
            P("seq", None, ("win", "wout")),
            P(None, None, ("win", "wout")),
            P(("win", "wout"), "seq"),
            P(),
            P(),
            P(("win", "wout"), None),
            P(("seq", "win", "wout"), None),
            P(),
            P("win", "wout"),
        ),
        out_specs=(
            P(("seq", "win"), "wout"),
            P(("seq", "win", "wout"), None),
            P(None, ("win", "wout"), None, None),
            P(None, None, None, ("win", "wout")),
        ),
        check_vma=False,
    )
```

```python
import functools

import jax
import jax.numpy as jnp
from jax import lax
from jax.experimental import pallas as pl
from jax.experimental.pallas import tpu as pltpu
from jax.sharding import PartitionSpec as P

DK = 128
CONV = 4
REQS = 4
HALO = 16
ROW = 4
EDGE_ROWS = 16
INTERPRET = False
F32 = jnp.float32
BF16 = jnp.bfloat16
NN = ((1,), (0,))
NT = ((1,), (1,))
TN = ((0,), (0,))
VMEM = pl.BlockSpec(memory_space=pltpu.VMEM)
SMEM = pl.BlockSpec(memory_space=pltpu.SMEM)
HBM = pl.BlockSpec(memory_space=pltpu.HBM)


def shift(value, axis, steps):
    count = lax.axis_size(axis)
    return lax.ppermute(value, axis, [(s, s + steps) for s in range(max(0, count - steps))])


def rotate(value, axis, steps):
    count = lax.axis_size(axis)
    return lax.ppermute(value, axis, [(s, (s + steps) % count) for s in range(count)])


def row_rotate(value, steps):
    count = lax.axis_size("seq")
    pairs = [(s, s // ROW * ROW + (s + steps) % ROW) for s in range(count)]
    return lax.ppermute(value, "seq", pairs)


def exchange(value, axis, bit):
    return lax.ppermute(value, axis, [(s, s ^ bit) for s in range(lax.axis_size(axis))])


def dot(left, right, dims=NN):
    return lax.dot_general(left, right, (dims, ((), ())), preferred_element_type=F32)


def split(value):
    high = value.astype(BF16)
    return high, (value - high.astype(F32)).astype(BF16)


def dot_split(left, right, dims=NN):
    lh, ll = left
    rh, rl = right
    return dot(lh, rh, dims) + (dot(lh, rl, dims) + dot(ll, rh, dims))


def dot32(left, right, dims=NN):
    return dot_split(split(left), split(right), dims)


def call(kernel, outs, name, flops, *args, scratch=(), smem=1, hbm=0):
    size = sum(a.size * a.dtype.itemsize for a in args) + sum(
        o.size * o.dtype.itemsize for o in outs
    )
    return pl.pallas_call(
        kernel,
        out_shape=outs,
        in_specs=[SMEM] * smem + [HBM] * hbm + [VMEM] * (len(args) - smem - hbm),
        out_specs=[VMEM] * len(outs),
        scratch_shapes=list(scratch),
        name=name,
        interpret=INTERPRET,
        cost_estimate=pl.CostEstimate(flops=flops, bytes_accessed=size, transcendentals=0),
        compiler_params=pltpu.CompilerParams(vmem_limit_bytes=40 * 1024 * 1024),
    )(*args)


def in_hbm(value):
    return value if INTERPRET else pltpu.with_memory_space_constraint(value, pltpu.HBM)


def out(shape, dtype):
    return jax.ShapeDtypeStruct(shape, dtype)


def request_ends(meta):
    ends = [meta[0]]
    for r in range(1, REQS):
        ends.append(ends[-1] + meta[r])
    return ends


def seg_of(pos, ends):
    total = jnp.where(pos >= ends[0], 1, 0)
    for r in range(1, REQS):
        total = total + jnp.where(pos >= ends[r], 1, 0)
    return total


def start_of(pos, ends):
    begin = jnp.where(pos >= ends[0], ends[0], 0)
    for r in range(1, REQS):
        begin = jnp.maximum(begin, jnp.where(pos >= ends[r], ends[r], 0))
    return begin


def iota(shape, dim):
    return lax.broadcasted_iota(jnp.int32, shape, dim)


def conv_rows(ext, taps, pos, begin):
    pre = ext[HALO:] * taps[CONV - 1 : CONV]
    for back in range(1, CONV):
        moved = pltpu.roll(ext, back, 0)[HALO:]
        ok = jnp.where(pos - back >= begin, 1.0, 0.0).astype(F32)
        pre = pre + moved * taps[CONV - 1 - back : CONV - back] * ok
    return (pre / (1.0 + jnp.exp(-pre))).astype(BF16)


def edge_select(meta, ends, first, last, ext_pos):
    edge_id = iota((EDGE_ROWS, 1), 0)
    wanted = jnp.full((EDGE_ROWS, 1), -1, jnp.int32)
    for r in range(REQS):
        begin = ends[r] - meta[r]
        owned = (ends[r] - 1 >= first) & (ends[r] - 1 <= last)
        for i in range(CONV - 1):
            spot = ends[r] - (CONV - 1) + i
            good = owned & (spot >= begin)
            wanted = jnp.where(edge_id == r * CONV + i, jnp.where(good, spot, -1), wanted)
    return jnp.where((ext_pos == wanted) & (ext_pos >= 0), 1.0, 0.0).astype(BF16)


def conv_kernel(
    meta, x_hbm, taps_hbm, beta_hbm,
    act_ref, head_ref, edge_ref, taps_ref, beta_ref, x_ref, sems,
):
    copies = [
        pltpu.make_async_copy(x_hbm, x_ref, sems.at[0]),
        pltpu.make_async_copy(taps_hbm, taps_ref, sems.at[1]),
        pltpu.make_async_copy(beta_hbm, beta_ref, sems.at[2]),
    ]
    for copy in copies:
        copy.start()
    for copy in copies:
        copy.wait()
    rows = x_ref.shape[1]
    ends = request_ends(meta)
    first = meta[4]
    pos = first + iota((rows, 1), 0)
    begin = start_of(pos, ends)
    select = edge_select(
        meta, ends, first, first + rows - 1, first + iota((EDGE_ROWS, rows), 1)
    )
    for c in range(3):
        x = x_ref[c]
        edge_ref[c] = dot(select, x).astype(BF16)
        head_ref[c] = x[:HALO]
        wide = x.astype(F32)
        act_ref[c, HALO:] = conv_rows(wide, taps_ref[c], pos[HALO:], begin[HALO:])
        act_ref[c, :HALO] = jnp.zeros((HALO, x.shape[1]), BF16)


def prep_kernel(
    meta, act_ref, head_ref, part_ref, taps_ref, beta_ref, halo_ref,
    map_ref, uw_ref, local_ref, link_ref, kb_ref, ks_ref, edge_ref,
):
    rows = act_ref.shape[1]
    heads = act_ref.shape[2] // DK
    half = rows // 2
    ends = request_ends(meta)
    first = meta[4]
    pos = first + iota((rows, 1), 0)
    pos_r = first + iota((1, rows), 1)
    seg = seg_of(pos, ends)
    seg_r = seg_of(pos_r, ends)
    begin = start_of(pos, ends)
    coupled = jnp.where(begin < first, 1.0, 0.0).astype(F32)
    last = first + rows - 1
    last_seg = seg_of(last, ends)
    last_link = start_of(last, ends) < first
    in_last = jnp.where(seg == last_seg, 1.0, 0.0).astype(F32)
    select = edge_select(meta, ends, first, last, first - HALO + iota((EDGE_ROWS, HALO), 1))
    edge_ref[...] = jnp.zeros_like(edge_ref)

    planes = []
    for c in range(3):
        halo = halo_ref[c]
        picked = part_ref[c] + dot(select, halo).astype(BF16)
        picked = picked.astype(F32)
        for r in range(REQS):
            edge_ref[r, c * CONV : (c + 1) * CONV] = picked[r * CONV : (r + 1) * CONV]
        ext = jnp.concatenate([halo, head_ref[c]], axis=0).astype(F32)
        lead = conv_rows(ext, taps_ref[c], pos[:HALO], begin[:HALO])
        planes.append(jnp.concatenate([lead, act_ref[c, HALO:]], axis=0))

    row_id = iota((rows, rows), 0)
    col_id = iota((rows, rows), 1)
    same = seg == seg_r
    strict = same & (row_id > col_id)
    causal = same & (row_id >= col_id)
    diag = row_id == col_id
    row_h = iota((half, half), 0)
    col_h = iota((half, half), 1)
    eye_h = jnp.where(row_h == col_h, 1.0, 0.0).astype(F32)

    def as_row(column):
        return jnp.sum(jnp.where(diag, column, 0.0), axis=0, keepdims=True)

    def as_column(row):
        return jnp.sum(jnp.where(diag, row, 0.0), axis=1, keepdims=True)

    state = []
    for h in range(heads):
        lanes = slice(h * DK, (h + 1) * DK)
        qb, kb, vb = (planes[c][:, lanes] for c in range(3))
        q32, k32, v32 = (t.astype(F32) for t in (qb, kb, vb))
        qs = lax.rsqrt(jnp.sum(q32 * q32, axis=1, keepdims=True) + 1e-06)
        ks = lax.rsqrt(jnp.sum(k32 * k32, axis=1, keepdims=True) + 1e-06)
        ks_row = as_row(ks)
        beta = as_column(1.0 / (1.0 + jnp.exp(-beta_ref[h : h + 1, :])))
        system = jnp.where(strict, dot(kb, kb, NT) * (beta * ks) * ks_row, 0.0)
        scores = jnp.where(causal, dot(qb, kb, NT) * qs * ks_row, 0.0)
        targets = jnp.concatenate([beta * v32, (beta * coupled * ks) * k32], axis=1)
        state.append((q32 * qs, kb, ks, system, scores, targets))

    blocks = []
    for h in range(heads):
        system = state[h][3]
        for d in range(2):
            blocks.append(system[d * half : (d + 1) * half, d * half : (d + 1) * half])
    inverses = []
    low = ((row_h ^ col_h) == 1) & (row_h > col_h)
    for a in blocks:
        inverses.append(eye_h - jnp.where(low, a, 0.0))
    level = 1
    while (2 << level) <= half:
        low = (((row_h >> level) ^ (col_h >> level)) == 1) & (row_h > col_h)
        parts = [split(x) for x in inverses]
        inner = [dot_split(split(jnp.where(low, a, 0.0)), p) for a, p in zip(blocks, parts)]
        inverses = [x - dot_split(p, split(t)) for x, p, t in zip(inverses, parts, inner)]
        level += 1

    for h in range(heads):
        q32, kb, ks, system, scores, targets = state[h]
        top = dot32(inverses[2 * h], targets[:half])
        rest = targets[half:] - dot32(system[half:, :half], top)
        uw = jnp.concatenate([top, dot32(inverses[2 * h + 1], rest)], axis=0)
        uw_ref[h] = uw
        mixed = dot32(scores, uw)
        local_ref[h] = mixed[:, :DK]
        link_ref[h] = coupled * q32 - mixed[:, DK:]
        kb_ref[h] = kb
        ks_ref[h] = ks
        scaled = jnp.concatenate([uw[:, DK:] * ks, uw[:, :DK] * (ks * in_last)], axis=1)
        high, less = split(scaled)
        fold = dot(kb, high, TN) + dot(kb, less, TN)
        eye_k = jnp.where(iota((DK, DK), 0) == iota((DK, DK), 1), 1.0, 0.0).astype(F32)
        map_ref[h, :, :DK] = jnp.where(last_link, fold[:, :DK], eye_k).astype(BF16)
        map_ref[h, :, DK:] = fold[:, DK:].astype(BF16)


def joined(newer, older):
    return newer.astype(F32) + older.astype(F32) - dot(newer[:, :DK], older)


def twin_kernel(meta, own_ref, came_ref, twin_ref):
    odd = lax.rem(meta[7], 2) == 1
    for h in range(own_ref.shape[0]):
        own, came = own_ref[h], came_ref[h]
        newer = jnp.where(odd, own, came)
        older = jnp.where(odd, came, own)
        twin_ref[h] = joined(newer, older).astype(BF16)


def row_kernel(
    meta, own_ref, came_ref, twin_ref, other_ref, below_ref, cross_ref,
    prefix_ref, both_ref, tail_ref,
):
    here = meta[7]
    late = here >= ROW // 2
    odd = lax.rem(here, 2) == 1
    for h in range(own_ref.shape[0]):
        totals = []
        for same_ref, far_ref in ((twin_ref, other_ref), (below_ref, cross_ref)):
            same, far = same_ref[h], far_ref[h]
            newer = jnp.where(late, same, far)
            totals.append(joined(newer, jnp.where(late, far, same)).astype(BF16))
        both = joined(*totals).astype(BF16)
        both_ref[h] = both
        tail_ref[h] = both[:, DK:]
        other = other_ref[h]
        step = jnp.where(odd, came_ref[h], jnp.zeros_like(other))
        prefix_ref[h] = joined(step, jnp.where(late, other, jnp.zeros_like(other)))


def ends_kernel(meta, uw_ref, kb_ref, ks_ref, prefix_ref, edge_ref, *piece_refs):
    heads, rows, _ = uw_ref.shape
    ends = request_ends(meta)
    first = meta[4]
    pos = first + iota((rows, 1), 0)
    seg = seg_of(pos, ends)
    eye = jnp.where(iota((DK, DK), 0) == iota((DK, DK), 1), 1.0, 0.0).astype(F32)
    for k, ref in enumerate(piece_refs):
        r = lax.rem(meta[7] + k, REQS)
        end = ends[0]
        for i in range(1, REQS):
            end = jnp.where(r == i, ends[i], end)
        owned = (end - 1 >= first) & (end - 1 <= first + rows - 1)
        carried = jnp.where(end - meta[r] < first, 1.0, 0.0)
        ref[heads * DK :] = edge_ref[r].astype(BF16)

        @pl.when(owned)
        def _():
            for h in range(heads):
                scaled = jnp.where(seg == r, uw_ref[h] * ks_ref[h], 0.0)
                high, less = split(scaled)
                fold = dot(kb_ref[h], high, TN) + dot(kb_ref[h], less, TN)
                link = carried * eye - fold[:, DK:]
                prefix = prefix_ref[h]
                both = dot32(link, prefix)
                ref[h * DK : (h + 1) * DK, :DK] = (link - both[:, :DK]).astype(BF16)
                ref[h * DK : (h + 1) * DK, DK:] = (both[:, DK:] + fold[:, :DK]).astype(BF16)

        @pl.when(jnp.logical_not(owned))
        def _():
            ref[: heads * DK] = jnp.zeros((heads * DK, 2 * DK), BF16)


def state_kernel(ahead_ref, *refs):
    *piece_refs, pay_ref = refs
    maps = piece_refs[0][...]
    for ref in piece_refs[1:]:
        maps = maps + ref[...]
    heads = ahead_ref.shape[0]
    for h in range(heads):
        mine = maps[h * DK : (h + 1) * DK]
        high, less = split(ahead_ref[h])
        final = dot(mine[:, :DK], high) + dot(mine[:, :DK], less) + mine[:, DK:].astype(F32)
        pay_ref[h * DK : (h + 1) * DK] = final.astype(BF16)
        base = heads * DK + h * EDGE_ROWS
        pay_ref[base : base + EDGE_ROWS] = maps[heads * DK :, h * DK : (h + 1) * DK]


def sum_kernel(pay_ref, came_ref, sum_ref):
    sum_ref[...] = pay_ref[...] + came_ref[...]


def attend_kernel(
    meta, prefix_ref, wide_ref, tail_ref, local_ref, link_ref, gain_ref, w_ref,
    own_ref, other_ref, ahead_ref, heads_ref,
):
    heads, rows, _ = local_ref.shape
    wins, cores, piece, _ = heads_ref.shape
    win, core = meta[5], meta[6]
    gain = gain_ref[...]
    for h in range(heads):
        wide, prefix, tail = wide_ref[h], prefix_ref[h], tail_ref[h]
        ahead = wide[:, DK:].astype(F32) + tail.astype(F32) - dot(wide[:, :DK], tail)
        enter = prefix[:, DK:] + ahead - dot32(prefix[:, :DK], ahead)
        parts = split(enter)
        attended = local_ref[h] + dot_split(split(link_ref[h]), parts)
        scale = lax.rsqrt(jnp.mean(attended * attended, axis=1, keepdims=True) + 1e-05)
        normed = attended * scale * gain
        lanes = slice(h * DK, (h + 1) * DK)
        for p in range(wins * cores):
            heads_ref[p // cores, p % cores, :, lanes] = normed[p * piece : (p + 1) * piece].astype(
                BF16
            )
        ahead_ref[h] = ahead
    order = [lax.rem(win + k, wins) for k in range(wins)]
    w = w_ref[...]
    mine = jnp.concatenate([heads_ref[o, core] for o in order], axis=0)
    own_ref[...] = dot(mine, w)
    theirs = jnp.concatenate([heads_ref[o, cores - 1 - core] for o in order], axis=0)
    other_ref[...] = dot(theirs, w).astype(BF16)


def pair_kernel(own_ref, got_ref, keep_ref, *send_refs):
    piece = keep_ref.shape[0]
    keep_ref[...] = own_ref[:piece] + got_ref[:piece].astype(F32)
    for k, ref in enumerate(send_refs):
        part = slice((k + 1) * piece, (k + 2) * piece)
        ref[...] = (own_ref[part] + got_ref[part].astype(F32)).astype(BF16)


def norm_kernel(hidden_ref, gain_ref, keep_ref, *refs):
    *got, stream_ref, normed_ref = refs
    total = keep_ref[...]
    for ref in got:
        total = total + ref[...].astype(F32)
    total = hidden_ref[...].astype(F32) + total
    stream_ref[...] = total.astype(BF16)
    scale = lax.rsqrt(jnp.mean(total * total, axis=1, keepdims=True) + 1e-05)
    normed_ref[...] = (total * scale * gain_ref[...]).astype(BF16)


def columns_kernel(meta, mine_ref, peer_ref, *refs):
    *piece_refs, cols_ref = refs
    wins, rows, width = cols_ref.shape
    mine, peer = mine_ref[...], peer_ref[...]
    lower = jnp.where(meta[6] == 0, mine, peer)
    upper = jnp.where(meta[6] == 0, peer, mine)
    for k in range(wins):
        cols_ref[k, : rows // 2] = lower[:, k * width : (k + 1) * width]
        cols_ref[k, rows // 2 :] = upper[:, k * width : (k + 1) * width]
    for k, ref in enumerate(piece_refs):
        ref[...] = cols_ref[lax.rem(meta[5] + k, wins)]


def last_kernel(own_ref, *refs):
    *came, all_ref = refs
    total = own_ref[...]
    for ref in came:
        total = total + ref[...].astype(F32)
    all_ref[...] = total.astype(BF16)


def finish_kernel(meta, *refs):
    *quarters, state_ref, edge_ref, pay_ref = refs
    for k, ref in enumerate(quarters):
        pay_ref[lax.rem(meta[7] + REQS - k, REQS)] = ref[...]
    reqs, rows, _ = state_ref.shape
    heads = rows // DK
    for r in range(reqs):
        state_ref[r] = pay_ref[r, :rows].astype(F32)
    for h in range(heads):
        base = rows + h * EDGE_ROWS
        edges = [pay_ref[r, base : base + EDGE_ROWS].astype(F32) for r in range(reqs)]
        for c in range(3):
            for i in range(CONV - 1):
                spot = c * CONV + i
                lines = jnp.concatenate([e[spot : spot + 1] for e in edges], axis=0)
                edge_ref[i, c, :, h * DK : (h + 1) * DK] = lines.astype(BF16)


def body(qkv_in, conv_w, beta_logits, lengths, out_gain, w_out, hidden_in, norm_gain, w_qkv):
    rows = qkv_in.shape[0]
    width = qkv_in.shape[2]
    heads = width // DK
    model = w_out.shape[1]
    n_seq, wins, cores = (lax.axis_size(a) for a in ("seq", "win", "wout"))
    piece = rows // (wins * cores)
    seq, win, core = (lax.axis_index(a).astype(jnp.int32) for a in ("seq", "win", "wout"))
    meta = jnp.concatenate([lengths, jnp.stack([seq * rows, win, core, seq % ROW])])
    x = qkv_in.transpose(1, 0, 2)
    halo = shift(x[:, rows - HALO :], "seq", 1)
    act, lead, parts, taps, beta = call(
        conv_kernel,
        [
            out((3, rows, width), BF16),
            out((3, HALO, width), BF16),
            out((3, EDGE_ROWS, width), BF16),
            out((3, CONV, width), F32),
            out((heads, rows), F32),
        ],
        "conv",
        10**8,
        meta, *(in_hbm(a) for a in (x, conv_w, beta_logits)),
        scratch=[pltpu.VMEM((3, rows, width), BF16), pltpu.SemaphoreType.DMA((3,))],
        hbm=3,
    )
    maps, uw, local, link, kb, ks, edges = call(
        prep_kernel,
        [
            out((heads, DK, 2 * DK), BF16),
            out((heads, rows, 2 * DK), F32),
            out((heads, rows, DK), F32),
            out((heads, rows, DK), F32),
            out((heads, rows, DK), BF16),
            out((heads, rows, 1), F32),
            out((REQS, EDGE_ROWS, width), F32),
        ],
        "prep",
        2 * 10**9,
        meta, act, lead, parts, taps, beta, halo,
    )

    maps_out = out((heads, DK, 2 * DK), BF16)
    came = exchange(maps, "seq", 1)
    (twin,) = call(twin_kernel, [maps_out], "twin", 10**8, meta, maps, came)
    cross = lax.ppermute(
        twin, "seq", [(s, (s ^ (ROW - 1)) + ROW) for s in range(n_seq - ROW)]
    )
    prefix, both, tail = call(
        row_kernel,
        [out((heads, DK, 2 * DK), F32), maps_out, out((heads, DK, DK), BF16)],
        "row",
        10**8,
        meta, maps, came, twin, exchange(twin, "seq", ROW - 1), shift(twin, "seq", ROW), cross,
    )
    tail = shift(tail, "seq", 3 * ROW)
    wide = shift(both, "seq", ROW)
    piece_rows = heads * DK + EDGE_ROWS
    quarter = out((heads * (DK + EDGE_ROWS), DK), BF16)
    pieces = call(
        ends_kernel,
        [out((piece_rows, 2 * DK), BF16)] * ROW,
        "ends",
        10**8,
        meta, uw, kb, ks, prefix, edges,
    )
    pieces = [pieces[0]] + [row_rotate(pieces[k], k) for k in range(1, ROW)]
    own, other, ahead = call(
        attend_kernel,
        [
            out((wins * piece, model), F32),
            out((wins * piece, model), BF16),
            out((heads, DK, DK), F32),
        ],
        "attend",
        10**9,
        meta, prefix, wide, tail, local, link, out_gain.reshape(1, DK), w_out,
        scratch=[pltpu.VMEM((wins, cores, piece, width), BF16)],
    )
    got = rotate(other, "wout", 1)
    (payload,) = call(state_kernel, [quarter], "state", 10**10, ahead, *pieces, smem=0)
    own, payload = lax.optimization_barrier((own, payload))
    sums = call(
        pair_kernel,
        [out((piece, model), F32)] + [out((piece, model), BF16)] * (wins - 1),
        "pair",
        10**6,
        own, got,
        smem=0,
    )
    reduced = [rotate(sums[k], "win", k) for k in range(1, wins)]
    lines = n_seq // ROW
    bits = [b for b in (4, 2, 1) if 2 * b <= lines]
    came = exchange(payload, "seq", bits[0] * ROW)
    stream_out, normed = call(
        norm_kernel,
        [out((piece, model), BF16)] * 2,
        "norm",
        10**6,
        hidden_in, norm_gain.reshape(1, model), sums[0], *reduced,
        smem=0,
    )
    peer = rotate(normed, "wout", 1)
    (payload,) = call(sum_kernel, [quarter], "sum", 10**10, payload, came, smem=0)
    normed, payload = lax.optimization_barrier((normed, payload))
    cols = call(
        columns_kernel,
        [out((2 * piece, model // wins), BF16)] * wins,
        "columns",
        10**6,
        meta, normed, peer,
        scratch=[pltpu.VMEM((wins, 2 * piece, model // wins), BF16)],
    )
    *cols, payload = lax.optimization_barrier((*cols, payload))
    blocks = [cols[0]] + [rotate(cols[k], "win", k) for k in range(1, wins)]

    def partial(k):
        return jnp.dot(blocks[(wins - k) % wins], w_qkv, preferred_element_type=F32)

    parts = [partial(k).astype(BF16) for k in range(1, wins)]
    arrived = [rotate(part, "win", k + 1) for k, part in enumerate(parts)]
    if lines == 8:
        turns = [rotate(payload, "seq", steps * ROW) for steps in (1, 7, 2)]
        payload = payload + (turns[0] + turns[1]) + turns[2]
    else:
        for bit in bits[1:]:
            payload = payload + exchange(payload, "seq", bit * ROW)
    quarters = [payload] + [row_rotate(payload, k) for k in range(1, ROW)]
    final_states, conv_edges = call(
        finish_kernel,
        [out((REQS, heads * DK, DK), F32), out((CONV - 1, 3, REQS, width), BF16)],
        "finish",
        10**6,
        meta, *quarters,
        scratch=[pltpu.VMEM((REQS, *quarter.shape), BF16)],
    )
    *arrived, conv_edges = lax.optimization_barrier((*arrived, conv_edges))
    (projected,) = call(
        last_kernel,
        [out((2 * piece, w_qkv.shape[1]), BF16)],
        "last",
        10**10,
        partial(0), *arrived,
        smem=0,
    )

    final_states = final_states.reshape(REQS, heads, DK, DK)
    conv_edges = conv_edges.transpose(2, 0, 1, 3)
    return (projected, stream_out, final_states, conv_edges)


def solution(mesh):
    return jax.shard_map(
        body,
        mesh=mesh,
        in_specs=(
            P("seq", None, ("win", "wout")),
            P(None, None, ("win", "wout")),
            P(("win", "wout"), "seq"),
            P(),
            P(),
            P(("win", "wout"), None),
            P(("seq", "win", "wout"), None),
            P(),
            P("win", "wout"),
        ),
        out_specs=(
            P(("seq", "win"), "wout"),
            P(("seq", "win", "wout"), None),
            P(None, ("win", "wout"), None, None),
            P(None, None, None, ("win", "wout")),
        ),
        check_vma=False,
    )
```

```python
import functools

import jax
import jax.numpy as jnp
from jax import lax
from jax.experimental import pallas as pl
from jax.experimental.pallas import tpu as pltpu
from jax.sharding import PartitionSpec as P

DK = 128
CONV = 4
REQS = 4
HALO = 16
ROW = 4
EDGE_ROWS = 16
INTERPRET = False
F32 = jnp.float32
BF16 = jnp.bfloat16
NN = ((1,), (0,))
NT = ((1,), (1,))
TN = ((0,), (0,))
VMEM = pl.BlockSpec(memory_space=pltpu.VMEM)
SMEM = pl.BlockSpec(memory_space=pltpu.SMEM)
HBM = pl.BlockSpec(memory_space=pltpu.HBM)


def shift(value, axis, steps):
    count = lax.axis_size(axis)
    return lax.ppermute(value, axis, [(s, s + steps) for s in range(max(0, count - steps))])


def rotate(value, axis, steps):
    count = lax.axis_size(axis)
    return lax.ppermute(value, axis, [(s, (s + steps) % count) for s in range(count)])


def row_rotate(value, steps):
    count = lax.axis_size("seq")
    pairs = [(s, s // ROW * ROW + (s + steps) % ROW) for s in range(count)]
    return lax.ppermute(value, "seq", pairs)


def exchange(value, axis, bit):
    return lax.ppermute(value, axis, [(s, s ^ bit) for s in range(lax.axis_size(axis))])


def dot(left, right, dims=NN):
    return lax.dot_general(left, right, (dims, ((), ())), preferred_element_type=F32)


def split(value):
    high = value.astype(BF16)
    return high, (value - high.astype(F32)).astype(BF16)


def dot_split(left, right, dims=NN):
    lh, ll = left
    rh, rl = right
    return dot(lh, rh, dims) + (dot(lh, rl, dims) + dot(ll, rh, dims))


def dot32(left, right, dims=NN):
    return dot_split(split(left), split(right), dims)


def call(kernel, outs, name, flops, *args, scratch=(), smem=1, hbm=0):
    size = sum(a.size * a.dtype.itemsize for a in args) + sum(
        o.size * o.dtype.itemsize for o in outs
    )
    return pl.pallas_call(
        kernel,
        out_shape=outs,
        in_specs=[SMEM] * smem + [HBM] * hbm + [VMEM] * (len(args) - smem - hbm),
        out_specs=[VMEM] * len(outs),
        scratch_shapes=list(scratch),
        name=name,
        interpret=INTERPRET,
        cost_estimate=pl.CostEstimate(flops=flops, bytes_accessed=size, transcendentals=0),
        compiler_params=pltpu.CompilerParams(vmem_limit_bytes=40 * 1024 * 1024),
    )(*args)


def in_hbm(value):
    return value if INTERPRET else pltpu.with_memory_space_constraint(value, pltpu.HBM)


def out(shape, dtype):
    return jax.ShapeDtypeStruct(shape, dtype)


def request_ends(meta):
    ends = [meta[0]]
    for r in range(1, REQS):
        ends.append(ends[-1] + meta[r])
    return ends


def seg_of(pos, ends):
    total = jnp.where(pos >= ends[0], 1, 0)
    for r in range(1, REQS):
        total = total + jnp.where(pos >= ends[r], 1, 0)
    return total


def start_of(pos, ends):
    begin = jnp.where(pos >= ends[0], ends[0], 0)
    for r in range(1, REQS):
        begin = jnp.maximum(begin, jnp.where(pos >= ends[r], ends[r], 0))
    return begin


def iota(shape, dim):
    return lax.broadcasted_iota(jnp.int32, shape, dim)


def conv_rows(ext, taps, pos, begin):
    pre = ext[HALO:] * taps[CONV - 1 : CONV]
    for back in range(1, CONV):
        moved = pltpu.roll(ext, back, 0)[HALO:]
        ok = jnp.where(pos - back >= begin, 1.0, 0.0).astype(F32)
        pre = pre + moved * taps[CONV - 1 - back : CONV - back] * ok
    return (pre / (1.0 + jnp.exp(-pre))).astype(BF16)


def edge_select(meta, ends, first, last, ext_pos):
    edge_id = iota((EDGE_ROWS, 1), 0)
    wanted = jnp.full((EDGE_ROWS, 1), -1, jnp.int32)
    for r in range(REQS):
        begin = ends[r] - meta[r]
        owned = (ends[r] - 1 >= first) & (ends[r] - 1 <= last)
        for i in range(CONV - 1):
            spot = ends[r] - (CONV - 1) + i
            good = owned & (spot >= begin)
            wanted = jnp.where(edge_id == r * CONV + i, jnp.where(good, spot, -1), wanted)
    return jnp.where((ext_pos == wanted) & (ext_pos >= 0), 1.0, 0.0).astype(BF16)


def conv_kernel(
    meta, x_hbm, taps_hbm, beta_hbm,
    act_ref, head_ref, edge_ref, taps_ref, beta_ref, x_ref, sems,
):
    copies = [
        pltpu.make_async_copy(x_hbm, x_ref, sems.at[0]),
        pltpu.make_async_copy(taps_hbm, taps_ref, sems.at[1]),
        pltpu.make_async_copy(beta_hbm, beta_ref, sems.at[2]),
    ]
    for copy in copies:
        copy.start()
    for copy in copies:
        copy.wait()
    rows = x_ref.shape[1]
    ends = request_ends(meta)
    first = meta[4]
    pos = first + iota((rows, 1), 0)
    begin = start_of(pos, ends)
    select = edge_select(
        meta, ends, first, first + rows - 1, first + iota((EDGE_ROWS, rows), 1)
    )
    for c in range(3):
        x = x_ref[c]
        edge_ref[c] = dot(select, x).astype(BF16)
        head_ref[c] = x[:HALO]
        wide = x.astype(F32)
        act_ref[c, HALO:] = conv_rows(wide, taps_ref[c], pos[HALO:], begin[HALO:])
        act_ref[c, :HALO] = jnp.zeros((HALO, x.shape[1]), BF16)


def prep_kernel(
    meta, act_ref, head_ref, part_ref, taps_ref, beta_ref, halo_ref,
    map_ref, uw_ref, local_ref, link_ref, kb_ref, ks_ref, edge_ref,
):
    rows = act_ref.shape[1]
    heads = act_ref.shape[2] // DK
    half = rows // 2
    ends = request_ends(meta)
    first = meta[4]
    pos = first + iota((rows, 1), 0)
    pos_r = first + iota((1, rows), 1)
    seg = seg_of(pos, ends)
    seg_r = seg_of(pos_r, ends)
    begin = start_of(pos, ends)
    coupled = jnp.where(begin < first, 1.0, 0.0).astype(F32)
    last = first + rows - 1
    last_seg = seg_of(last, ends)
    last_link = start_of(last, ends) < first
    in_last = jnp.where(seg == last_seg, 1.0, 0.0).astype(F32)
    select = edge_select(meta, ends, first, last, first - HALO + iota((EDGE_ROWS, HALO), 1))
    edge_ref[...] = jnp.zeros_like(edge_ref)

    planes = []
    for c in range(3):
        halo = halo_ref[c]
        picked = part_ref[c] + dot(select, halo).astype(BF16)
        picked = picked.astype(F32)
        for r in range(REQS):
            edge_ref[r, c * CONV : (c + 1) * CONV] = picked[r * CONV : (r + 1) * CONV]
        ext = jnp.concatenate([halo, head_ref[c]], axis=0).astype(F32)
        lead = conv_rows(ext, taps_ref[c], pos[:HALO], begin[:HALO])
        planes.append(jnp.concatenate([lead, act_ref[c, HALO:]], axis=0))

    row_id = iota((rows, rows), 0)
    col_id = iota((rows, rows), 1)
    same = seg == seg_r
    strict = same & (row_id > col_id)
    causal = same & (row_id >= col_id)
    diag = row_id == col_id
    row_h = iota((half, half), 0)
    col_h = iota((half, half), 1)
    eye_h = jnp.where(row_h == col_h, 1.0, 0.0).astype(F32)

    def as_row(column):
        return jnp.sum(jnp.where(diag, column, 0.0), axis=0, keepdims=True)

    def as_column(row):
        return jnp.sum(jnp.where(diag, row, 0.0), axis=1, keepdims=True)

    state = []
    for h in range(heads):
        lanes = slice(h * DK, (h + 1) * DK)
        qb, kb, vb = (planes[c][:, lanes] for c in range(3))
        q32, k32, v32 = (t.astype(F32) for t in (qb, kb, vb))
        qs = lax.rsqrt(jnp.sum(q32 * q32, axis=1, keepdims=True) + 1e-06)
        ks = lax.rsqrt(jnp.sum(k32 * k32, axis=1, keepdims=True) + 1e-06)
        ks_row = as_row(ks)
        beta = as_column(1.0 / (1.0 + jnp.exp(-beta_ref[h : h + 1, :])))
        system = jnp.where(strict, dot(kb, kb, NT) * (beta * ks) * ks_row, 0.0)
        scores = jnp.where(causal, dot(qb, kb, NT) * qs * ks_row, 0.0)
        targets = jnp.concatenate([beta * v32, (beta * coupled * ks) * k32], axis=1)
        state.append((q32 * qs, kb, ks, system, scores, targets))

    blocks = []
    for h in range(heads):
        system = state[h][3]
        for d in range(2):
            blocks.append(system[d * half : (d + 1) * half, d * half : (d + 1) * half])
    inverses = []
    low = ((row_h ^ col_h) == 1) & (row_h > col_h)
    for a in blocks:
        inverses.append(eye_h - jnp.where(low, a, 0.0))
    level = 1
    while (2 << level) <= half:
        low = (((row_h >> level) ^ (col_h >> level)) == 1) & (row_h > col_h)
        parts = [split(x) for x in inverses]
        inner = [dot_split(split(jnp.where(low, a, 0.0)), p) for a, p in zip(blocks, parts)]
        inverses = [x - dot_split(p, split(t)) for x, p, t in zip(inverses, parts, inner)]
        level += 1

    for h in range(heads):
        q32, kb, ks, system, scores, targets = state[h]
        top = dot32(inverses[2 * h], targets[:half])
        rest = targets[half:] - dot32(system[half:, :half], top)
        uw = jnp.concatenate([top, dot32(inverses[2 * h + 1], rest)], axis=0)
        uw_ref[h] = uw
        mixed = dot32(scores, uw)
        local_ref[h] = mixed[:, :DK]
        link_ref[h] = coupled * q32 - mixed[:, DK:]
        kb_ref[h] = kb
        ks_ref[h] = ks
        scaled = jnp.concatenate([uw[:, DK:] * ks, uw[:, :DK] * (ks * in_last)], axis=1)
        high, less = split(scaled)
        fold = dot(kb, high, TN) + dot(kb, less, TN)
        eye_k = jnp.where(iota((DK, DK), 0) == iota((DK, DK), 1), 1.0, 0.0).astype(F32)
        map_ref[h, :, :DK] = jnp.where(last_link, fold[:, :DK], eye_k).astype(BF16)
        map_ref[h, :, DK:] = fold[:, DK:].astype(BF16)


def joined(newer, older):
    return newer.astype(F32) + older.astype(F32) - dot(newer[:, :DK], older)


def twin_kernel(meta, own_ref, came_ref, twin_ref):
    odd = lax.rem(meta[7], 2) == 1
    for h in range(own_ref.shape[0]):
        own, came = own_ref[h], came_ref[h]
        newer = jnp.where(odd, own, came)
        older = jnp.where(odd, came, own)
        twin_ref[h] = joined(newer, older).astype(BF16)


def row_kernel(
    meta, own_ref, came_ref, twin_ref, other_ref, below_ref, cross_ref,
    prefix_ref, both_ref, tail_ref,
):
    here = meta[7]
    late = here >= ROW // 2
    odd = lax.rem(here, 2) == 1
    for h in range(own_ref.shape[0]):
        totals = []
        for same_ref, far_ref in ((twin_ref, other_ref), (below_ref, cross_ref)):
            same, far = same_ref[h], far_ref[h]
            newer = jnp.where(late, same, far)
            totals.append(joined(newer, jnp.where(late, far, same)).astype(BF16))
        both = joined(*totals).astype(BF16)
        both_ref[h] = both
        tail_ref[h] = both[:, DK:]
        other = other_ref[h]
        step = jnp.where(odd, came_ref[h], jnp.zeros_like(other))
        prefix_ref[h] = joined(step, jnp.where(late, other, jnp.zeros_like(other)))


def ends_kernel(meta, uw_ref, kb_ref, ks_ref, prefix_ref, edge_ref, *piece_refs):
    heads, rows, _ = uw_ref.shape
    ends = request_ends(meta)
    first = meta[4]
    pos = first + iota((rows, 1), 0)
    seg = seg_of(pos, ends)
    eye = jnp.where(iota((DK, DK), 0) == iota((DK, DK), 1), 1.0, 0.0).astype(F32)
    for k, ref in enumerate(piece_refs):
        r = lax.rem(meta[7] + k, REQS)
        end = ends[0]
        for i in range(1, REQS):
            end = jnp.where(r == i, ends[i], end)
        owned = (end - 1 >= first) & (end - 1 <= first + rows - 1)
        carried = jnp.where(end - meta[r] < first, 1.0, 0.0)
        ref[heads * DK :] = edge_ref[r].astype(BF16)

        @pl.when(owned)
        def _():
            for h in range(heads):
                scaled = jnp.where(seg == r, uw_ref[h] * ks_ref[h], 0.0)
                high, less = split(scaled)
                fold = dot(kb_ref[h], high, TN) + dot(kb_ref[h], less, TN)
                link = carried * eye - fold[:, DK:]
                prefix = prefix_ref[h]
                both = dot32(link, prefix)
                ref[h * DK : (h + 1) * DK, :DK] = (link - both[:, :DK]).astype(BF16)
                ref[h * DK : (h + 1) * DK, DK:] = (both[:, DK:] + fold[:, :DK]).astype(BF16)

        @pl.when(jnp.logical_not(owned))
        def _():
            ref[: heads * DK] = jnp.zeros((heads * DK, 2 * DK), BF16)


def state_kernel(ahead_ref, *refs):
    *piece_refs, pay_ref = refs
    maps = piece_refs[0][...]
    for ref in piece_refs[1:]:
        maps = maps + ref[...]
    heads = ahead_ref.shape[0]
    for h in range(heads):
        mine = maps[h * DK : (h + 1) * DK]
        high, less = split(ahead_ref[h])
        final = dot(mine[:, :DK], high) + dot(mine[:, :DK], less) + mine[:, DK:].astype(F32)
        pay_ref[h * DK : (h + 1) * DK] = final.astype(BF16)
        base = heads * DK + h * EDGE_ROWS
        pay_ref[base : base + EDGE_ROWS] = maps[heads * DK :, h * DK : (h + 1) * DK]


def sum_kernel(pay_ref, came_ref, sum_ref):
    sum_ref[...] = pay_ref[...] + came_ref[...]


def attend_kernel(
    meta, prefix_ref, wide_ref, tail_ref, local_ref, link_ref, gain_ref, w_ref,
    own_ref, other_ref, ahead_ref, heads_ref,
):
    heads, rows, _ = local_ref.shape
    wins, cores, piece, _ = heads_ref.shape
    win, core = meta[5], meta[6]
    gain = gain_ref[...]
    for h in range(heads):
        wide, prefix, tail = wide_ref[h], prefix_ref[h], tail_ref[h]
        ahead = wide[:, DK:].astype(F32) + tail.astype(F32) - dot(wide[:, :DK], tail)
        enter = prefix[:, DK:] + ahead - dot32(prefix[:, :DK], ahead)
        parts = split(enter)
        attended = local_ref[h] + dot_split(split(link_ref[h]), parts)
        scale = lax.rsqrt(jnp.mean(attended * attended, axis=1, keepdims=True) + 1e-05)
        normed = attended * scale * gain
        lanes = slice(h * DK, (h + 1) * DK)
        for p in range(wins * cores):
            heads_ref[p // cores, p % cores, :, lanes] = normed[p * piece : (p + 1) * piece].astype(
                BF16
            )
        ahead_ref[h] = ahead
    order = [lax.rem(win + k, wins) for k in range(wins)]
    w = w_ref[...]
    mine = jnp.concatenate([heads_ref[o, core] for o in order], axis=0)
    own_ref[...] = dot(mine, w)
    theirs = jnp.concatenate([heads_ref[o, cores - 1 - core] for o in order], axis=0)
    other_ref[...] = dot(theirs, w).astype(BF16)


def pair_kernel(own_ref, got_ref, keep_ref, *send_refs):
    piece = keep_ref.shape[0]
    keep_ref[...] = own_ref[:piece] + got_ref[:piece].astype(F32)
    for k, ref in enumerate(send_refs):
        part = slice((k + 1) * piece, (k + 2) * piece)
        ref[...] = (own_ref[part] + got_ref[part].astype(F32)).astype(BF16)


def norm_kernel(hidden_ref, gain_ref, keep_ref, *refs):
    *got, stream_ref, normed_ref = refs
    total = keep_ref[...]
    for ref in got:
        total = total + ref[...].astype(F32)
    total = hidden_ref[...].astype(F32) + total
    stream_ref[...] = total.astype(BF16)
    scale = lax.rsqrt(jnp.mean(total * total, axis=1, keepdims=True) + 1e-05)
    normed_ref[...] = (total * scale * gain_ref[...]).astype(BF16)


def columns_kernel(meta, mine_ref, peer_ref, *refs):
    *piece_refs, cols_ref = refs
    wins, rows, width = cols_ref.shape
    mine, peer = mine_ref[...], peer_ref[...]
    lower = jnp.where(meta[6] == 0, mine, peer)
    upper = jnp.where(meta[6] == 0, peer, mine)
    for k in range(wins):
        cols_ref[k, : rows // 2] = lower[:, k * width : (k + 1) * width]
        cols_ref[k, rows // 2 :] = upper[:, k * width : (k + 1) * width]
    for k, ref in enumerate(piece_refs):
        ref[...] = cols_ref[lax.rem(meta[5] + k, wins)]


def last_kernel(own_ref, *refs):
    *came, all_ref = refs
    total = own_ref[...]
    for ref in came:
        total = total + ref[...].astype(F32)
    all_ref[...] = total.astype(BF16)


def finish_kernel(meta, *refs):
    *quarters, state_ref, edge_ref, pay_ref = refs
    for k, ref in enumerate(quarters):
        pay_ref[lax.rem(meta[7] + REQS - k, REQS)] = ref[...]
    reqs, rows, _ = state_ref.shape
    heads = rows // DK
    for r in range(reqs):
        state_ref[r] = pay_ref[r, :rows].astype(F32)
    for h in range(heads):
        base = rows + h * EDGE_ROWS
        edges = [pay_ref[r, base : base + EDGE_ROWS].astype(F32) for r in range(reqs)]
        for c in range(3):
            for i in range(CONV - 1):
                spot = c * CONV + i
                lines = jnp.concatenate([e[spot : spot + 1] for e in edges], axis=0)
                edge_ref[i, c, :, h * DK : (h + 1) * DK] = lines.astype(BF16)


def body(qkv_in, conv_w, beta_logits, lengths, out_gain, w_out, hidden_in, norm_gain, w_qkv):
    rows = qkv_in.shape[0]
    width = qkv_in.shape[2]
    heads = width // DK
    model = w_out.shape[1]
    n_seq, wins, cores = (lax.axis_size(a) for a in ("seq", "win", "wout"))
    piece = rows // (wins * cores)
    seq, win, core = (lax.axis_index(a).astype(jnp.int32) for a in ("seq", "win", "wout"))
    meta = jnp.concatenate([lengths, jnp.stack([seq * rows, win, core, seq % ROW])])
    x = qkv_in.transpose(1, 0, 2)
    halo = shift(x[:, rows - HALO :], "seq", 1)
    act, lead, parts, taps, beta = call(
        conv_kernel,
        [
            out((3, rows, width), BF16),
            out((3, HALO, width), BF16),
            out((3, EDGE_ROWS, width), BF16),
            out((3, CONV, width), F32),
            out((heads, rows), F32),
        ],
        "conv",
        10**8,
        meta, *(in_hbm(a) for a in (x, conv_w, beta_logits)),
        scratch=[pltpu.VMEM((3, rows, width), BF16), pltpu.SemaphoreType.DMA((3,))],
        hbm=3,
    )
    maps, uw, local, link, kb, ks, edges = call(
        prep_kernel,
        [
            out((heads, DK, 2 * DK), BF16),
            out((heads, rows, 2 * DK), F32),
            out((heads, rows, DK), F32),
            out((heads, rows, DK), F32),
            out((heads, rows, DK), BF16),
            out((heads, rows, 1), F32),
            out((REQS, EDGE_ROWS, width), F32),
        ],
        "prep",
        2 * 10**9,
        meta, act, lead, parts, taps, beta, halo,
    )

    maps_out = out((heads, DK, 2 * DK), BF16)
    came = exchange(maps, "seq", 1)
    (twin,) = call(twin_kernel, [maps_out], "twin", 10**8, meta, maps, came)
    cross = lax.ppermute(
        twin, "seq", [(s, (s ^ (ROW - 1)) + ROW) for s in range(n_seq - ROW)]
    )
    prefix, both, tail = call(
        row_kernel,
        [out((heads, DK, 2 * DK), F32), maps_out, out((heads, DK, DK), BF16)],
        "row",
        10**8,
        meta, maps, came, twin, exchange(twin, "seq", ROW - 1), shift(twin, "seq", ROW), cross,
    )
    tail = shift(tail, "seq", 3 * ROW)
    wide = shift(both, "seq", ROW)
    piece_rows = heads * DK + EDGE_ROWS
    quarter = out((heads * (DK + EDGE_ROWS), DK), BF16)
    pieces = call(
        ends_kernel,
        [out((piece_rows, 2 * DK), BF16)] * ROW,
        "ends",
        10**8,
        meta, uw, kb, ks, prefix, edges,
    )
    pieces = [pieces[0]] + [row_rotate(pieces[k], k) for k in range(1, ROW)]
    own, other, ahead = call(
        attend_kernel,
        [
            out((wins * piece, model), F32),
            out((wins * piece, model), BF16),
            out((heads, DK, DK), F32),
        ],
        "attend",
        10**9,
        meta, prefix, wide, tail, local, link, out_gain.reshape(1, DK), w_out,
        scratch=[pltpu.VMEM((wins, cores, piece, width), BF16)],
    )
    got = rotate(other, "wout", 1)
    (payload,) = call(state_kernel, [quarter], "state", 10**10, ahead, *pieces, smem=0)
    own, payload = lax.optimization_barrier((own, payload))
    sums = call(
        pair_kernel,
        [out((piece, model), F32)] + [out((piece, model), BF16)] * (wins - 1),
        "pair",
        10**6,
        own, got,
        smem=0,
    )
    reduced = [rotate(sums[k], "win", k) for k in range(1, wins)]
    lines = n_seq // ROW
    bits = [b for b in (4, 2, 1) if 2 * b <= lines]
    came = exchange(payload, "seq", bits[0] * ROW)
    stream_out, normed = call(
        norm_kernel,
        [out((piece, model), BF16)] * 2,
        "norm",
        10**6,
        hidden_in, norm_gain.reshape(1, model), sums[0], *reduced,
        smem=0,
    )
    peer = rotate(normed, "wout", 1)
    (payload,) = call(sum_kernel, [quarter], "sum", 10**10, payload, came, smem=0)
    cols = call(
        columns_kernel,
        [out((2 * piece, model // wins), BF16)] * wins,
        "columns",
        10**6,
        meta, normed, peer,
        scratch=[pltpu.VMEM((wins, 2 * piece, model // wins), BF16)],
    )
    *cols, payload = lax.optimization_barrier((*cols, payload))
    blocks = [cols[0]] + [rotate(cols[k], "win", k) for k in range(1, wins)]

    def partial(k):
        return jnp.dot(blocks[(wins - k) % wins], w_qkv, preferred_element_type=F32)

    parts = [partial(k).astype(BF16) for k in range(1, wins)]
    arrived = [rotate(part, "win", k + 1) for k, part in enumerate(parts)]
    if lines == 8:
        turns = [rotate(payload, "seq", steps * ROW) for steps in (1, 7, 2)]
        payload = payload + (turns[0] + turns[1]) + turns[2]
    else:
        for bit in bits[1:]:
            payload = payload + exchange(payload, "seq", bit * ROW)
    quarters = [payload] + [row_rotate(payload, k) for k in range(1, ROW)]
    final_states, conv_edges = call(
        finish_kernel,
        [out((REQS, heads * DK, DK), F32), out((CONV - 1, 3, REQS, width), BF16)],
        "finish",
        10**6,
        meta, *quarters,
        scratch=[pltpu.VMEM((REQS, *quarter.shape), BF16)],
    )
    *arrived, conv_edges = lax.optimization_barrier((*arrived, conv_edges))
    (projected,) = call(
        last_kernel,
        [out((2 * piece, w_qkv.shape[1]), BF16)],
        "last",
        10**10,
        partial(0), *arrived,
        smem=0,
    )

    final_states = final_states.reshape(REQS, heads, DK, DK)
    conv_edges = conv_edges.transpose(2, 0, 1, 3)
    return (projected, stream_out, final_states, conv_edges)


def solution(mesh):
    return jax.shard_map(
        body,
        mesh=mesh,
        in_specs=(
            P("seq", None, ("win", "wout")),
            P(None, None, ("win", "wout")),
            P(("win", "wout"), "seq"),
            P(),
            P(),
            P(("win", "wout"), None),
            P(("seq", "win", "wout"), None),
            P(),
            P("win", "wout"),
        ),
        out_specs=(
            P(("seq", "win"), "wout"),
            P(("seq", "win", "wout"), None),
            P(None, ("win", "wout"), None, None),
            P(None, None, None, ("win", "wout")),
        ),
        check_vma=False,
    )
```
